32 devices in a mesh: seq: 8 (over y, x, core), wt: 4 (over z).
Axes of the slice: x: 2, y: 2, z: 4, core: 2. Of those that a mesh axis runs over, the one named last changes fastest.
Arguments:
- layer_input: bfloat16 [1024, 2048], P(('seq', 'wt')), may hold values from -6 to 6
- token_shift_rates: float32 [5, 2048], replicated, may hold values from 0 to 1
- input_projection_weight: bfloat16 [3, 2048, 2048], P(None, None, 'wt'), may hold values from -0.125 to 0.125
- output_matrix: bfloat16 [2048, 2048], P('wt'), may hold values from -0.125 to 0.125
- decay_lowrank_first: bfloat16 [2048, 96], replicated, may hold values from -0.125 to 0.125
- decay_lowrank_second: bfloat16 [96, 2048], P(None, 'wt'), may hold values from -0.625 to 0.625
- learning_rate_first: bfloat16 [2048, 96], replicated, may hold values from -0.125 to 0.125
- learning_rate_second: bfloat16 [96, 2048], P(None, 'wt'), may hold values from -0.625 to 0.625
- decay_channel_bias: float32 [2048], P('wt'), may hold values from -10 to 1
- learning_rate_bias: float32 [2048], P('wt'), may hold values from -6 to 2
- prenorm_key_scale: float32 [2048], P('wt'), may hold values from 0.5 to 1.5
- written_key_share: float32 [2048], P('wt'), may hold values from 0 to 1
- present_step_coefficient: float32 [2048], P('wt'), may hold values from -3 to 3
- head_norm_gain: float32 [2048], P('wt'), may hold values from 0.5 to 1.5
- packed_request_length: int32 [8], replicated, may hold values from 1 to 512, 1024 in all
Outputs:
- layer_out: bfloat16 [1024, 2048], P(('seq', 'wt'))
The draws below stay inside these ranges and needn't reach their ends.
Inputs may be any that keep to these rules, and one draw needn't show every extreme that they name: `packed_request_length`: the 8 lengths sum to 1024, and the longest is exactly 512.
All inputs are finite; a program needn't handle non-finite values.
Results may differ from the reference program's by a relative error of at most 0.0069.
Values may be sent and summed in bfloat16 or wider, within the bound.
A program may use at most 128 MiB of HBM per device.

```python
import math
import jax
import jax.numpy as jnp
import numpy as np
from jax import lax

EMBED_DIMENSION = 2048
H = 32
HS = 64
RANK_W = 96
RANK_A = 96
REQS = 8
TOTAL_POSITIONS = 1024
MAXLEN = 512


def steps_of(rng, extent, split, low, top_value):
    level = 1.0
    for axis_at, parts in split:
        steps = jax.random.uniform(jax.random.fold_in(jax.random.fold_in(rng, 6), axis_at), (parts,), jnp.float32, low / len(split), top_value / len(split))
        level = level * jnp.repeat(jnp.exp(steps), extent[axis_at] // parts).reshape((-1,) + (1,) * (len(extent) - 1 - axis_at))
    return level


def length_profile(number_of, total, limit, slope):
    portions = [(1 << 20) // math.isqrt(grade ** slope) + 1 for grade in range(2, number_of + 1)]
    surplus, given = total - limit - (number_of - 1), [1] * (number_of - 1)
    while surplus > 0:
        movable = [i for i in range(number_of - 1) if given[i] < limit]
        mass, budget = sum([portions[i] for i in movable]), surplus
        for i in movable:
            more = min(limit - given[i], max(1, budget * portions[i] // mass), surplus)
            given[i] = given[i] + more
            surplus = surplus - more
    return np.array([limit] + given)


def ragged(key, amount, total, bound, slope):
    if amount == 2:
        one = jax.random.randint(key, (), max(1, total - bound), min(bound, total - 1) + 1)
        return jnp.stack([one, total - one])
    tallies = jnp.asarray(length_profile(amount, total, bound, slope), jnp.int32)
    pairs = (amount - 1) // 2
    giver, taker = tallies[1:1 + 2 * pairs:2], tallies[2:2 + 2 * pairs:2]
    room = jnp.minimum(giver - 1, bound - taker)
    moved = jax.random.randint(jax.random.fold_in(key, 1), (pairs,), 0, 1 << 20) % (room + 1)
    tallies = tallies.at[1:1 + 2 * pairs:2].set(giver - moved).at[2:2 + 2 * pairs:2].set(taker + moved)
    return tallies[jax.random.permutation(jax.random.fold_in(key, 2), amount)]


def normal_values(own_key, dims, width, most, pieces=(), kind=jnp.bfloat16):
    drawn = width * jax.random.normal(own_key, dims, jnp.float32)
    if pieces:
        drawn = drawn * steps_of(own_key, dims, pieces, -0.22, 0.18)
    return jnp.clip(drawn, -most, most).astype(kind)


def setup_inputs(seed: int = 0) -> dict:
    arg_keys = jax.random.split(jax.random.key(seed), 16)
    layer_input = normal_values(arg_keys[0], (TOTAL_POSITIONS, EMBED_DIMENSION), 1.0, 6.0, ((0, 32),))
    token_shift_rates = jnp.clip(jax.random.uniform(arg_keys[1], (5, EMBED_DIMENSION), jnp.float32, 0.0, 1.0), 0.0, 1.0)
    input_projection_weight = normal_values(arg_keys[2], (3, EMBED_DIMENSION, EMBED_DIMENSION), EMBED_DIMENSION ** -0.5, 0.125, ((2, 4),))
    output_matrix = normal_values(arg_keys[3], (EMBED_DIMENSION, EMBED_DIMENSION), EMBED_DIMENSION ** -0.5, 0.125, ((0, 4),))
    decay_lowrank_first = normal_values(arg_keys[4], (EMBED_DIMENSION, RANK_W), EMBED_DIMENSION ** -0.5, 0.125)
    decay_lowrank_second = normal_values(arg_keys[5], (RANK_W, EMBED_DIMENSION), RANK_W ** -0.5, 0.625, ((1, 4),))
    learning_rate_first = normal_values(arg_keys[6], (EMBED_DIMENSION, RANK_A), EMBED_DIMENSION ** -0.5, 0.125)
    learning_rate_second = normal_values(arg_keys[7], (RANK_A, EMBED_DIMENSION), RANK_A ** -0.5, 0.625, ((1, 4),))
    decay_channel_bias = jnp.clip(-10.0 + 11.0 * jax.random.uniform(arg_keys[8], (EMBED_DIMENSION,), jnp.float32) ** steps_of(arg_keys[8], (EMBED_DIMENSION,), ((0, 4),), -0.2, 0.2), -10.0, 1.0)
    learning_rate_bias = jnp.clip(-6.0 + 8.0 * jax.random.uniform(arg_keys[9], (EMBED_DIMENSION,), jnp.float32) ** steps_of(arg_keys[9], (EMBED_DIMENSION,), ((0, 4),), -0.2, 0.2), -6.0, 2.0)
    prenorm_key_scale = jnp.clip(0.5 + 1.0 * jax.random.uniform(arg_keys[10], (EMBED_DIMENSION,), jnp.float32) ** steps_of(arg_keys[10], (EMBED_DIMENSION,), ((0, 4),), -0.2, 0.2), 0.5, 1.5)
    written_key_share = jnp.clip(1.0 * jax.random.uniform(arg_keys[11], (EMBED_DIMENSION,), jnp.float32) ** steps_of(arg_keys[11], (EMBED_DIMENSION,), ((0, 4),), -0.2, 0.2), 0.0, 1.0)
    present_step_coefficient = normal_values(arg_keys[12], (EMBED_DIMENSION,), 0.5, 3.0, ((0, 4),), jnp.float32)
    head_norm_gain = jnp.clip(0.5 + 1.0 * jax.random.uniform(arg_keys[13], (EMBED_DIMENSION,), jnp.float32) ** steps_of(arg_keys[13], (EMBED_DIMENSION,), ((0, 4),), -0.2, 0.2), 0.5, 1.5)
    packed_request_length = ragged(arg_keys[14], REQS, TOTAL_POSITIONS, MAXLEN, 2).astype(jnp.int32)
    return {"layer_input": layer_input, "token_shift_rates": token_shift_rates, "input_projection_weight": input_projection_weight, "output_matrix": output_matrix, "decay_lowrank_first": decay_lowrank_first, "decay_lowrank_second": decay_lowrank_second, "learning_rate_first": learning_rate_first, "learning_rate_second": learning_rate_second, "decay_channel_bias": decay_channel_bias, "learning_rate_bias": learning_rate_bias, "prenorm_key_scale": prenorm_key_scale, "written_key_share": written_key_share, "present_step_coefficient": present_step_coefficient, "head_norm_gain": head_norm_gain, "packed_request_length": packed_request_length}


LOG_SCALE = 0.6065306597126334

def advance(memory, decay_row, unit_key, removal, values_t, keys_t):
    projected = lax.optimization_barrier(jnp.sum(memory * unit_key[..., None, :], axis=-1))
    kept = memory * decay_row[..., None, :] - projected[..., :, None] * removal[..., None, :]
    return kept + values_t[..., :, None] * keys_t[..., None, :]

def head_norm(heads_y, gain):
    center = heads_y - lax.optimization_barrier(jnp.mean(heads_y, axis=-1, keepdims=True))
    spread = lax.optimization_barrier(jnp.mean(center * center, axis=-1, keepdims=True))
    return center / jnp.sqrt(spread + 0.00064) * gain

def split_across_attention_groups(matrix):
    return matrix.reshape(matrix.shape[0], -1, HS)

def reference(layer_input, token_shift_rates, input_projection_weight, output_matrix, decay_lowrank_first, decay_lowrank_second, learning_rate_first, learning_rate_second, decay_channel_bias, learning_rate_bias, prenorm_key_scale, written_key_share, present_step_coefficient, head_norm_gain, packed_request_length):
    current = layer_input.astype(jnp.float32)
    starts = (jnp.cumsum(packed_request_length) - packed_request_length).astype(jnp.int32)
    positions = jnp.arange(TOTAL_POSITIONS, dtype=jnp.int32)
    resets = jnp.any(positions[:, None] == starts[None, :], axis=1)
    previous = jnp.concatenate([jnp.zeros((1, EMBED_DIMENSION), jnp.float32), current[:-1]], axis=0)
    previous = jnp.where(resets[:, None], jnp.zeros_like(previous), previous)
    mixed = [(current + (previous - current) * token_shift_rates[which]).astype(jnp.bfloat16) for which in range(5)]
    acceptance_vectors = jnp.dot(mixed[0], input_projection_weight[0], preferred_element_type=jnp.float32)
    keys = jnp.dot(mixed[1], input_projection_weight[1], preferred_element_type=jnp.float32)
    content_vectors = jnp.dot(mixed[2], input_projection_weight[2], preferred_element_type=jnp.float32)
    decay_low = jnp.tanh(jnp.dot(mixed[3], decay_lowrank_first, preferred_element_type=jnp.float32)).astype(jnp.bfloat16)
    decay = jnp.exp(-LOG_SCALE * jax.nn.sigmoid(decay_channel_bias + jnp.dot(decay_low, decay_lowrank_second, preferred_element_type=jnp.float32)))
    iclr_low = jnp.dot(mixed[4], learning_rate_first, preferred_element_type=jnp.float32).astype(jnp.bfloat16)
    rate = jax.nn.sigmoid(learning_rate_bias + jnp.dot(iclr_low, learning_rate_second, preferred_element_type=jnp.float32))
    scaled = split_across_attention_groups(keys * prenorm_key_scale)
    unit_key = scaled / jnp.sqrt(lax.optimization_barrier(jnp.sum(scaled * scaled, axis=-1, keepdims=True)) + 1e-06)
    removal = unit_key * split_across_attention_groups(rate)
    modified_lookup_vectors = keys * (1.0 + (rate - 1.0) * written_key_share)

    def step_token(memory, inputs):
        decay_t, unit_t, removal_t, value_t, key_t, recept_t, reset_t = inputs
        memory = jnp.where(reset_t, jnp.zeros_like(memory), memory)
        memory = advance(memory, decay_t, unit_t, removal_t, value_t, key_t)
        return (memory, lax.optimization_barrier(jnp.sum(memory * recept_t[:, None, :], axis=-1)))
    initial = jnp.zeros((H, HS, HS), jnp.float32)
    _, heads_y = lax.scan(step_token, initial, (split_across_attention_groups(decay), unit_key, removal, split_across_attention_groups(content_vectors), split_across_attention_groups(modified_lookup_vectors), split_across_attention_groups(acceptance_vectors), resets))
    rescaled_attention_groups = head_norm(heads_y, head_norm_gain.reshape(H, HS))
    diagonal_reward_contribution = lax.optimization_barrier(jnp.sum(split_across_attention_groups(acceptance_vectors * modified_lookup_vectors * present_step_coefficient), axis=-1, keepdims=True))
    combined_attention_groups = (rescaled_attention_groups + diagonal_reward_contribution * split_across_attention_groups(content_vectors)).reshape(TOTAL_POSITIONS, EMBED_DIMENSION).astype(jnp.bfloat16)
    return (current + jnp.dot(combined_attention_groups, output_matrix, preferred_element_type=jnp.float32)).astype(jnp.bfloat16)
```

```python
import functools
import jax
import jax.numpy as jnp
from jax import lax
from jax.experimental import pallas as pl
from jax.experimental.pallas import tpu as pltpu
from jax.sharding import PartitionSpec as P

HS = 64
LANES = 128
LOG_SCALE = 0.6065306597126334
MESH = pl.DeviceIdType.MESH
F32 = jnp.float32
BF16 = jnp.bfloat16
STATE_TYPE = BF16
OUT_CHUNKS = 4


def mm(a, b, ca=1, cb=0):
    return lax.dot_general(
        a.astype(BF16), b.astype(BF16), (((ca,), (cb,)), ((), ())), preferred_element_type=F32
    )


def lane(shape):
    return lax.broadcasted_iota(jnp.int32, shape, 1)


def apart(z):
    left = lane(z.shape) < z.shape[1] // 2
    z = z.astype(F32)
    return jnp.concatenate([jnp.where(left, z, 0.0), jnp.where(left, 0.0, z)], axis=0).astype(BF16)


def own_blocks(z):
    rows = z.shape[0] // 2
    return jnp.where(lane((rows, z.shape[1])) < z.shape[1] // 2, z[:rows], z[rows:])


def pieces(z, count):
    out = []
    for _ in range(count):
        part = z.astype(BF16)
        out.append(part)
        z = z - part.astype(F32)
    return out


def head_sums(z):
    row = lax.broadcasted_iota(jnp.int32, (2 * LANES, LANES), 0) % LANES
    same = jnp.where(row // HS == lane((2 * LANES, LANES)) // HS, 1.0, 0.0).astype(BF16)
    return mm(jnp.concatenate(pieces(z, 2), axis=1), same)


def by_pair(fn, width):
    return jnp.concatenate([fn(slice(k, k + LANES)) for k in range(0, width, LANES)], axis=1)


def token_tables(first, rows, lengths):
    pos_c = first + lax.broadcasted_iota(jnp.int32, (rows, 1), 0)
    pos_r = first + lane((1, 2 * rows)) % rows
    far = jnp.int32(2**30)
    start = jnp.int32(0)
    reset = jnp.zeros((rows, 1), jnp.int32)
    seg_c = jnp.zeros((rows, 1), jnp.int32)
    seg_r = jnp.zeros((1, 2 * rows), jnp.int32)
    seg_last = jnp.int32(0)
    for length in lengths:
        reset = jnp.maximum(reset, jnp.where(pos_c == start, 1, 0))
        inside = jnp.where(start >= first, start, far)
        seg_c = seg_c + jnp.where(pos_c >= inside, 1, 0)
        seg_r = seg_r + jnp.where(pos_r >= inside, 1, 0)
        seg_last = seg_last + jnp.where(first + (rows - 1) >= inside, 1, 0)
        start = start + length
    return reset, seg_c, seg_r, seg_last


def chunk_terms(recept, keys, values, decay_in, rate_in, chan, seg_c, seg_r, seg_last):
    rows, width = keys.shape
    decay_bias, rate_bias, key_scale, share, coefficient = chan[:5]
    logw = -LOG_SCALE * jax.nn.sigmoid(decay_bias + decay_in)
    rate = jax.nn.sigmoid(rate_bias + rate_in)
    tri_r = lax.broadcasted_iota(jnp.int32, (rows, 3 * rows), 0)
    tri = jnp.where(tri_r >= lane((rows, 3 * rows)) % rows, 1.0, 0.0).astype(BF16)
    cum = mm(tri, jnp.concatenate(pieces(logw, 3), axis=0))
    center = cum[rows // 2 - 1 : rows // 2]
    last = cum[rows - 1 : rows]
    grow = jnp.exp(cum - center)
    grow_x = jnp.exp(cum - logw - center)
    shrink = jnp.exp(center - cum)
    to_start = jnp.exp(center) * jnp.where(seg_c == 0, 1.0, 0.0)
    to_end = jnp.exp(last - center) * jnp.where(seg_c == seg_last, 1.0, 0.0)
    scaled = keys * key_scale
    squares = scaled * scaled
    norm = by_pair(lambda s: lax.rsqrt(head_sums(squares[:, s]) + 1e-06), width)
    unit = scaled * norm
    keys_mod = keys * (1.0 + (rate - 1.0) * share)
    u_c = unit * grow_x
    q_c = recept * grow
    r_c = unit * rate * shrink
    k_c = keys_mod * shrink
    u_0 = u_c * to_start
    q_0 = q_c * to_start
    r_e = r_c * to_end
    k_e = k_c * to_end
    row = lax.broadcasted_iota(jnp.int32, (rows, 2 * rows), 0)
    col = lane((rows, 2 * rows)) % rows
    same = seg_c == seg_r
    strict = jnp.logical_and(same, row > col)
    causal = jnp.logical_and(same, row >= col)
    pairs = [slice(k, k + LANES) for k in range(0, width, LANES)]
    a_ur, a_k, a_qr = [], [], []
    for s in pairs:
        left = jnp.concatenate([u_c[:, s], q_c[:, s]], axis=0)
        right = jnp.concatenate([apart(r_c[:, s]), apart(k_c[:, s])], axis=0)
        both = mm(left, right, 1, 1)
        a_ur.append(jnp.where(strict, both[:rows, : 2 * rows], 0.0))
        a_qr.append(jnp.where(causal, both[rows:, : 2 * rows], 0.0).astype(BF16))
        a_k.append(
            jnp.concatenate(
                [
                    jnp.where(strict, both[:rows, 2 * rows :], 0.0),
                    jnp.where(causal, both[rows:, 2 * rows :], 0.0),
                ],
                axis=0,
            ).astype(BF16)
        )
    kvs = [mm(a, apart(values[:, s])) for a, s in zip(a_k, pairs)]
    eye = jnp.where(row == col, 1.0, 0.0)
    inverse = None
    size = 1
    while size < rows:
        tile_r, tile_c = row // size, col // size
        corner = jnp.logical_and(tile_r == tile_c + 1, tile_r % 2 == 1)
        lows = [jnp.where(corner, a, 0.0) for a in a_ur]
        if inverse is None:
            inverse = [eye - low for low in lows]
        else:
            halves = [mm(x, apart(low)) for x, low in zip(inverse, lows)]
            inverse = [x - mm(half, apart(x)) for x, half in zip(inverse, halves)]
        size *= 2
    solved = [
        mm(x, jnp.concatenate([apart(u_0[:, s]), apart(kv[:rows])], axis=1))
        for x, kv, s in zip(inverse, kvs, pairs)
    ]
    small_r = lax.broadcasted_iota(jnp.int32, (HS, LANES), 0)
    decay_all = jnp.exp(last) * jnp.where(seg_last == 0, 1.0, 0.0)
    diagonal = small_r == lane((HS, LANES)) % HS
    maps, adds = [], []
    for sol, s in zip(solved, pairs):
        into = jnp.concatenate([r_e[:, s], k_e[:, s]], axis=0)
        right = jnp.concatenate(
            [-sol, jnp.concatenate([jnp.zeros((rows, LANES), F32), values[:, s]], axis=1)], axis=0
        )
        end = mm(into, right, 0, 0)
        diag = jnp.where(diagonal, jnp.broadcast_to(decay_all[:, s], (HS, LANES)), 0.0)
        maps.append(diag + own_blocks(end[:, :LANES]))
        adds.append(own_blocks(end[:, LANES:]))

    def rest():
        reads, offsets, bonus = [], [], []
        own = recept * keys_mod * coefficient
        for a, sol, kv, s in zip(a_qr, solved, kvs, pairs):
            right = jnp.concatenate([apart(sol[:, :LANES]), apart(sol[:, LANES:])], axis=1)
            out = jnp.concatenate([q_0[:, s], kv[rows:]], axis=1) - mm(a, right)
            reads.append(out[:, :LANES])
            offsets.append(out[:, LANES:])
            bonus.append(head_sums(own[:, s]) * values[:, s])
        return [jnp.concatenate(z, axis=1) for z in (reads, offsets, bonus)]

    return jnp.concatenate(maps, axis=1), jnp.concatenate(adds, axis=1), rest


def kernel(
    n_seq, n_wt, hops,
    x_hbm, rates_hbm, win_hbm, wout_hbm, d1_hbm, d2_hbm, a1_hbm, a2_hbm,
    db_hbm, rb_hbm, ks_hbm, sh_hbm, co_hbm, ga_hbm, len_ref,
    out_ref,
    x_all, edge_src, edge_in, win, wout, rates, d1, d2, a1, a2, chans,
    maps, adds, reads, offsets, bonus,
    lo_src, pair_in, chip_src, lo_in, state, full, part, part_16, rs_in, acc,
    w_sem, edge_send, edge_recv, x_send, x_recv, fwd_sem, pair_sem, lo_send, lo_recv, full_sem,
    rs_send, rs_recv,
):
    b = lax.axis_index("seq")
    w = lax.axis_index("wt")
    shard, model = x_hbm.shape
    rows = shard * n_wt
    width = win.shape[2]
    half_w = width // 2
    chunk = rows // 2
    mid = n_wt // 2
    top = n_wt - 1
    odd = lax.rem(b, 2)
    chip = b // 2
    piece = model // 8
    near = w // mid

    def wt_peer(d):
        return (b, lax.rem(w + d, n_wt))

    def seq_peer(d):
        return (lax.rem(b + d, n_seq), w)

    pair_peer = (b + 1 - 2 * odd, w)
    before = lax.rem(b + n_seq - 1, n_seq)
    after = lax.rem(b + 1, n_seq)

    barrier = pltpu.get_barrier_semaphore()

    def greet(target):
        pl.semaphore_signal(barrier, inc=1, device_id=target, device_id_type=MESH)

    for d in range(1, n_wt):
        greet(wt_peer(d))
    greet(pair_peer)
    for d in range(1, hops + 1):
        @pl.when(b >= 2 * d)
        def _():
            greet((lax.rem(b + n_seq - 2 * d, n_seq), w))

    @pl.when(b >= 1)
    def _():
        greet((before, top))

    mine = pl.ds(pl.multiple_of(w * shard, shard), shard)
    x_load = pltpu.make_async_copy(x_hbm, x_all.at[mine], w_sem.at[0])
    x_load.start()
    small = [(rates_hbm, rates), (d1_hbm, d1), (a1_hbm, a1), (d2_hbm, d2), (a2_hbm, a2)]
    small += [(ref, chans.at[i]) for i, ref in enumerate((db_hbm, rb_hbm, ks_hbm, sh_hbm, co_hbm, ga_hbm))]
    small += [(win_hbm.at[c], win.at[c]) for c in range(3)]
    loads = [pltpu.make_async_copy(src, dst, w_sem.at[1 + i]) for i, (src, dst) in enumerate(small)]
    out_load = pltpu.make_async_copy(wout_hbm, wout, w_sem.at[1 + len(small)])
    for load in loads:
        load.start()
    out_load.start()
    x_load.wait()
    last_row = x_all[pl.ds(pl.multiple_of(w * shard + shard - 16, 16), 16), :][15:16].astype(F32)
    for i in range(8):
        edge_src[i : i + 1, :] = last_row[:, i * piece : (i + 1) * piece]

    sends_edge = jnp.logical_and(w == top, b < n_seq - 1)
    expected = top + 1 + jnp.where(sends_edge, n_wt, 0)
    for d in range(1, hops + 1):
        expected = expected + jnp.where(b + 2 * d < n_seq, 1, 0)
    pl.semaphore_wait(barrier, expected)

    def remote(src, dst, send, recv, target):
        return pltpu.make_async_remote_copy(
            src_ref=src, dst_ref=dst, send_sem=send, recv_sem=recv, device_id=target, device_id_type=MESH
        )

    block_edges = [
        remote(edge_src, edge_in.at[0], edge_send.at[i], edge_recv.at[0], (after, i)) for i in range(n_wt)
    ]
    mid_edges = [
        remote(edge_src, edge_in.at[1], edge_send.at[i], edge_recv.at[1], (b, i)) for i in range(mid, n_wt)
    ]

    @pl.when(sends_edge)
    def _():
        for copy in block_edges:
            copy.start()

    @pl.when(w == mid - 1)
    def _():
        for copy in mid_edges:
            copy.start()

    line = n_wt == 4
    half = shard // 2

    def rows_of(owner, h):
        return pl.ds(pl.multiple_of(owner * shard + h * half, half), half)

    def x_copy(d, h):
        place = x_all.at[rows_of(w, h)]
        return remote(place, place, x_send.at[d - 1, h], x_recv.at[d - 1, h], wt_peer(d))

    def sends(d):
        if line and d == 2:
            return jnp.logical_or(w == 0, w == top)
        return w >= 0

    orders = [list(range(1, n_wt)), list(range(n_wt - 1, 0, -1))]
    if line:
        orders = [[1, 3, 2], [3, 1, 2]]
    for side, order in enumerate(orders):
        @pl.when(near == side)
        def _():
            for d in order:
                @pl.when(sends(d))
                def _():
                    for h in range(2):
                        x_copy(d, h).start()

    relays = [(1, 2, 0, 3), (2, 1, 3, 1)] if line else []

    def relay_copy(owner, target, h):
        place = x_all.at[rows_of(owner, h)]
        return remote(place, place, fwd_sem.at[h], x_recv.at[1, h], (b, target))

    for at, owner, target, d in relays:
        @pl.when(w == at)
        def _():
            for h in range(2):
                x_copy(d, h).wait_recv()
                relay_copy(owner, target, h).start()

    def is_near(d):
        return lax.rem(w + n_wt - d, n_wt) // mid == near

    def relayed(d):
        out = w < 0
        for at, _, _, which in relays:
            if which == d:
                out = jnp.logical_or(out, w == at)
        return out

    for d in range(1, n_wt):
        @pl.when(is_near(d))
        def _():
            for h in range(2):
                x_copy(d, h).wait_recv()

    @pl.when(b >= 1)
    def _():
        block_edges[0].wait_recv()

    @pl.when(near == 1)
    def _():
        mid_edges[0].wait_recv()

    for load in loads:
        load.wait()
    lengths = [len_ref[i] for i in range(len_ref.shape[0])]
    chan = [chans[i] for i in range(6)]
    step = min(512, model)
    first_row = lax.broadcasted_iota(jnp.int32, (chunk, 1), 0) == 0

    def do_chunk(which, edge):
        base = pl.ds(pl.multiple_of(which * chunk, chunk), chunk)
        reset, seg_c, seg_r, seg_last = token_tables(b * rows + which * chunk, chunk, lengths)
        sums = [None] * 5
        for k in range(0, model, step):
            cols = slice(k, k + step)
            current = x_all[base, cols].astype(F32)
            previous = jnp.where(first_row, edge[:, cols], pltpu.roll(current, 1, 0))
            previous = jnp.where(reset == 1, 0.0, previous)
            delta = previous - current
            for c in range(5):
                mixed = (current + delta * rates[c : c + 1, cols]).astype(BF16)
                if c < 3:
                    term = mm(mixed, win[c, cols, :])
                else:
                    term = mm(mixed, (d1 if c == 3 else a1)[:, cols], 1, 1)
                sums[c] = term if sums[c] is None else sums[c] + term
        decay_in = mm(jnp.tanh(sums[3]), d2[...])
        rate_in = mm(sums[4], a2[...])
        m, a, rest = chunk_terms(*sums[:3], decay_in, rate_in, chan, seg_c, seg_r, seg_last)
        maps[which] = m
        adds[which] = a

        def finish():
            reads[which], offsets[which], bonus[which] = rest()

        return finish

    def edge_row(i):
        return jnp.concatenate([edge_in[i, r : r + 1, :] for r in range(8)], axis=1)

    def row_at(at):
        return x_all[at - 16 : at, :][15:16].astype(F32)

    do_chunk(near, jnp.where(near == 0, edge_row(0), edge_row(1)))()

    for d in range(1, n_wt):
        @pl.when(jnp.logical_not(jnp.logical_or(is_near(d), relayed(d))))
        def _():
            for h in range(2):
                x_copy(d, h).wait_recv()

    far_rest = do_chunk(1 - near, jnp.where(near == 1, edge_row(0), row_at(chunk)))

    pairs = [slice(k, k + LANES) for k in range(0, width, LANES)]
    half_pairs = [slice(k, k + LANES) for k in range(0, half_w, LANES)]

    def compose(later, earlier):
        both = mm(later[0], jnp.concatenate([apart(earlier[0]), apart(earlier[1])], axis=1))
        return both[:, :LANES], both[:, LANES:] + later[1]

    for i, s in enumerate(pairs):
        m, a = compose((maps[1, :, s], adds[1, :, s]), (maps[0, :, s], adds[0, :, s]))
        at, cols = divmod(i * LANES, half_w)
        lo_src[at, 0, :, cols : cols + LANES] = m.astype(STATE_TYPE)
        lo_src[at, 1, :, cols : cols + LANES] = a.astype(STATE_TYPE)
    pair_copy = remote(lo_src.at[1 - odd], pair_in, pair_sem.at[0], pair_sem.at[1], pair_peer)
    pair_copy.start()
    far_rest()
    pair_copy.wait_recv()
    is_odd = odd == 1
    mine_lo = lo_src[odd].astype(F32)
    other_lo = pair_in[...].astype(F32)
    even_lo = jnp.where(is_odd, other_lo, mine_lo)
    odd_lo = jnp.where(is_odd, mine_lo, other_lo)
    for s in half_pairs:
        m, a = compose((odd_lo[0, :, s], odd_lo[1, :, s]), (even_lo[0, :, s], even_lo[1, :, s]))
        chip_src[0, :, s] = m.astype(STATE_TYPE)
        chip_src[1, :, s] = a.astype(STATE_TYPE)

    def lo_copy(d):
        if d == hops:
            return remote(
                chip_src.at[1], lo_in.at[d - 1, 1], lo_send.at[d - 1], lo_recv.at[d - 1], seq_peer(2 * d)
            )
        return remote(chip_src, lo_in.at[d - 1], lo_send.at[d - 1], lo_recv.at[d - 1], seq_peer(2 * d))

    for d in range(1, hops + 1):
        @pl.when(b + 2 * d < n_seq)
        def _():
            lo_copy(d).start()

    state[...] = jnp.zeros_like(state)
    inner = []
    for s in pairs:
        right = jnp.concatenate([apart(maps[0, :, s]), apart(adds[0, :, s])], axis=1)
        late = mm(reads[1, :, s], right)
        inner.append(
            (
                jnp.concatenate([reads[0, :, s], late[:, :LANES]], axis=0).astype(BF16),
                jnp.concatenate([offsets[0, :, s], offsets[1, :, s] + late[:, LANES:]], axis=0),
            )
        )
    for d in range(hops, 0, -1):
        @pl.when(chip >= d)
        def _():
            lo_copy(d).wait_recv()
            if d == hops:
                state[...] = lo_in[d - 1, 1].astype(F32)
            else:
                for s in half_pairs:
                    state[:, s] = mm(lo_in[d - 1, 0, :, s], apart(state[:, s])) + lo_in[
                        d - 1, 1, :, s
                    ].astype(F32)

    for s in half_pairs:
        here = state[:, s]
        later = mm(even_lo[0, :, s], apart(here)) + even_lo[1, :, s]
        full[odd, 0, :, s] = jnp.where(is_odd, later, here)
        full[odd, 1, :, s] = jnp.where(is_odd, here, later)
    full_copy = remote(full.at[odd, 1], full.at[odd, 0], full_sem.at[0], full_sem.at[1], pair_peer)
    full_copy.start()
    full_copy.wait_recv()
    mixed = []
    for i, s in enumerate(pairs):
        at, cols = divmod(i * LANES, half_w)
        read, offset = inner[i]
        y = mm(read, apart(full[at, 0, :, cols : cols + LANES])) + offset
        centered = y - head_sums(y) * (1.0 / HS)
        spread = head_sums(centered * centered) * (1.0 / HS)
        extra = jnp.concatenate([bonus[0, :, s], bonus[1, :, s]], axis=0)
        mixed.append(centered * lax.rsqrt(spread + 0.00064) * chan[5][:, s] + extra)
    head_mix = jnp.concatenate(mixed, axis=1).astype(BF16)

    out_load.wait()
    span = model // OUT_CHUNKS
    right_peer, left_peer = wt_peer(1), wt_peer(n_wt - 1)

    def rs_copy(way, t, c):
        owned, cols = pl.ds(t * shard, shard), pl.ds(c * span, span)
        return remote(
            part_16.at[owned, cols], rs_in.at[way, t, :, cols], rs_send.at[way, t, c], rs_recv.at[way, t, c],
            right_peer if way == 0 else left_peer,
        )

    for c in range(OUT_CHUNKS):
        cols = slice(c * span, (c + 1) * span)
        term = mm(head_mix, wout[:, cols])
        part[:, cols] = term
        part_16[:, cols] = term.astype(BF16)

        @pl.when(w == 0)
        def _():
            rs_copy(0, top, c).start()

        @pl.when(w == top)
        def _():
            rs_copy(1, 0, c).start()

    @pl.when(w == 0)
    def _():
        for t in range(top - 1, 0, -1):
            for c in range(OUT_CHUNKS):
                rs_copy(0, t, c).start()

    @pl.when(w == top)
    def _():
        for t in range(1, top):
            for c in range(OUT_CHUNKS):
                rs_copy(1, t, c).start()

    acc[...] = part[mine, :] + x_all[mine, :].astype(F32)

    def merge(way, t):
        owned = slice(t * shard, (t + 1) * shard)
        for c in range(OUT_CHUNKS):
            cols = slice(c * span, (c + 1) * span)
            rs_copy(way, t, c).wait_recv()
            part_16[owned, cols] = (part[owned, cols] + rs_in[way, t, :, cols].astype(F32)).astype(BF16)
            rs_copy(way, t, c).start()

    for k in range(n_wt - 1):
        t_right, t_left = top - k, k
        go_right = jnp.logical_and(w > 0, w < t_right)
        go_left = jnp.logical_and(w > t_left, w < top)

        @pl.when(jnp.logical_and(go_right, near == 0))
        def _():
            merge(0, t_right)

        @pl.when(go_left)
        def _():
            merge(1, t_left)

        @pl.when(jnp.logical_and(go_right, near == 1))
        def _():
            merge(0, t_right)

    for t in range(n_wt):
        for way in (0, 1):
            if (t == 0 and way == 0) or (t == top and way == 1):
                continue

            @pl.when(jnp.logical_and(w == t, near == (1 - way)))
            def _():
                for c in range(OUT_CHUNKS):
                    cols = slice(c * span, (c + 1) * span)
                    rs_copy(way, t, c).wait_recv()
                    acc[:, cols] += rs_in[way, t, :, cols].astype(F32)

        for way in (0, 1):
            if (t == 0 and way == 0) or (t == top and way == 1):
                continue

            @pl.when(jnp.logical_and(w == t, near == way))
            def _():
                for c in range(OUT_CHUNKS):
                    cols = slice(c * span, (c + 1) * span)
                    rs_copy(way, t, c).wait_recv()
                    acc[:, cols] += rs_in[way, t, :, cols].astype(F32)

    out_ref[...] = acc[...].astype(out_ref.dtype)

    @pl.when(sends_edge)
    def _():
        for copy in block_edges:
            copy.wait_send()

    @pl.when(w == mid - 1)
    def _():
        for copy in mid_edges:
            copy.wait_send()

    for d in range(1, n_wt):
        @pl.when(sends(d))
        def _():
            for h in range(2):
                x_copy(d, h).wait_send()

    for at, owner, target, d in relays:
        @pl.when(w == at)
        def _():
            for h in range(2):
                relay_copy(owner, target, h).wait_send()

    pair_copy.wait_send()
    full_copy.wait_send()
    for d in range(1, hops + 1):
        @pl.when(b + 2 * d < n_seq)
        def _():
            lo_copy(d).wait_send()

    for t in range(n_wt):
        for way in (0, 1):
            @pl.when((w < t) if way == 0 else (w > t))
            def _():
                for c in range(OUT_CHUNKS):
                    rs_copy(way, t, c).wait_send()


def shards(
    n_seq, n_wt,
    layer_input, token_shift_rates, input_projection_weight, output_matrix,
    decay_lowrank_first, decay_lowrank_second, learning_rate_first, learning_rate_second,
    decay_channel_bias, learning_rate_bias, prenorm_key_scale, written_key_share,
    present_step_coefficient, head_norm_gain, packed_request_length,
):
    shard, model = layer_input.shape
    rows = shard * n_wt
    width = decay_lowrank_second.shape[1]
    rank_w, rank_a = decay_lowrank_second.shape[0], learning_rate_second.shape[0]
    hops = (n_seq // 2 + 1) // 2
    half_w, chunk = width // 2, rows // 2
    chan = [
        v.reshape(1, width)
        for v in (
            decay_channel_bias, learning_rate_bias, prenorm_key_scale,
            written_key_share, present_step_coefficient, head_norm_gain,
        )
    ]
    vmem = pl.BlockSpec(memory_space=pltpu.VMEM)
    far = pl.BlockSpec(memory_space=pl.ANY)
    dma = pltpu.SemaphoreType.DMA
    return pl.pallas_call(
        functools.partial(kernel, n_seq, n_wt, hops),
        out_shape=jax.ShapeDtypeStruct((shard, model), BF16),
        in_specs=[far] * 14 + [pl.BlockSpec(memory_space=pltpu.SMEM)],
        out_specs=vmem,
        scratch_shapes=[
            pltpu.VMEM((rows, model), BF16),
            pltpu.VMEM((8, model // 8), F32),
            pltpu.VMEM((2, 8, model // 8), F32),
            pltpu.VMEM((3, model, width), BF16),
            pltpu.VMEM((width, model), BF16),
            pltpu.VMEM((5, model), F32),
            pltpu.VMEM((rank_w, model), BF16),
            pltpu.VMEM((rank_w, width), BF16),
            pltpu.VMEM((rank_a, model), BF16),
            pltpu.VMEM((rank_a, width), BF16),
            pltpu.VMEM((6, 1, width), F32),
            pltpu.VMEM((2, HS, width), F32),
            pltpu.VMEM((2, HS, width), F32),
            pltpu.VMEM((2, chunk, width), F32),
            pltpu.VMEM((2, chunk, width), F32),
            pltpu.VMEM((2, chunk, width), F32),
            pltpu.VMEM((2, 2, HS, half_w), STATE_TYPE),
            pltpu.VMEM((2, HS, half_w), STATE_TYPE),
            pltpu.VMEM((2, HS, half_w), STATE_TYPE),
            pltpu.VMEM((hops, 2, HS, half_w), STATE_TYPE),
            pltpu.VMEM((HS, half_w), F32),
            pltpu.VMEM((2, 2, HS, half_w), F32),
            pltpu.VMEM((rows, model), F32),
            pltpu.VMEM((rows, model), BF16),
            pltpu.VMEM((2, n_wt, shard, model), BF16),
            pltpu.VMEM((shard, model), F32),
            dma((16,)), dma((n_wt,)), dma((2,)),
            dma((n_wt - 1, 2)), dma((n_wt - 1, 2)), dma((2,)),
            dma((2,)), dma((hops,)), dma((hops,)), dma((2,)),
            dma((2, n_wt, OUT_CHUNKS)), dma((2, n_wt, OUT_CHUNKS)),
        ],
        compiler_params=pltpu.CompilerParams(
            collective_id=0, has_side_effects=True, vmem_limit_bytes=56 * 1024 * 1024
        ),
    )(
        layer_input, token_shift_rates, input_projection_weight, output_matrix,
        decay_lowrank_first.T, decay_lowrank_second, learning_rate_first.T, learning_rate_second,
        *chan, packed_request_length,
    )


def solution(mesh):
    placed = (
        P(("seq", "wt"), None),
        P(),
        P(None, None, "wt"),
        P("wt", None),
        P(),
        P(None, "wt"),
        P(),
        P(None, "wt"),
        P("wt"),
        P("wt"),
        P("wt"),
        P("wt"),
        P("wt"),
        P("wt"),
        P(),
    )
    return jax.shard_map(
        functools.partial(shards, mesh.shape["seq"], mesh.shape["wt"]),
        mesh=mesh, in_specs=placed, out_specs=P(("seq", "wt"), None), check_vma=False,
    )
```

```python
import functools
import jax
import jax.numpy as jnp
from jax import lax
from jax.experimental import pallas as pl
from jax.experimental.pallas import tpu as pltpu
from jax.sharding import PartitionSpec as P

HS = 64
LANES = 128
LOG_SCALE = 0.6065306597126334
MESH = pl.DeviceIdType.MESH
F32 = jnp.float32
BF16 = jnp.bfloat16
STATE_TYPE = BF16
OUT_CHUNKS = 4
X_PIECES = 4


def mm(a, b, ca=1, cb=0):
    return lax.dot_general(
        a.astype(BF16), b.astype(BF16), (((ca,), (cb,)), ((), ())), preferred_element_type=F32
    )


def lane(shape):
    return lax.broadcasted_iota(jnp.int32, shape, 1)


def apart(z):
    left = lane(z.shape) < z.shape[1] // 2
    z = z.astype(F32)
    return jnp.concatenate([jnp.where(left, z, 0.0), jnp.where(left, 0.0, z)], axis=0).astype(BF16)


def own_blocks(z):
    rows = z.shape[0] // 2
    return jnp.where(lane((rows, z.shape[1])) < z.shape[1] // 2, z[:rows], z[rows:])


def pieces(z, count):
    out = []
    for _ in range(count):
        part = z.astype(BF16)
        out.append(part)
        z = z - part.astype(F32)
    return out


def head_sums(z):
    row = lax.broadcasted_iota(jnp.int32, (2 * LANES, LANES), 0) % LANES
    same = jnp.where(row // HS == lane((2 * LANES, LANES)) // HS, 1.0, 0.0).astype(BF16)
    return mm(jnp.concatenate(pieces(z, 2), axis=1), same)


def by_pair(fn, width):
    return jnp.concatenate([fn(slice(k, k + LANES)) for k in range(0, width, LANES)], axis=1)


def token_tables(first, rows, lengths):
    pos_c = first + lax.broadcasted_iota(jnp.int32, (rows, 1), 0)
    pos_r = first + lane((1, 2 * rows)) % rows
    far = jnp.int32(2**30)
    start = jnp.int32(0)
    reset = jnp.zeros((rows, 1), jnp.int32)
    seg_c = jnp.zeros((rows, 1), jnp.int32)
    seg_r = jnp.zeros((1, 2 * rows), jnp.int32)
    seg_last = jnp.int32(0)
    for length in lengths:
        reset = jnp.maximum(reset, jnp.where(pos_c == start, 1, 0))
        inside = jnp.where(start >= first, start, far)
        seg_c = seg_c + jnp.where(pos_c >= inside, 1, 0)
        seg_r = seg_r + jnp.where(pos_r >= inside, 1, 0)
        seg_last = seg_last + jnp.where(first + (rows - 1) >= inside, 1, 0)
        start = start + length
    return reset, seg_c, seg_r, seg_last


def chunk_terms(recept, keys, values, decay_in, rate_in, chan, seg_c, seg_r, seg_last):
    rows, width = keys.shape
    decay_bias, rate_bias, key_scale, share, coefficient = chan[:5]
    logw = -LOG_SCALE * jax.nn.sigmoid(decay_bias + decay_in)
    rate = jax.nn.sigmoid(rate_bias + rate_in)
    tri_r = lax.broadcasted_iota(jnp.int32, (rows, 3 * rows), 0)
    tri = jnp.where(tri_r >= lane((rows, 3 * rows)) % rows, 1.0, 0.0).astype(BF16)
    cum = mm(tri, jnp.concatenate(pieces(logw, 3), axis=0))
    center = cum[rows // 2 - 1 : rows // 2]
    last = cum[rows - 1 : rows]
    grow = jnp.exp(cum - center)
    grow_x = jnp.exp(cum - logw - center)
    shrink = jnp.exp(center - cum)
    to_start = jnp.exp(center) * jnp.where(seg_c == 0, 1.0, 0.0)
    to_end = jnp.exp(last - center) * jnp.where(seg_c == seg_last, 1.0, 0.0)
    scaled = keys * key_scale
    squares = scaled * scaled
    norm = by_pair(lambda s: lax.rsqrt(head_sums(squares[:, s]) + 1e-06), width)
    unit = scaled * norm
    keys_mod = keys * (1.0 + (rate - 1.0) * share)
    centered = values - by_pair(lambda s: head_sums(values[:, s]) * (1.0 / HS), width)
    u_c = unit * grow_x
    q_c = recept * grow
    r_c = unit * rate * shrink
    k_c = keys_mod * shrink
    u_0 = u_c * to_start
    q_0 = q_c * to_start
    r_e = r_c * to_end
    k_e = k_c * to_end
    row = lax.broadcasted_iota(jnp.int32, (rows, 2 * rows), 0)
    col = lane((rows, 2 * rows)) % rows
    same = seg_c == seg_r
    strict = jnp.logical_and(same, row > col)
    causal = jnp.logical_and(same, row >= col)
    pairs = [slice(k, k + LANES) for k in range(0, width, LANES)]
    a_ur, a_k, a_qr = [], [], []
    for s in pairs:
        left = jnp.concatenate([u_c[:, s], q_c[:, s]], axis=0)
        right = jnp.concatenate([apart(r_c[:, s]), apart(k_c[:, s])], axis=0)
        both = mm(left, right, 1, 1)
        a_ur.append(jnp.where(strict, both[:rows, : 2 * rows], 0.0))
        a_qr.append(jnp.where(causal, both[rows:, : 2 * rows], 0.0).astype(BF16))
        a_k.append(
            jnp.concatenate(
                [
                    jnp.where(strict, both[:rows, 2 * rows :], 0.0),
                    jnp.where(causal, both[rows:, 2 * rows :], 0.0),
                ],
                axis=0,
            ).astype(BF16)
        )
    kvs = [mm(a, apart(centered[:, s])) for a, s in zip(a_k, pairs)]
    eye = jnp.where(row == col, 1.0, 0.0)
    inverse = None
    size = 1
    while size < rows:
        tile_r, tile_c = row // size, col // size
        corner = jnp.logical_and(tile_r == tile_c + 1, tile_r % 2 == 1)
        lows = [jnp.where(corner, a, 0.0) for a in a_ur]
        if inverse is None:
            inverse = [eye - low for low in lows]
        else:
            halves = [mm(x, apart(low)) for x, low in zip(inverse, lows)]
            inverse = [x - mm(half, apart(x)) for x, half in zip(inverse, halves)]
        size *= 2
    solved = [
        mm(x, jnp.concatenate([apart(u_0[:, s]), apart(kv[:rows])], axis=1))
        for x, kv, s in zip(inverse, kvs, pairs)
    ]
    small_r = lax.broadcasted_iota(jnp.int32, (HS, LANES), 0)
    decay_all = jnp.exp(last) * jnp.where(seg_last == 0, 1.0, 0.0)
    diagonal = small_r == lane((HS, LANES)) % HS
    maps, adds = [], []
    for sol, s in zip(solved, pairs):
        into = jnp.concatenate([r_e[:, s], k_e[:, s]], axis=0)
        right = jnp.concatenate(
            [-sol, jnp.concatenate([jnp.zeros((rows, LANES), F32), centered[:, s]], axis=1)], axis=0
        )
        end = mm(into, right, 0, 0)
        diag = jnp.where(diagonal, jnp.broadcast_to(decay_all[:, s], (HS, LANES)), 0.0)
        maps.append(diag + own_blocks(end[:, :LANES]))
        adds.append(own_blocks(end[:, LANES:]))

    def rest():
        reads, offsets, bonus = [], [], []
        own = recept * keys_mod * coefficient
        for a, sol, kv, s in zip(a_qr, solved, kvs, pairs):
            right = jnp.concatenate([apart(sol[:, :LANES]), apart(sol[:, LANES:])], axis=1)
            out = jnp.concatenate([q_0[:, s], kv[rows:]], axis=1) - mm(a, right)
            reads.append(out[:, :LANES])
            offsets.append(out[:, LANES:])
            bonus.append(head_sums(own[:, s]) * values[:, s])
        return [jnp.concatenate(z, axis=1) for z in (reads, offsets, bonus)]

    return jnp.concatenate(maps, axis=1), jnp.concatenate(adds, axis=1), rest


def kernel(
    n_seq, n_wt, hops,
    x_hbm, rates_hbm, win_hbm, wout_hbm, d1_hbm, d2_hbm, a1_hbm, a2_hbm,
    db_hbm, rb_hbm, ks_hbm, sh_hbm, co_hbm, ga_hbm, len_ref,
    out_ref,
    x_all, edge_src, edge_in, win, wout, rates, d1, d2, a1, a2, chans,
    maps, adds, reads, offsets, bonus,
    lo_src, pair_in, chip_src, lo_in, state, full, part, part_16, rs_in, acc,
    w_sem, edge_send, edge_recv, x_send, x_recv, fwd_sem, pair_sem, lo_send, lo_recv, full_sem,
    rs_send, rs_recv,
):
    b = lax.axis_index("seq")
    w = lax.axis_index("wt")
    shard, model = x_hbm.shape
    rows = shard * n_wt
    width = win.shape[2]
    half_w = width // 2
    chunk = rows // 2
    mid = n_wt // 2
    top = n_wt - 1
    odd = lax.rem(b, 2)
    chip = b // 2
    piece = model // 8
    near = w // mid

    def wt_peer(d):
        return (b, lax.rem(w + d, n_wt))

    def seq_peer(d):
        return (lax.rem(b + d, n_seq), w)

    pair_peer = (b + 1 - 2 * odd, w)
    before = lax.rem(b + n_seq - 1, n_seq)
    after = lax.rem(b + 1, n_seq)

    barrier = pltpu.get_barrier_semaphore()

    def greet(target):
        pl.semaphore_signal(barrier, inc=1, device_id=target, device_id_type=MESH)

    for d in range(1, n_wt):
        greet(wt_peer(d))
    greet(pair_peer)
    for d in range(1, hops + 1):
        @pl.when(b >= 2 * d)
        def _():
            greet((lax.rem(b + n_seq - 2 * d, n_seq), w))

    @pl.when(b >= 1)
    def _():
        greet((before, top))

    mine = pl.ds(pl.multiple_of(w * shard, shard), shard)
    x_load = pltpu.make_async_copy(x_hbm, x_all.at[mine], w_sem.at[0])
    x_load.start()
    small = [(rates_hbm, rates), (d1_hbm, d1), (a1_hbm, a1), (d2_hbm, d2), (a2_hbm, a2)]
    small += [(ref, chans.at[i]) for i, ref in enumerate((db_hbm, rb_hbm, ks_hbm, sh_hbm, co_hbm, ga_hbm))]
    small += [(win_hbm.at[c], win.at[c]) for c in range(3)]
    loads = [pltpu.make_async_copy(src, dst, w_sem.at[1 + i]) for i, (src, dst) in enumerate(small)]
    out_load = pltpu.make_async_copy(wout_hbm, wout, w_sem.at[1 + len(small)])
    for load in loads:
        load.start()
    out_load.start()
    x_load.wait()
    last_row = x_all[pl.ds(pl.multiple_of(w * shard + shard - 16, 16), 16), :][15:16].astype(F32)
    for i in range(8):
        edge_src[i : i + 1, :] = last_row[:, i * piece : (i + 1) * piece]

    sends_edge = jnp.logical_and(w == top, b < n_seq - 1)
    expected = top + 1 + jnp.where(sends_edge, n_wt, 0)
    for d in range(1, hops + 1):
        expected = expected + jnp.where(b + 2 * d < n_seq, 1, 0)
    pl.semaphore_wait(barrier, expected)

    def remote(src, dst, send, recv, target):
        return pltpu.make_async_remote_copy(
            src_ref=src, dst_ref=dst, send_sem=send, recv_sem=recv, device_id=target, device_id_type=MESH
        )

    block_edges = [
        remote(edge_src, edge_in.at[0], edge_send.at[i], edge_recv.at[0], (after, i)) for i in range(n_wt)
    ]
    mid_edges = [
        remote(edge_src, edge_in.at[1], edge_send.at[i], edge_recv.at[1], (b, i)) for i in range(mid, n_wt)
    ]

    @pl.when(sends_edge)
    def _():
        for copy in block_edges:
            copy.start()

    @pl.when(w == mid - 1)
    def _():
        for copy in mid_edges:
            copy.start()

    line = n_wt == 4
    step = model // X_PIECES

    def piece_of(owner, h):
        return x_all.at[pl.ds(pl.multiple_of(owner * shard, shard), shard), pl.ds(h * step, step)]

    def x_copy(d, h):
        place = piece_of(w, h)
        return remote(place, place, x_send.at[d - 1, h], x_recv.at[d - 1, h], wt_peer(d))

    def sends(d):
        if line and d == 2:
            return jnp.logical_or(w == 0, w == top)
        return w >= 0

    for side in range(2):
        @pl.when(near == side)
        def _():
            order = list(range(1, n_wt)) if side == 0 else list(range(top, 0, -1))
            for h in range(X_PIECES):
                x_copy(order[0], h).start()
            for h in range(X_PIECES):
                for d in order[1:]:
                    @pl.when(sends(d))
                    def _():
                        x_copy(d, h).start()

    relays = [(1, 2, 0, 3), (2, 1, 3, 1)] if line else []

    def relay_copy(owner, target, h):
        place = piece_of(owner, h)
        return remote(place, place, fwd_sem.at[h], x_recv.at[1, h], (b, target))

    for at, owner, target, d in relays:
        @pl.when(w == at)
        def _():
            for h in range(X_PIECES):
                x_copy(d, h).wait_recv()
                relay_copy(owner, target, h).start()

    def is_near(d):
        return lax.rem(w + n_wt - d, n_wt) // mid == near

    def relayed(d):
        out = w < 0
        for at, _, _, which in relays:
            if which == d:
                out = jnp.logical_or(out, w == at)
        return out

    for d in range(1, n_wt):
        @pl.when(is_near(d))
        def _():
            for h in range(X_PIECES):
                x_copy(d, h).wait_recv()

    @pl.when(b >= 1)
    def _():
        block_edges[0].wait_recv()

    @pl.when(near == 1)
    def _():
        mid_edges[0].wait_recv()

    for load in loads:
        load.wait()
    lengths = [len_ref[i] for i in range(len_ref.shape[0])]
    chan = [chans[i] for i in range(6)]
    first_row = lax.broadcasted_iota(jnp.int32, (chunk, 1), 0) == 0

    def do_chunk(which, edge, arrival=None):
        base = pl.ds(pl.multiple_of(which * chunk, chunk), chunk)
        reset, seg_c, seg_r, seg_last = token_tables(b * rows + which * chunk, chunk, lengths)
        sums = [None] * 5
        for h in range(X_PIECES):
            if arrival is not None:
                arrival(h)
            cols = slice(h * step, (h + 1) * step)
            current = x_all[base, cols].astype(F32)
            previous = jnp.where(first_row, edge[:, cols], pltpu.roll(current, 1, 0))
            previous = jnp.where(reset == 1, 0.0, previous)
            delta = previous - current
            for c in range(5):
                mixed = (current + delta * rates[c : c + 1, cols]).astype(BF16)
                if c < 3:
                    term = mm(mixed, win[c, cols, :])
                else:
                    term = mm(mixed, (d1 if c == 3 else a1)[:, cols], 1, 1)
                sums[c] = term if sums[c] is None else sums[c] + term
        decay_in = mm(jnp.tanh(sums[3]), d2[...])
        rate_in = mm(sums[4], a2[...])
        m, a, rest = chunk_terms(*sums[:3], decay_in, rate_in, chan, seg_c, seg_r, seg_last)
        maps[which] = m
        adds[which] = a

        def finish():
            reads[which], offsets[which], bonus[which] = rest()

        return finish

    def edge_row(i):
        return jnp.concatenate([edge_in[i, r : r + 1, :] for r in range(8)], axis=1)

    def near_last_row():
        at = pl.ds(pl.multiple_of((near + 1) * chunk - 16, 16), 16)
        return x_all[at, :][15:16].astype(F32)

    do_chunk(near, jnp.where(near == 0, edge_row(0), edge_row(1)))()

    def far_arrival(h):
        for d in range(1, n_wt):
            @pl.when(jnp.logical_not(jnp.logical_or(is_near(d), relayed(d))))
            def _():
                x_copy(d, h).wait_recv()

    far_rest = do_chunk(1 - near, jnp.where(near == 1, edge_row(0), near_last_row()), far_arrival)

    pairs = [slice(k, k + LANES) for k in range(0, width, LANES)]
    half_pairs = [slice(k, k + LANES) for k in range(0, half_w, LANES)]

    def compose(later, earlier):
        both = mm(later[0], jnp.concatenate([apart(earlier[0]), apart(earlier[1])], axis=1))
        return both[:, :LANES], both[:, LANES:] + later[1]

    for i, s in enumerate(pairs):
        m, a = compose((maps[1, :, s], adds[1, :, s]), (maps[0, :, s], adds[0, :, s]))
        at, cols = divmod(i * LANES, half_w)
        lo_src[at, 0, :, cols : cols + LANES] = m.astype(STATE_TYPE)
        lo_src[at, 1, :, cols : cols + LANES] = a.astype(STATE_TYPE)
    pair_copy = remote(lo_src.at[1 - odd], pair_in, pair_sem.at[0], pair_sem.at[1], pair_peer)
    pair_copy.start()
    far_rest()
    pair_copy.wait_recv()
    is_odd = odd == 1
    mine_lo = lo_src[odd].astype(F32)
    other_lo = pair_in[...].astype(F32)
    even_lo = jnp.where(is_odd, other_lo, mine_lo)
    odd_lo = jnp.where(is_odd, mine_lo, other_lo)
    for s in half_pairs:
        m, a = compose((odd_lo[0, :, s], odd_lo[1, :, s]), (even_lo[0, :, s], even_lo[1, :, s]))
        chip_src[0, :, s] = m.astype(STATE_TYPE)
        chip_src[1, :, s] = a.astype(STATE_TYPE)

    def lo_copy(d):
        if d == hops:
            return remote(
                chip_src.at[1], lo_in.at[d - 1, 1], lo_send.at[d - 1], lo_recv.at[d - 1], seq_peer(2 * d)
            )
        return remote(chip_src, lo_in.at[d - 1], lo_send.at[d - 1], lo_recv.at[d - 1], seq_peer(2 * d))

    for d in range(1, hops + 1):
        @pl.when(b + 2 * d < n_seq)
        def _():
            lo_copy(d).start()

    state[...] = jnp.zeros_like(state)
    inner = []
    for s in pairs:
        right = jnp.concatenate([apart(maps[0, :, s]), apart(adds[0, :, s])], axis=1)
        late = mm(reads[1, :, s], right)
        inner.append(
            (
                jnp.concatenate([reads[0, :, s], late[:, :LANES]], axis=0).astype(BF16),
                jnp.concatenate([offsets[0, :, s], offsets[1, :, s] + late[:, LANES:]], axis=0),
            )
        )
    for d in range(hops, 0, -1):
        @pl.when(chip >= d)
        def _():
            lo_copy(d).wait_recv()
            if d == hops:
                state[...] = lo_in[d - 1, 1].astype(F32)
            else:
                for s in half_pairs:
                    state[:, s] = mm(lo_in[d - 1, 0, :, s], apart(state[:, s])) + lo_in[
                        d - 1, 1, :, s
                    ].astype(F32)

    for s in half_pairs:
        here = state[:, s]
        later = mm(even_lo[0, :, s], apart(here)) + even_lo[1, :, s]
        full[odd, 0, :, s] = jnp.where(is_odd, later, here)
        full[odd, 1, :, s] = jnp.where(is_odd, here, later)
    full_copy = remote(full.at[odd, 1], full.at[odd, 0], full_sem.at[0], full_sem.at[1], pair_peer)
    full_copy.start()
    full_copy.wait_recv()
    mixed = []
    for i, s in enumerate(pairs):
        at, cols = divmod(i * LANES, half_w)
        read, offset = inner[i]
        y = mm(read, apart(full[at, 0, :, cols : cols + LANES])) + offset
        spread = head_sums(y * y) * (1.0 / HS)
        extra = jnp.concatenate([bonus[0, :, s], bonus[1, :, s]], axis=0)
        mixed.append(y * lax.rsqrt(spread + 0.00064) * chan[5][:, s] + extra)
    head_mix = jnp.concatenate(mixed, axis=1).astype(BF16)

    out_load.wait()
    span = model // OUT_CHUNKS
    right_peer, left_peer = wt_peer(1), wt_peer(n_wt - 1)

    def rs_copy(way, t, c):
        owned, cols = pl.ds(t * shard, shard), pl.ds(c * span, span)
        return remote(
            part_16.at[owned, cols], rs_in.at[way, t, :, cols], rs_send.at[way, t, c], rs_recv.at[way, t, c],
            right_peer if way == 0 else left_peer,
        )

    for c in range(OUT_CHUNKS):
        cols = slice(c * span, (c + 1) * span)
        term = mm(head_mix, wout[:, cols])
        part[:, cols] = term
        part_16[:, cols] = term.astype(BF16)

        @pl.when(w == 0)
        def _():
            rs_copy(0, top, c).start()

        @pl.when(w == top)
        def _():
            rs_copy(1, 0, c).start()

    @pl.when(w == 0)
    def _():
        for t in range(top - 1, 0, -1):
            for c in range(OUT_CHUNKS):
                rs_copy(0, t, c).start()

    @pl.when(w == top)
    def _():
        for t in range(1, top):
            for c in range(OUT_CHUNKS):
                rs_copy(1, t, c).start()

    acc[...] = part[mine, :] + x_all[mine, :].astype(F32)

    def merge(way, t):
        owned = slice(t * shard, (t + 1) * shard)
        for c in range(OUT_CHUNKS):
            cols = slice(c * span, (c + 1) * span)
            rs_copy(way, t, c).wait_recv()
            part_16[owned, cols] = (part[owned, cols] + rs_in[way, t, :, cols].astype(F32)).astype(BF16)
            rs_copy(way, t, c).start()

    for k in range(n_wt - 1):
        t_right, t_left = top - k, k
        go_right = jnp.logical_and(w > 0, w < t_right)
        go_left = jnp.logical_and(w > t_left, w < top)

        @pl.when(jnp.logical_and(go_right, near == 0))
        def _():
            merge(0, t_right)

        @pl.when(go_left)
        def _():
            merge(1, t_left)

        @pl.when(jnp.logical_and(go_right, near == 1))
        def _():
            merge(0, t_right)

    for t in range(n_wt):
        for way in (0, 1):
            if (t == 0 and way == 0) or (t == top and way == 1):
                continue

            @pl.when(jnp.logical_and(w == t, near == (1 - way)))
            def _():
                for c in range(OUT_CHUNKS):
                    cols = slice(c * span, (c + 1) * span)
                    rs_copy(way, t, c).wait_recv()
                    acc[:, cols] += rs_in[way, t, :, cols].astype(F32)

        for way in (0, 1):
            if (t == 0 and way == 0) or (t == top and way == 1):
                continue

            @pl.when(jnp.logical_and(w == t, near == way))
            def _():
                for c in range(OUT_CHUNKS):
                    cols = slice(c * span, (c + 1) * span)
                    rs_copy(way, t, c).wait_recv()
                    acc[:, cols] += rs_in[way, t, :, cols].astype(F32)

    out_ref[...] = acc[...].astype(out_ref.dtype)

    @pl.when(sends_edge)
    def _():
        for copy in block_edges:
            copy.wait_send()

    @pl.when(w == mid - 1)
    def _():
        for copy in mid_edges:
            copy.wait_send()

    for d in range(1, n_wt):
        @pl.when(sends(d))
        def _():
            for h in range(X_PIECES):
                x_copy(d, h).wait_send()

    for at, owner, target, d in relays:
        @pl.when(w == at)
        def _():
            for h in range(X_PIECES):
                relay_copy(owner, target, h).wait_send()

    pair_copy.wait_send()
    full_copy.wait_send()
    for d in range(1, hops + 1):
        @pl.when(b + 2 * d < n_seq)
        def _():
            lo_copy(d).wait_send()

    for t in range(n_wt):
        for way in (0, 1):
            @pl.when((w < t) if way == 0 else (w > t))
            def _():
                for c in range(OUT_CHUNKS):
                    rs_copy(way, t, c).wait_send()


def shards(
    n_seq, n_wt,
    layer_input, token_shift_rates, input_projection_weight, output_matrix,
    decay_lowrank_first, decay_lowrank_second, learning_rate_first, learning_rate_second,
    decay_channel_bias, learning_rate_bias, prenorm_key_scale, written_key_share,
    present_step_coefficient, head_norm_gain, packed_request_length,
):
    shard, model = layer_input.shape
    rows = shard * n_wt
    width = decay_lowrank_second.shape[1]
    rank_w, rank_a = decay_lowrank_second.shape[0], learning_rate_second.shape[0]
    hops = (n_seq // 2 + 1) // 2
    half_w, chunk = width // 2, rows // 2
    chan = [
        v.reshape(1, width)
        for v in (
            decay_channel_bias, learning_rate_bias, prenorm_key_scale,
            written_key_share, present_step_coefficient, head_norm_gain,
        )
    ]
    vmem = pl.BlockSpec(memory_space=pltpu.VMEM)
    far = pl.BlockSpec(memory_space=pl.ANY)
    dma = pltpu.SemaphoreType.DMA
    return pl.pallas_call(
        functools.partial(kernel, n_seq, n_wt, hops),
        out_shape=pltpu.VMEM((shard, model), BF16),
        in_specs=[far] * 14 + [pl.BlockSpec(memory_space=pltpu.SMEM)],
        out_specs=vmem,
        scratch_shapes=[
            pltpu.VMEM((rows, model), BF16),
            pltpu.VMEM((8, model // 8), F32),
            pltpu.VMEM((2, 8, model // 8), F32),
            pltpu.VMEM((3, model, width), BF16),
            pltpu.VMEM((width, model), BF16),
            pltpu.VMEM((5, model), F32),
            pltpu.VMEM((rank_w, model), BF16),
            pltpu.VMEM((rank_w, width), BF16),
            pltpu.VMEM((rank_a, model), BF16),
            pltpu.VMEM((rank_a, width), BF16),
            pltpu.VMEM((6, 1, width), F32),
            pltpu.VMEM((2, HS, width), F32),
            pltpu.VMEM((2, HS, width), F32),
            pltpu.VMEM((2, chunk, width), F32),
            pltpu.VMEM((2, chunk, width), F32),
            pltpu.VMEM((2, chunk, width), F32),
            pltpu.VMEM((2, 2, HS, half_w), STATE_TYPE),
            pltpu.VMEM((2, HS, half_w), STATE_TYPE),
            pltpu.VMEM((2, HS, half_w), STATE_TYPE),
            pltpu.VMEM((hops, 2, HS, half_w), STATE_TYPE),
            pltpu.VMEM((HS, half_w), F32),
            pltpu.VMEM((2, 2, HS, half_w), F32),
            pltpu.VMEM((rows, model), F32),
            pltpu.VMEM((rows, model), BF16),
            pltpu.VMEM((2, n_wt, shard, model), BF16),
            pltpu.VMEM((shard, model), F32),
            dma((16,)), dma((n_wt,)), dma((2,)),
            dma((n_wt - 1, X_PIECES)), dma((n_wt - 1, X_PIECES)), dma((X_PIECES,)),
            dma((2,)), dma((hops,)), dma((hops,)), dma((2,)),
            dma((2, n_wt, OUT_CHUNKS)), dma((2, n_wt, OUT_CHUNKS)),
        ],
        compiler_params=pltpu.CompilerParams(
            collective_id=0, has_side_effects=True, vmem_limit_bytes=56 * 1024 * 1024
        ),
    )(
        layer_input, token_shift_rates, input_projection_weight, output_matrix,
        decay_lowrank_first.T, decay_lowrank_second, learning_rate_first.T, learning_rate_second,
        *chan, packed_request_length,
    )


def solution(mesh):
    placed = (
        P(("seq", "wt"), None),
        P(),
        P(None, None, "wt"),
        P("wt", None),
        P(),
        P(None, "wt"),
        P(),
        P(None, "wt"),
        P("wt"),
        P("wt"),
        P("wt"),
        P("wt"),
        P("wt"),
        P("wt"),
        P(),
    )
    return jax.shard_map(
        functools.partial(shards, mesh.shape["seq"], mesh.shape["wt"]),
        mesh=mesh, in_specs=placed, out_specs=P(("seq", "wt"), None), check_vma=False,
    )
```

```python
import functools
import jax
import jax.numpy as jnp
from jax import lax
from jax.experimental import pallas as pl
from jax.experimental.pallas import tpu as pltpu
from jax.sharding import PartitionSpec as P

HS = 64
LANES = 128
LOG_SCALE = 0.6065306597126334
MESH = pl.DeviceIdType.MESH
F32 = jnp.float32
BF16 = jnp.bfloat16
STATE_TYPE = BF16
OUT_CHUNKS = 4
X_PIECES = 4


def mm(a, b, ca=1, cb=0):
    return lax.dot_general(
        a.astype(BF16), b.astype(BF16), (((ca,), (cb,)), ((), ())), preferred_element_type=F32
    )


def lane(shape):
    return lax.broadcasted_iota(jnp.int32, shape, 1)


def apart(z):
    left = lane(z.shape) < z.shape[1] // 2
    z = z.astype(F32)
    return jnp.concatenate([jnp.where(left, z, 0.0), jnp.where(left, 0.0, z)], axis=0).astype(BF16)


def own_blocks(z):
    rows = z.shape[0] // 2
    return jnp.where(lane((rows, z.shape[1])) < z.shape[1] // 2, z[:rows], z[rows:])


def pieces(z, count):
    out = []
    for _ in range(count):
        part = z.astype(BF16)
        out.append(part)
        z = z - part.astype(F32)
    return out


def head_sums(z):
    row = lax.broadcasted_iota(jnp.int32, (2 * LANES, LANES), 0) % LANES
    same = jnp.where(row // HS == lane((2 * LANES, LANES)) // HS, 1.0, 0.0).astype(BF16)
    return mm(jnp.concatenate(pieces(z, 2), axis=1), same)


def by_pair(fn, width):
    return jnp.concatenate([fn(slice(k, k + LANES)) for k in range(0, width, LANES)], axis=1)


def token_tables(first, rows, lengths):
    pos_c = first + lax.broadcasted_iota(jnp.int32, (rows, 1), 0)
    pos_r = first + lane((1, 2 * rows)) % rows
    far = jnp.int32(2**30)
    start = jnp.int32(0)
    reset = jnp.zeros((rows, 1), jnp.int32)
    seg_c = jnp.zeros((rows, 1), jnp.int32)
    seg_r = jnp.zeros((1, 2 * rows), jnp.int32)
    seg_last = jnp.int32(0)
    for length in lengths:
        reset = jnp.maximum(reset, jnp.where(pos_c == start, 1, 0))
        inside = jnp.where(start >= first, start, far)
        seg_c = seg_c + jnp.where(pos_c >= inside, 1, 0)
        seg_r = seg_r + jnp.where(pos_r >= inside, 1, 0)
        seg_last = seg_last + jnp.where(first + (rows - 1) >= inside, 1, 0)
        start = start + length
    return reset, seg_c, seg_r, seg_last


def chunk_terms(recept, keys, values, decay_in, rate_in, chan, seg_c, seg_r, seg_last):
    rows, width = keys.shape
    decay_bias, rate_bias, key_scale, share, coefficient = chan[:5]
    logw = -LOG_SCALE * jax.nn.sigmoid(decay_bias + decay_in)
    rate = jax.nn.sigmoid(rate_bias + rate_in)
    tri_r = lax.broadcasted_iota(jnp.int32, (rows, 3 * rows), 0)
    tri = jnp.where(tri_r >= lane((rows, 3 * rows)) % rows, 1.0, 0.0).astype(BF16)
    cum = mm(tri, jnp.concatenate(pieces(logw, 3), axis=0))
    center = cum[rows // 2 - 1 : rows // 2]
    last = cum[rows - 1 : rows]
    grow = jnp.exp(cum - center)
    grow_x = jnp.exp(cum - logw - center)
    shrink = jnp.exp(center - cum)
    to_start = jnp.exp(center) * jnp.where(seg_c == 0, 1.0, 0.0)
    to_end = jnp.exp(last - center) * jnp.where(seg_c == seg_last, 1.0, 0.0)
    scaled = keys * key_scale
    squares = scaled * scaled
    norm = by_pair(lambda s: lax.rsqrt(head_sums(squares[:, s]) + 1e-06), width)
    unit = scaled * norm
    keys_mod = keys * (1.0 + (rate - 1.0) * share)
    centered = values - by_pair(lambda s: head_sums(values[:, s]) * (1.0 / HS), width)
    u_c = unit * grow_x
    q_c = recept * grow
    r_c = unit * rate * shrink
    k_c = keys_mod * shrink
    u_0 = u_c * to_start
    q_0 = q_c * to_start
    r_e = r_c * to_end
    k_e = k_c * to_end
    row = lax.broadcasted_iota(jnp.int32, (rows, 2 * rows), 0)
    col = lane((rows, 2 * rows)) % rows
    same = seg_c == seg_r
    strict = jnp.logical_and(same, row > col)
    causal = jnp.logical_and(same, row >= col)
    pairs = [slice(k, k + LANES) for k in range(0, width, LANES)]
    a_ur, a_k, a_qr = [], [], []
    for s in pairs:
        left = jnp.concatenate([u_c[:, s], q_c[:, s]], axis=0)
        right = jnp.concatenate([apart(r_c[:, s]), apart(k_c[:, s])], axis=0)
        both = mm(left, right, 1, 1)
        a_ur.append(jnp.where(strict, both[:rows, : 2 * rows], 0.0))
        a_qr.append(jnp.where(causal, both[rows:, : 2 * rows], 0.0).astype(BF16))
        a_k.append(
            jnp.concatenate(
                [
                    jnp.where(strict, both[:rows, 2 * rows :], 0.0),
                    jnp.where(causal, both[rows:, 2 * rows :], 0.0),
                ],
                axis=0,
            ).astype(BF16)
        )
    kvs = [mm(a, apart(centered[:, s])) for a, s in zip(a_k, pairs)]
    eye = jnp.where(row == col, 1.0, 0.0)
    inverse = None
    size = 1
    while size < rows:
        tile_r, tile_c = row // size, col // size
        corner = jnp.logical_and(tile_r == tile_c + 1, tile_r % 2 == 1)
        lows = [jnp.where(corner, a, 0.0) for a in a_ur]
        if inverse is None:
            inverse = [eye - low for low in lows]
        else:
            halves = [mm(x, apart(low)) for x, low in zip(inverse, lows)]
            inverse = [x - mm(half, apart(x)) for x, half in zip(inverse, halves)]
        size *= 2
    solved = [
        mm(x, jnp.concatenate([apart(u_0[:, s]), apart(kv[:rows])], axis=1))
        for x, kv, s in zip(inverse, kvs, pairs)
    ]
    small_r = lax.broadcasted_iota(jnp.int32, (HS, LANES), 0)
    decay_all = jnp.exp(last) * jnp.where(seg_last == 0, 1.0, 0.0)
    diagonal = small_r == lane((HS, LANES)) % HS
    maps, adds = [], []
    for sol, s in zip(solved, pairs):
        into = jnp.concatenate([r_e[:, s], k_e[:, s]], axis=0)
        right = jnp.concatenate(
            [-sol, jnp.concatenate([jnp.zeros((rows, LANES), F32), centered[:, s]], axis=1)], axis=0
        )
        end = mm(into, right, 0, 0)
        diag = jnp.where(diagonal, jnp.broadcast_to(decay_all[:, s], (HS, LANES)), 0.0)
        maps.append(diag + own_blocks(end[:, :LANES]))
        adds.append(own_blocks(end[:, LANES:]))

    def rest():
        reads, offsets, bonus = [], [], []
        own = recept * keys_mod * coefficient
        for a, sol, kv, s in zip(a_qr, solved, kvs, pairs):
            right = jnp.concatenate([apart(sol[:, :LANES]), apart(sol[:, LANES:])], axis=1)
            out = jnp.concatenate([q_0[:, s], kv[rows:]], axis=1) - mm(a, right)
            reads.append(out[:, :LANES])
            offsets.append(out[:, LANES:])
            bonus.append(head_sums(own[:, s]) * values[:, s])
        return [jnp.concatenate(z, axis=1) for z in (reads, offsets, bonus)]

    return jnp.concatenate(maps, axis=1), jnp.concatenate(adds, axis=1), rest


def kernel(
    n_seq, n_wt, hops,
    x_hbm, rates_hbm, win_hbm, wout_hbm, d1_hbm, d2_hbm, a1_hbm, a2_hbm,
    db_hbm, rb_hbm, ks_hbm, sh_hbm, co_hbm, ga_hbm, len_ref,
    out_ref,
    x_all, edge_src, edge_in, win, wout, rates, d1, d2, a1, a2, chans,
    maps, adds, reads, offsets, bonus,
    lo_src, pair_in, chip_src, lo_in, state, full, part, part_16, rs_in, acc,
    w_sem, edge_send, edge_recv, x_send, x_recv, fwd_sem, pair_sem, lo_send, lo_recv, full_sem,
    rs_send, rs_recv,
):
    b = lax.axis_index("seq")
    w = lax.axis_index("wt")
    shard, model = x_hbm.shape
    rows = shard * n_wt
    width = win.shape[2]
    half_w = width // 2
    chunk = rows // 2
    mid = n_wt // 2
    top = n_wt - 1
    odd = lax.rem(b, 2)
    chip = b // 2
    piece = model // 8
    near = w // mid

    def wt_peer(d):
        return (b, lax.rem(w + d, n_wt))

    def seq_peer(d):
        return (lax.rem(b + d, n_seq), w)

    pair_peer = (b + 1 - 2 * odd, w)
    before = lax.rem(b + n_seq - 1, n_seq)
    after = lax.rem(b + 1, n_seq)

    barrier = pltpu.get_barrier_semaphore()

    def greet(target):
        pl.semaphore_signal(barrier, inc=1, device_id=target, device_id_type=MESH)

    for d in range(1, n_wt):
        greet(wt_peer(d))
    greet(pair_peer)
    for d in range(1, hops + 1):
        @pl.when(b >= 2 * d)
        def _():
            greet((lax.rem(b + n_seq - 2 * d, n_seq), w))

    @pl.when(b >= 1)
    def _():
        greet((before, top))

    mine = pl.ds(pl.multiple_of(w * shard, shard), shard)
    x_load = pltpu.make_async_copy(x_hbm, x_all.at[mine], w_sem.at[0])
    x_load.start()
    small = [(rates_hbm, rates), (d1_hbm, d1), (a1_hbm, a1), (d2_hbm, d2), (a2_hbm, a2)]
    small += [(ref, chans.at[i]) for i, ref in enumerate((db_hbm, rb_hbm, ks_hbm, sh_hbm, co_hbm, ga_hbm))]
    small += [(win_hbm.at[c], win.at[c]) for c in range(3)]
    loads = [pltpu.make_async_copy(src, dst, w_sem.at[1 + i]) for i, (src, dst) in enumerate(small)]
    out_load = pltpu.make_async_copy(wout_hbm, wout, w_sem.at[1 + len(small)])
    for load in loads:
        load.start()
    out_load.start()
    x_load.wait()
    last_row = x_all[pl.ds(pl.multiple_of(w * shard + shard - 16, 16), 16), :][15:16].astype(F32)
    for i in range(8):
        edge_src[i : i + 1, :] = last_row[:, i * piece : (i + 1) * piece]

    sends_edge = jnp.logical_and(w == top, b < n_seq - 1)
    expected = top + 1 + jnp.where(sends_edge, n_wt, 0)
    for d in range(1, hops + 1):
        expected = expected + jnp.where(b + 2 * d < n_seq, 1, 0)
    pl.semaphore_wait(barrier, expected)

    def remote(src, dst, send, recv, target):
        return pltpu.make_async_remote_copy(
            src_ref=src, dst_ref=dst, send_sem=send, recv_sem=recv, device_id=target, device_id_type=MESH
        )

    block_edges = [
        remote(edge_src, edge_in.at[0], edge_send.at[i], edge_recv.at[0], (after, i)) for i in range(n_wt)
    ]
    mid_edges = [
        remote(edge_src, edge_in.at[1], edge_send.at[i], edge_recv.at[1], (b, i)) for i in range(mid, n_wt)
    ]

    @pl.when(sends_edge)
    def _():
        for copy in block_edges:
            copy.start()

    @pl.when(w == mid - 1)
    def _():
        for copy in mid_edges:
            copy.start()

    line = n_wt == 4
    step = model // X_PIECES

    def piece_of(owner, h):
        return x_all.at[pl.ds(pl.multiple_of(owner * shard, shard), shard), pl.ds(h * step, step)]

    def x_copy(d, h):
        place = piece_of(w, h)
        return remote(place, place, x_send.at[d - 1, h], x_recv.at[d - 1, h], wt_peer(d))

    def sends(d):
        if line and d == 2:
            return jnp.logical_or(w == 0, w == top)
        return w >= 0

    for side in range(2):
        @pl.when(near == side)
        def _():
            order = list(range(1, n_wt)) if side == 0 else list(range(top, 0, -1))
            if line:
                order = [1, 3, 2] if side == 0 else [3, 1, 2]
            for d in order:
                @pl.when(sends(d))
                def _():
                    for h in range(X_PIECES):
                        x_copy(d, h).start()

    relays = [(1, 2, 0, 3), (2, 1, 3, 1)] if line else []

    def relay_copy(owner, target, h):
        place = piece_of(owner, h)
        return remote(place, place, fwd_sem.at[h], x_recv.at[1, h], (b, target))

    for at, owner, target, d in relays:
        @pl.when(w == at)
        def _():
            for h in range(X_PIECES):
                x_copy(d, h).wait_recv()
                relay_copy(owner, target, h).start()

    def is_near(d):
        return lax.rem(w + n_wt - d, n_wt) // mid == near

    def relayed(d):
        out = w < 0
        for at, _, _, which in relays:
            if which == d:
                out = jnp.logical_or(out, w == at)
        return out

    for d in range(1, n_wt):
        @pl.when(is_near(d))
        def _():
            for h in range(X_PIECES):
                x_copy(d, h).wait_recv()

    @pl.when(b >= 1)
    def _():
        block_edges[0].wait_recv()

    @pl.when(near == 1)
    def _():
        mid_edges[0].wait_recv()

    for load in loads:
        load.wait()
    lengths = [len_ref[i] for i in range(len_ref.shape[0])]
    chan = [chans[i] for i in range(6)]
    first_row = lax.broadcasted_iota(jnp.int32, (chunk, 1), 0) == 0

    def do_chunk(which, edge, arrival=None):
        base = pl.ds(pl.multiple_of(which * chunk, chunk), chunk)
        reset, seg_c, seg_r, seg_last = token_tables(b * rows + which * chunk, chunk, lengths)
        sums = [None] * 5
        for h in range(X_PIECES):
            if arrival is not None:
                arrival(h)
            cols = slice(h * step, (h + 1) * step)
            current = x_all[base, cols].astype(F32)
            previous = jnp.where(first_row, edge[:, cols], pltpu.roll(current, 1, 0))
            previous = jnp.where(reset == 1, 0.0, previous)
            delta = previous - current
            for c in range(5):
                mixed = (current + delta * rates[c : c + 1, cols]).astype(BF16)
                if c < 3:
                    term = mm(mixed, win[c, cols, :])
                else:
                    term = mm(mixed, (d1 if c == 3 else a1)[:, cols], 1, 1)
                sums[c] = term if sums[c] is None else sums[c] + term
        decay_in = mm(jnp.tanh(sums[3]), d2[...])
        rate_in = mm(sums[4], a2[...])
        m, a, rest = chunk_terms(*sums[:3], decay_in, rate_in, chan, seg_c, seg_r, seg_last)
        maps[which] = m
        adds[which] = a

        def finish():
            reads[which], offsets[which], bonus[which] = rest()

        return finish

    def edge_row(i):
        return jnp.concatenate([edge_in[i, r : r + 1, :] for r in range(8)], axis=1)

    def near_last_row():
        at = pl.ds(pl.multiple_of((near + 1) * chunk - 16, 16), 16)
        return x_all[at, :][15:16].astype(F32)

    do_chunk(near, jnp.where(near == 0, edge_row(0), edge_row(1)))()

    def far_arrival(h):
        for d in range(1, n_wt):
            @pl.when(jnp.logical_not(jnp.logical_or(is_near(d), relayed(d))))
            def _():
                x_copy(d, h).wait_recv()

    far_rest = do_chunk(1 - near, jnp.where(near == 1, edge_row(0), near_last_row()), far_arrival)

    pairs = [slice(k, k + LANES) for k in range(0, width, LANES)]
    half_pairs = [slice(k, k + LANES) for k in range(0, half_w, LANES)]

    def compose(later, earlier):
        both = mm(later[0], jnp.concatenate([apart(earlier[0]), apart(earlier[1])], axis=1))
        return both[:, :LANES], both[:, LANES:] + later[1]

    for i, s in enumerate(pairs):
        m, a = compose((maps[1, :, s], adds[1, :, s]), (maps[0, :, s], adds[0, :, s]))
        at, cols = divmod(i * LANES, half_w)
        lo_src[at, 0, :, cols : cols + LANES] = m.astype(STATE_TYPE)
        lo_src[at, 1, :, cols : cols + LANES] = a.astype(STATE_TYPE)
    pair_copy = remote(lo_src.at[1 - odd], pair_in, pair_sem.at[0], pair_sem.at[1], pair_peer)
    pair_copy.start()
    far_rest()
    pair_copy.wait_recv()
    is_odd = odd == 1
    mine_lo = lo_src[odd].astype(F32)
    other_lo = pair_in[...].astype(F32)
    even_lo = jnp.where(is_odd, other_lo, mine_lo)
    odd_lo = jnp.where(is_odd, mine_lo, other_lo)
    for s in half_pairs:
        m, a = compose((odd_lo[0, :, s], odd_lo[1, :, s]), (even_lo[0, :, s], even_lo[1, :, s]))
        chip_src[0, :, s] = m.astype(STATE_TYPE)
        chip_src[1, :, s] = a.astype(STATE_TYPE)

    def lo_copy(d):
        if d == hops:
            return remote(
                chip_src.at[1], lo_in.at[d - 1, 1], lo_send.at[d - 1], lo_recv.at[d - 1], seq_peer(2 * d)
            )
        return remote(chip_src, lo_in.at[d - 1], lo_send.at[d - 1], lo_recv.at[d - 1], seq_peer(2 * d))

    for d in range(1, hops + 1):
        @pl.when(b + 2 * d < n_seq)
        def _():
            lo_copy(d).start()

    state[...] = jnp.zeros_like(state)
    inner = []
    for s in pairs:
        right = jnp.concatenate([apart(maps[0, :, s]), apart(adds[0, :, s])], axis=1)
        late = mm(reads[1, :, s], right)
        inner.append(
            (
                jnp.concatenate([reads[0, :, s], late[:, :LANES]], axis=0).astype(BF16),
                jnp.concatenate([offsets[0, :, s], offsets[1, :, s] + late[:, LANES:]], axis=0),
            )
        )
    for d in range(hops, 0, -1):
        @pl.when(chip >= d)
        def _():
            lo_copy(d).wait_recv()
            if d == hops:
                state[...] = lo_in[d - 1, 1].astype(F32)
            else:
                for s in half_pairs:
                    state[:, s] = mm(lo_in[d - 1, 0, :, s], apart(state[:, s])) + lo_in[
                        d - 1, 1, :, s
                    ].astype(F32)

    for s in half_pairs:
        here = state[:, s]
        later = mm(even_lo[0, :, s], apart(here)) + even_lo[1, :, s]
        full[odd, 0, :, s] = jnp.where(is_odd, later, here)
        full[odd, 1, :, s] = jnp.where(is_odd, here, later)
    full_copy = remote(full.at[odd, 1], full.at[odd, 0], full_sem.at[0], full_sem.at[1], pair_peer)
    full_copy.start()
    full_copy.wait_recv()
    mixed = []
    for i, s in enumerate(pairs):
        at, cols = divmod(i * LANES, half_w)
        read, offset = inner[i]
        y = mm(read, apart(full[at, 0, :, cols : cols + LANES])) + offset
        spread = head_sums(y * y) * (1.0 / HS)
        extra = jnp.concatenate([bonus[0, :, s], bonus[1, :, s]], axis=0)
        mixed.append(y * lax.rsqrt(spread + 0.00064) * chan[5][:, s] + extra)
    head_mix = jnp.concatenate(mixed, axis=1).astype(BF16)

    out_load.wait()
    span = model // OUT_CHUNKS
    right_peer, left_peer = wt_peer(1), wt_peer(n_wt - 1)

    def rs_copy(way, t, c):
        owned, cols = pl.ds(t * shard, shard), pl.ds(c * span, span)
        return remote(
            part_16.at[owned, cols], rs_in.at[way, t, :, cols], rs_send.at[way, t, c], rs_recv.at[way, t, c],
            right_peer if way == 0 else left_peer,
        )

    for c in range(OUT_CHUNKS):
        cols = slice(c * span, (c + 1) * span)
        term = mm(head_mix, wout[:, cols])
        part[:, cols] = term
        part_16[:, cols] = term.astype(BF16)

        @pl.when(w == 0)
        def _():
            rs_copy(0, top, c).start()

        @pl.when(w == top)
        def _():
            rs_copy(1, 0, c).start()

    @pl.when(w == 0)
    def _():
        for t in range(top - 1, 0, -1):
            for c in range(OUT_CHUNKS):
                rs_copy(0, t, c).start()

    @pl.when(w == top)
    def _():
        for t in range(1, top):
            for c in range(OUT_CHUNKS):
                rs_copy(1, t, c).start()

    acc[...] = part[mine, :] + x_all[mine, :].astype(F32)

    def merge(way, t):
        owned = slice(t * shard, (t + 1) * shard)
        for c in range(OUT_CHUNKS):
            cols = slice(c * span, (c + 1) * span)
            rs_copy(way, t, c).wait_recv()
            part_16[owned, cols] = (part[owned, cols] + rs_in[way, t, :, cols].astype(F32)).astype(BF16)
            rs_copy(way, t, c).start()

    for k in range(n_wt - 1):
        t_right, t_left = top - k, k
        go_right = jnp.logical_and(w > 0, w < t_right)
        go_left = jnp.logical_and(w > t_left, w < top)

        @pl.when(jnp.logical_and(go_right, near == 0))
        def _():
            merge(0, t_right)

        @pl.when(go_left)
        def _():
            merge(1, t_left)

        @pl.when(jnp.logical_and(go_right, near == 1))
        def _():
            merge(0, t_right)

    for t in range(n_wt):
        for way in (0, 1):
            if (t == 0 and way == 0) or (t == top and way == 1):
                continue

            @pl.when(jnp.logical_and(w == t, near == (1 - way)))
            def _():
                for c in range(OUT_CHUNKS):
                    cols = slice(c * span, (c + 1) * span)
                    rs_copy(way, t, c).wait_recv()
                    acc[:, cols] += rs_in[way, t, :, cols].astype(F32)

        for way in (0, 1):
            if (t == 0 and way == 0) or (t == top and way == 1):
                continue

            @pl.when(jnp.logical_and(w == t, near == way))
            def _():
                for c in range(OUT_CHUNKS):
                    cols = slice(c * span, (c + 1) * span)
                    rs_copy(way, t, c).wait_recv()
                    acc[:, cols] += rs_in[way, t, :, cols].astype(F32)

    out_ref[...] = acc[...].astype(out_ref.dtype)

    @pl.when(sends_edge)
    def _():
        for copy in block_edges:
            copy.wait_send()

    @pl.when(w == mid - 1)
    def _():
        for copy in mid_edges:
            copy.wait_send()

    for d in range(1, n_wt):
        @pl.when(sends(d))
        def _():
            for h in range(X_PIECES):
                x_copy(d, h).wait_send()

    for at, owner, target, d in relays:
        @pl.when(w == at)
        def _():
            for h in range(X_PIECES):
                relay_copy(owner, target, h).wait_send()

    pair_copy.wait_send()
    full_copy.wait_send()
    for d in range(1, hops + 1):
        @pl.when(b + 2 * d < n_seq)
        def _():
            lo_copy(d).wait_send()

    for t in range(n_wt):
        for way in (0, 1):
            @pl.when((w < t) if way == 0 else (w > t))
            def _():
                for c in range(OUT_CHUNKS):
                    rs_copy(way, t, c).wait_send()


def shards(
    n_seq, n_wt,
    layer_input, token_shift_rates, input_projection_weight, output_matrix,
    decay_lowrank_first, decay_lowrank_second, learning_rate_first, learning_rate_second,
    decay_channel_bias, learning_rate_bias, prenorm_key_scale, written_key_share,
    present_step_coefficient, head_norm_gain, packed_request_length,
):
    shard, model = layer_input.shape
    rows = shard * n_wt
    width = decay_lowrank_second.shape[1]
    rank_w, rank_a = decay_lowrank_second.shape[0], learning_rate_second.shape[0]
    hops = (n_seq // 2 + 1) // 2
    half_w, chunk = width // 2, rows // 2
    chan = [
        v.reshape(1, width)
        for v in (
            decay_channel_bias, learning_rate_bias, prenorm_key_scale,
            written_key_share, present_step_coefficient, head_norm_gain,
        )
    ]
    vmem = pl.BlockSpec(memory_space=pltpu.VMEM)
    far = pl.BlockSpec(memory_space=pl.ANY)
    dma = pltpu.SemaphoreType.DMA
    return pl.pallas_call(
        functools.partial(kernel, n_seq, n_wt, hops),
        out_shape=pltpu.VMEM((shard, model), BF16),
        in_specs=[far] * 14 + [pl.BlockSpec(memory_space=pltpu.SMEM)],
        out_specs=vmem,
        scratch_shapes=[
            pltpu.VMEM((rows, model), BF16),
            pltpu.VMEM((8, model // 8), F32),
            pltpu.VMEM((2, 8, model // 8), F32),
            pltpu.VMEM((3, model, width), BF16),
            pltpu.VMEM((width, model), BF16),
            pltpu.VMEM((5, model), F32),
            pltpu.VMEM((rank_w, model), BF16),
            pltpu.VMEM((rank_w, width), BF16),
            pltpu.VMEM((rank_a, model), BF16),
            pltpu.VMEM((rank_a, width), BF16),
            pltpu.VMEM((6, 1, width), F32),
            pltpu.VMEM((2, HS, width), F32),
            pltpu.VMEM((2, HS, width), F32),
            pltpu.VMEM((2, chunk, width), F32),
            pltpu.VMEM((2, chunk, width), F32),
            pltpu.VMEM((2, chunk, width), F32),
            pltpu.VMEM((2, 2, HS, half_w), STATE_TYPE),
            pltpu.VMEM((2, HS, half_w), STATE_TYPE),
            pltpu.VMEM((2, HS, half_w), STATE_TYPE),
            pltpu.VMEM((hops, 2, HS, half_w), STATE_TYPE),
            pltpu.VMEM((HS, half_w), F32),
            pltpu.VMEM((2, 2, HS, half_w), F32),
            pltpu.VMEM((rows, model), F32),
            pltpu.VMEM((rows, model), BF16),
            pltpu.VMEM((2, n_wt, shard, model), BF16),
            pltpu.VMEM((shard, model), F32),
            dma((16,)), dma((n_wt,)), dma((2,)),
            dma((n_wt - 1, X_PIECES)), dma((n_wt - 1, X_PIECES)), dma((X_PIECES,)),
            dma((2,)), dma((hops,)), dma((hops,)), dma((2,)),
            dma((2, n_wt, OUT_CHUNKS)), dma((2, n_wt, OUT_CHUNKS)),
        ],
        compiler_params=pltpu.CompilerParams(
            collective_id=0, has_side_effects=True, vmem_limit_bytes=56 * 1024 * 1024
        ),
    )(
        layer_input, token_shift_rates, input_projection_weight, output_matrix,
        decay_lowrank_first.T, decay_lowrank_second, learning_rate_first.T, learning_rate_second,
        *chan, packed_request_length,
    )


def solution(mesh):
    placed = (
        P(("seq", "wt"), None),
        P(),
        P(None, None, "wt"),
        P("wt", None),
        P(),
        P(None, "wt"),
        P(),
        P(None, "wt"),
        P("wt"),
        P("wt"),
        P("wt"),
        P("wt"),
        P("wt"),
        P("wt"),
        P(),
    )
    return jax.shard_map(
        functools.partial(shards, mesh.shape["seq"], mesh.shape["wt"]),
        mesh=mesh, in_specs=placed, out_specs=P(("seq", "wt"), None), check_vma=False,
    )
```

```python
import functools
import jax
import jax.numpy as jnp
from jax import lax
from jax.experimental import pallas as pl
from jax.experimental.pallas import tpu as pltpu
from jax.sharding import PartitionSpec as P

HS = 64
LANES = 128
LOG_SCALE = 0.6065306597126334
MESH = pl.DeviceIdType.MESH
F32 = jnp.float32
BF16 = jnp.bfloat16
STATE_TYPE = BF16
OUT_CHUNKS = 4
X_PIECES = 4


def mm(a, b, ca=1, cb=0):
    return lax.dot_general(
        a.astype(BF16), b.astype(BF16), (((ca,), (cb,)), ((), ())), preferred_element_type=F32
    )


def lane(shape):
    return lax.broadcasted_iota(jnp.int32, shape, 1)


def apart(z):
    left = lane(z.shape) < z.shape[1] // 2
    z = z.astype(F32)
    return jnp.concatenate([jnp.where(left, z, 0.0), jnp.where(left, 0.0, z)], axis=0).astype(BF16)


def own_blocks(z):
    rows = z.shape[0] // 2
    return jnp.where(lane((rows, z.shape[1])) < z.shape[1] // 2, z[:rows], z[rows:])


def pieces(z, count):
    out = []
    for _ in range(count):
        part = z.astype(BF16)
        out.append(part)
        z = z - part.astype(F32)
    return out


def head_sums(z):
    row = lax.broadcasted_iota(jnp.int32, (2 * LANES, LANES), 0) % LANES
    same = jnp.where(row // HS == lane((2 * LANES, LANES)) // HS, 1.0, 0.0).astype(BF16)
    return mm(jnp.concatenate(pieces(z, 2), axis=1), same)


def by_pair(fn, width):
    return jnp.concatenate([fn(slice(k, k + LANES)) for k in range(0, width, LANES)], axis=1)


def token_tables(first, rows, lengths):
    pos_c = first + lax.broadcasted_iota(jnp.int32, (rows, 1), 0)
    pos_r = first + lane((1, 2 * rows)) % rows
    far = jnp.int32(2**30)
    start = jnp.int32(0)
    reset = jnp.zeros((rows, 1), jnp.int32)
    seg_c = jnp.zeros((rows, 1), jnp.int32)
    seg_r = jnp.zeros((1, 2 * rows), jnp.int32)
    seg_last = jnp.int32(0)
    for length in lengths:
        reset = jnp.maximum(reset, jnp.where(pos_c == start, 1, 0))
        inside = jnp.where(start >= first, start, far)
        seg_c = seg_c + jnp.where(pos_c >= inside, 1, 0)
        seg_r = seg_r + jnp.where(pos_r >= inside, 1, 0)
        seg_last = seg_last + jnp.where(first + (rows - 1) >= inside, 1, 0)
        start = start + length
    return reset, seg_c, seg_r, seg_last


def chunk_terms(recept, keys, values, decay_in, rate_in, chan, seg_c, seg_r, seg_last):
    rows, width = keys.shape
    decay_bias, rate_bias, key_scale, share, coefficient = chan[:5]
    logw = -LOG_SCALE * jax.nn.sigmoid(decay_bias + decay_in)
    rate = jax.nn.sigmoid(rate_bias + rate_in)
    tri_r = lax.broadcasted_iota(jnp.int32, (rows, 3 * rows), 0)
    tri = jnp.where(tri_r >= lane((rows, 3 * rows)) % rows, 1.0, 0.0).astype(BF16)
    cum = mm(tri, jnp.concatenate(pieces(logw, 3), axis=0))
    center = cum[rows // 2 - 1 : rows // 2]
    last = cum[rows - 1 : rows]
    grow = jnp.exp(cum - center)
    grow_x = jnp.exp(cum - logw - center)
    shrink = jnp.exp(center - cum)
    to_start = jnp.exp(center) * jnp.where(seg_c == 0, 1.0, 0.0)
    to_end = jnp.exp(last - center) * jnp.where(seg_c == seg_last, 1.0, 0.0)
    scaled = keys * key_scale
    squares = scaled * scaled
    norm = by_pair(lambda s: lax.rsqrt(head_sums(squares[:, s]) + 1e-06), width)
    unit = scaled * norm
    keys_mod = keys * (1.0 + (rate - 1.0) * share)
    centered = values - by_pair(lambda s: head_sums(values[:, s]) * (1.0 / HS), width)
    u_c = unit * grow_x
    q_c = recept * grow
    r_c = unit * rate * shrink
    k_c = keys_mod * shrink
    u_0 = u_c * to_start
    q_0 = q_c * to_start
    r_e = r_c * to_end
    k_e = k_c * to_end
    row = lax.broadcasted_iota(jnp.int32, (rows, 2 * rows), 0)
    col = lane((rows, 2 * rows)) % rows
    same = seg_c == seg_r
    strict = jnp.logical_and(same, row > col)
    causal = jnp.logical_and(same, row >= col)
    pairs = [slice(k, k + LANES) for k in range(0, width, LANES)]
    a_ur, a_k, a_qr = [], [], []
    for s in pairs:
        left = jnp.concatenate([u_c[:, s], q_c[:, s]], axis=0)
        right = jnp.concatenate([apart(r_c[:, s]), apart(k_c[:, s])], axis=0)
        both = mm(left, right, 1, 1)
        a_ur.append(jnp.where(strict, both[:rows, : 2 * rows], 0.0))
        a_qr.append(jnp.where(causal, both[rows:, : 2 * rows], 0.0).astype(BF16))
        a_k.append(
            jnp.concatenate(
                [
                    jnp.where(strict, both[:rows, 2 * rows :], 0.0),
                    jnp.where(causal, both[rows:, 2 * rows :], 0.0),
                ],
                axis=0,
            ).astype(BF16)
        )
    kvs = [mm(a, apart(centered[:, s])) for a, s in zip(a_k, pairs)]
    eye = jnp.where(row == col, 1.0, 0.0)
    inverse = None
    size = 1
    while size < rows:
        tile_r, tile_c = row // size, col // size
        corner = jnp.logical_and(tile_r == tile_c + 1, tile_r % 2 == 1)
        lows = [jnp.where(corner, a, 0.0) for a in a_ur]
        if inverse is None:
            inverse = [eye - low for low in lows]
        else:
            halves = [mm(x, apart(low)) for x, low in zip(inverse, lows)]
            inverse = [x - mm(half, apart(x)) for x, half in zip(inverse, halves)]
        size *= 2
    solved = [
        mm(x, jnp.concatenate([apart(u_0[:, s]), apart(kv[:rows])], axis=1))
        for x, kv, s in zip(inverse, kvs, pairs)
    ]
    small_r = lax.broadcasted_iota(jnp.int32, (HS, LANES), 0)
    decay_all = jnp.exp(last) * jnp.where(seg_last == 0, 1.0, 0.0)
    diagonal = small_r == lane((HS, LANES)) % HS
    maps, adds = [], []
    for sol, s in zip(solved, pairs):
        into = jnp.concatenate([r_e[:, s], k_e[:, s]], axis=0)
        right = jnp.concatenate(
            [-sol, jnp.concatenate([jnp.zeros((rows, LANES), F32), centered[:, s]], axis=1)], axis=0
        )
        end = mm(into, right, 0, 0)
        diag = jnp.where(diagonal, jnp.broadcast_to(decay_all[:, s], (HS, LANES)), 0.0)
        maps.append(diag + own_blocks(end[:, :LANES]))
        adds.append(own_blocks(end[:, LANES:]))

    def rest():
        reads, offsets, bonus = [], [], []
        own = recept * keys_mod * coefficient
        for a, sol, kv, s in zip(a_qr, solved, kvs, pairs):
            right = jnp.concatenate([apart(sol[:, :LANES]), apart(sol[:, LANES:])], axis=1)
            out = jnp.concatenate([q_0[:, s], kv[rows:]], axis=1) - mm(a, right)
            reads.append(out[:, :LANES])
            offsets.append(out[:, LANES:])
            bonus.append(head_sums(own[:, s]) * values[:, s])
        return [jnp.concatenate(z, axis=1) for z in (reads, offsets, bonus)]

    return jnp.concatenate(maps, axis=1), jnp.concatenate(adds, axis=1), rest


def kernel(
    n_seq, n_wt, hops,
    x_hbm, rates_hbm, win_hbm, wout_hbm, d1_hbm, d2_hbm, a1_hbm, a2_hbm,
    db_hbm, rb_hbm, ks_hbm, sh_hbm, co_hbm, ga_hbm, len_ref,
    out_ref,
    x_all, edge_src, edge_in, win, wout, rates, d1, d2, a1, a2, chans,
    maps, adds, reads, offsets, bonus,
    lo_src, pair_in, chip_src, lo_in, state, full, part, part_16, rs_in, acc,
    w_sem, edge_send, edge_recv, x_send, x_recv, fwd_sem, pair_sem, lo_send, lo_recv, full_sem,
    rs_send, rs_recv,
):
    b = lax.axis_index("seq")
    w = lax.axis_index("wt")
    shard, model = x_hbm.shape
    rows = shard * n_wt
    width = win.shape[2]
    half_w = width // 2
    chunk = rows // 2
    mid = n_wt // 2
    top = n_wt - 1
    odd = lax.rem(b, 2)
    chip = b // 2
    piece = model // 8
    near = w // mid

    def wt_peer(d):
        return (b, lax.rem(w + d, n_wt))

    def seq_peer(d):
        return (lax.rem(b + d, n_seq), w)

    pair_peer = (b + 1 - 2 * odd, w)
    before = lax.rem(b + n_seq - 1, n_seq)
    after = lax.rem(b + 1, n_seq)

    barrier = pltpu.get_barrier_semaphore()

    def greet(target):
        pl.semaphore_signal(barrier, inc=1, device_id=target, device_id_type=MESH)

    for d in range(1, n_wt):
        greet(wt_peer(d))
    greet(pair_peer)
    for d in range(1, hops + 1):
        @pl.when(b >= 2 * d)
        def _():
            greet((lax.rem(b + n_seq - 2 * d, n_seq), w))

    @pl.when(b >= 1)
    def _():
        greet((before, top))

    mine = pl.ds(pl.multiple_of(w * shard, shard), shard)
    x_load = pltpu.make_async_copy(x_hbm, x_all.at[mine], w_sem.at[0])
    x_load.start()
    small = [(rates_hbm, rates), (d1_hbm, d1), (a1_hbm, a1), (d2_hbm, d2), (a2_hbm, a2)]
    small += [(ref, chans.at[i]) for i, ref in enumerate((db_hbm, rb_hbm, ks_hbm, sh_hbm, co_hbm, ga_hbm))]
    small += [(win_hbm.at[c], win.at[c]) for c in range(3)]
    loads = [pltpu.make_async_copy(src, dst, w_sem.at[1 + i]) for i, (src, dst) in enumerate(small)]
    out_load = pltpu.make_async_copy(wout_hbm, wout, w_sem.at[1 + len(small)])
    for load in loads:
        load.start()
    out_load.start()
    x_load.wait()
    last_row = x_all[pl.ds(pl.multiple_of(w * shard + shard - 16, 16), 16), :][15:16].astype(F32)
    for i in range(8):
        edge_src[i : i + 1, :] = last_row[:, i * piece : (i + 1) * piece]

    sends_edge = jnp.logical_and(w == top, b < n_seq - 1)
    expected = top + 1 + jnp.where(sends_edge, n_wt, 0)
    for d in range(1, hops + 1):
        expected = expected + jnp.where(b + 2 * d < n_seq, 1, 0)
    pl.semaphore_wait(barrier, expected)

    def remote(src, dst, send, recv, target):
        return pltpu.make_async_remote_copy(
            src_ref=src, dst_ref=dst, send_sem=send, recv_sem=recv, device_id=target, device_id_type=MESH
        )

    block_edges = [
        remote(edge_src, edge_in.at[0], edge_send.at[i], edge_recv.at[0], (after, i)) for i in range(n_wt)
    ]
    mid_edges = [
        remote(edge_src, edge_in.at[1], edge_send.at[i], edge_recv.at[1], (b, i)) for i in range(mid, n_wt)
    ]

    @pl.when(sends_edge)
    def _():
        for copy in block_edges:
            copy.start()

    @pl.when(w == mid - 1)
    def _():
        for copy in mid_edges:
            copy.start()

    line = n_wt == 4
    step = model // X_PIECES

    def piece_of(owner, h):
        return x_all.at[pl.ds(pl.multiple_of(owner * shard, shard), shard), pl.ds(h * step, step)]

    def x_copy(d, h):
        place = piece_of(w, h)
        return remote(place, place, x_send.at[d - 1, h], x_recv.at[d - 1, h], wt_peer(d))

    def sends(d):
        if line and d == 2:
            return jnp.logical_or(w == 0, w == top)
        return w >= 0

    for side in range(2):
        @pl.when(near == side)
        def _():
            order = list(range(1, n_wt)) if side == 0 else list(range(top, 0, -1))
            if line:
                order = [1, 3, 2] if side == 0 else [3, 1, 2]
            for d in order:
                @pl.when(sends(d))
                def _():
                    for h in range(X_PIECES):
                        x_copy(d, h).start()

    relays = [(1, 2, 0, 3), (2, 1, 3, 1)] if line else []

    def relay_copy(owner, target, h):
        place = piece_of(owner, h)
        return remote(place, place, fwd_sem.at[h], x_recv.at[1, h], (b, target))

    for at, owner, target, d in relays:
        @pl.when(w == at)
        def _():
            for h in range(X_PIECES):
                x_copy(d, h).wait_recv()
                relay_copy(owner, target, h).start()

    def is_near(d):
        return lax.rem(w + n_wt - d, n_wt) // mid == near

    def relayed(d):
        out = w < 0
        for at, _, _, which in relays:
            if which == d:
                out = jnp.logical_or(out, w == at)
        return out

    for d in range(1, n_wt):
        @pl.when(is_near(d))
        def _():
            for h in range(X_PIECES):
                x_copy(d, h).wait_recv()

    @pl.when(b >= 1)
    def _():
        block_edges[0].wait_recv()

    @pl.when(near == 1)
    def _():
        mid_edges[0].wait_recv()

    for load in loads:
        load.wait()
    lengths = [len_ref[i] for i in range(len_ref.shape[0])]
    chan = [chans[i] for i in range(6)]
    first_row = lax.broadcasted_iota(jnp.int32, (chunk, 1), 0) == 0

    def do_chunk(which, edge, arrival=None):
        base = pl.ds(pl.multiple_of(which * chunk, chunk), chunk)
        reset, seg_c, seg_r, seg_last = token_tables(b * rows + which * chunk, chunk, lengths)
        sums = [None] * 5
        for h in range(X_PIECES):
            if arrival is not None:
                arrival(h)
            cols = slice(h * step, (h + 1) * step)
            current = x_all[base, cols].astype(F32)
            previous = jnp.where(first_row, edge[:, cols], pltpu.roll(current, 1, 0))
            previous = jnp.where(reset == 1, 0.0, previous)
            delta = previous - current
            for c in range(5):
                mixed = (current + delta * rates[c : c + 1, cols]).astype(BF16)
                if c < 3:
                    term = mm(mixed, win[c, cols, :])
                else:
                    term = mm(mixed, (d1 if c == 3 else a1)[:, cols], 1, 1)
                sums[c] = term if sums[c] is None else sums[c] + term
        decay_in = mm(jnp.tanh(sums[3]), d2[...])
        rate_in = mm(sums[4], a2[...])
        m, a, rest = chunk_terms(*sums[:3], decay_in, rate_in, chan, seg_c, seg_r, seg_last)
        maps[which] = m
        adds[which] = a

        def finish():
            reads[which], offsets[which], bonus[which] = rest()

        return finish

    def edge_row(i):
        return jnp.concatenate([edge_in[i, r : r + 1, :] for r in range(8)], axis=1)

    def near_last_row():
        at = pl.ds(pl.multiple_of((near + 1) * chunk - 16, 16), 16)
        return x_all[at, :][15:16].astype(F32)

    do_chunk(near, jnp.where(near == 0, edge_row(0), edge_row(1)))()

    def far_arrival(h):
        for d in range(1, n_wt):
            @pl.when(jnp.logical_not(jnp.logical_or(is_near(d), relayed(d))))
            def _():
                x_copy(d, h).wait_recv()

    far_rest = do_chunk(1 - near, jnp.where(near == 1, edge_row(0), near_last_row()), far_arrival)

    pairs = [slice(k, k + LANES) for k in range(0, width, LANES)]
    half_pairs = [slice(k, k + LANES) for k in range(0, half_w, LANES)]

    def compose(later, earlier):
        both = mm(later[0], jnp.concatenate([apart(earlier[0]), apart(earlier[1])], axis=1))
        return both[:, :LANES], both[:, LANES:] + later[1]

    for i, s in enumerate(pairs):
        m, a = compose((maps[1, :, s], adds[1, :, s]), (maps[0, :, s], adds[0, :, s]))
        at, cols = divmod(i * LANES, half_w)
        lo_src[at, 0, :, cols : cols + LANES] = m.astype(STATE_TYPE)
        lo_src[at, 1, :, cols : cols + LANES] = a.astype(STATE_TYPE)
    pair_copy = remote(lo_src.at[1 - odd], pair_in, pair_sem.at[0], pair_sem.at[1], pair_peer)
    pair_copy.start()
    far_rest()
    pair_copy.wait_recv()
    is_odd = odd == 1
    mine_lo = lo_src[odd].astype(F32)
    other_lo = pair_in[...].astype(F32)
    even_lo = jnp.where(is_odd, other_lo, mine_lo)
    odd_lo = jnp.where(is_odd, mine_lo, other_lo)
    for s in half_pairs:
        m, a = compose((odd_lo[0, :, s], odd_lo[1, :, s]), (even_lo[0, :, s], even_lo[1, :, s]))
        chip_src[0, :, s] = m.astype(STATE_TYPE)
        chip_src[1, :, s] = a.astype(STATE_TYPE)

    def lo_copy(d):
        if d == hops:
            return remote(
                chip_src.at[1], lo_in.at[d - 1, 1], lo_send.at[d - 1], lo_recv.at[d - 1], seq_peer(2 * d)
            )
        return remote(chip_src, lo_in.at[d - 1], lo_send.at[d - 1], lo_recv.at[d - 1], seq_peer(2 * d))

    for d in range(1, hops + 1):
        @pl.when(b + 2 * d < n_seq)
        def _():
            lo_copy(d).start()

    state[...] = jnp.zeros_like(state)
    inner = []
    for s in pairs:
        right = jnp.concatenate([apart(maps[0, :, s]), apart(adds[0, :, s])], axis=1)
        late = mm(reads[1, :, s], right)
        inner.append(
            (
                jnp.concatenate([reads[0, :, s], late[:, :LANES]], axis=0).astype(BF16),
                jnp.concatenate([offsets[0, :, s], offsets[1, :, s] + late[:, LANES:]], axis=0),
            )
        )
    for d in range(hops, 0, -1):
        @pl.when(chip >= d)
        def _():
            lo_copy(d).wait_recv()
            if d == hops:
                state[...] = lo_in[d - 1, 1].astype(F32)
            else:
                for s in half_pairs:
                    state[:, s] = mm(lo_in[d - 1, 0, :, s], apart(state[:, s])) + lo_in[
                        d - 1, 1, :, s
                    ].astype(F32)

    for s in half_pairs:
        here = state[:, s]
        later = mm(even_lo[0, :, s], apart(here)) + even_lo[1, :, s]
        full[odd, 0, :, s] = jnp.where(is_odd, later, here)
        full[odd, 1, :, s] = jnp.where(is_odd, here, later)
    full_copy = remote(full.at[odd, 1], full.at[odd, 0], full_sem.at[0], full_sem.at[1], pair_peer)
    full_copy.start()
    full_copy.wait_recv()
    mixed = []
    for i, s in enumerate(pairs):
        at, cols = divmod(i * LANES, half_w)
        read, offset = inner[i]
        y = mm(read, apart(full[at, 0, :, cols : cols + LANES])) + offset
        spread = head_sums(y * y) * (1.0 / HS)
        extra = jnp.concatenate([bonus[0, :, s], bonus[1, :, s]], axis=0)
        mixed.append(y * lax.rsqrt(spread + 0.00064) * chan[5][:, s] + extra)
    head_mix = jnp.concatenate(mixed, axis=1).astype(BF16)

    out_load.wait()
    span = model // OUT_CHUNKS
    if line:
        routes = [
            ([(3, 1, n_wt)], [(1, 1, 0), (2, 2, 0)], (0, 0, [1, 2])),
            ([(2, 2, 1), (0, 0, 1)], [], (3, 3, [2, 0, 3])),
            ([(1, 1, 2), (3, 3, 2)], [], (0, 0, [1, 3, 0])),
            ([(0, 2, n_wt)], [(2, 2, 3), (1, 1, 3)], (0, 0, [2, 1])),
        ]
    else:
        routes = []
        for me in range(n_wt):
            others = [(me + d) % n_wt for d in range(1, n_wt)]
            routes.append(([(t, t, me) for t in others], [], (0, 0, others)))
    merging = (1, 2) if line else ()

    def rs_copy(t, to, slot, c):
        owned, cols = pl.ds(t * shard, shard), pl.ds(c * span, span)
        return remote(
            part_16.at[owned, cols], rs_in.at[slot, :, cols], rs_send.at[t, c], rs_recv.at[slot, c], (b, to)
        )

    for c in range(OUT_CHUNKS):
        cols = slice(c * span, (c + 1) * span)
        term = mm(head_mix, wout[:, cols])
        part[:, cols] = term
        part_16[:, cols] = term.astype(BF16)
        for me, (first, _, _) in enumerate(routes):
            @pl.when(w == me)
            def _():
                for route in first:
                    rs_copy(*route, c).start()

    for me, (_, later, (t, to, sources)) in enumerate(routes):
        @pl.when(w == me)
        def _():
            for route in later:
                for c in range(OUT_CHUNKS):
                    rs_copy(*route, c).start()
            if me in merging:
                owned = slice(t * shard, (t + 1) * shard)
                for c in range(OUT_CHUNKS):
                    cols = slice(c * span, (c + 1) * span)
                    rs_copy(t, to, n_wt, c).wait_recv()
                    part_16[owned, cols] = (part[owned, cols] + rs_in[n_wt, :, cols].astype(F32)).astype(BF16)
                    rs_copy(t, to, me, c).start()
            held = slice(me * shard, (me + 1) * shard)
            acc[...] = part[held, :] + x_all[held, :].astype(F32)
            for source in sources:
                for c in range(OUT_CHUNKS):
                    cols = slice(c * span, (c + 1) * span)
                    rs_copy(me, to, source, c).wait_recv()
                    acc[:, cols] += rs_in[source, :, cols].astype(F32)

    out_ref[...] = acc[...].astype(out_ref.dtype)

    @pl.when(sends_edge)
    def _():
        for copy in block_edges:
            copy.wait_send()

    @pl.when(w == mid - 1)
    def _():
        for copy in mid_edges:
            copy.wait_send()

    for d in range(1, n_wt):
        @pl.when(sends(d))
        def _():
            for h in range(X_PIECES):
                x_copy(d, h).wait_send()

    for at, owner, target, d in relays:
        @pl.when(w == at)
        def _():
            for h in range(X_PIECES):
                relay_copy(owner, target, h).wait_send()

    pair_copy.wait_send()
    full_copy.wait_send()
    for d in range(1, hops + 1):
        @pl.when(b + 2 * d < n_seq)
        def _():
            lo_copy(d).wait_send()

    for me, (first, later, (t, to, _)) in enumerate(routes):
        @pl.when(w == me)
        def _():
            for route in first + later + ([(t, to, me)] if me in merging else []):
                for c in range(OUT_CHUNKS):
                    rs_copy(*route, c).wait_send()


def shards(
    n_seq, n_wt,
    layer_input, token_shift_rates, input_projection_weight, output_matrix,
    decay_lowrank_first, decay_lowrank_second, learning_rate_first, learning_rate_second,
    decay_channel_bias, learning_rate_bias, prenorm_key_scale, written_key_share,
    present_step_coefficient, head_norm_gain, packed_request_length,
):
    shard, model = layer_input.shape
    rows = shard * n_wt
    width = decay_lowrank_second.shape[1]
    rank_w, rank_a = decay_lowrank_second.shape[0], learning_rate_second.shape[0]
    hops = (n_seq // 2 + 1) // 2
    half_w, chunk = width // 2, rows // 2
    chan = [
        v.reshape(1, width)
        for v in (
            decay_channel_bias, learning_rate_bias, prenorm_key_scale,
            written_key_share, present_step_coefficient, head_norm_gain,
        )
    ]
    vmem = pl.BlockSpec(memory_space=pltpu.VMEM)
    far = pl.BlockSpec(memory_space=pl.ANY)
    dma = pltpu.SemaphoreType.DMA
    return pl.pallas_call(
        functools.partial(kernel, n_seq, n_wt, hops),
        out_shape=pltpu.VMEM((shard, model), BF16),
        in_specs=[far] * 14 + [pl.BlockSpec(memory_space=pltpu.SMEM)],
        out_specs=vmem,
        scratch_shapes=[
            pltpu.VMEM((rows, model), BF16),
            pltpu.VMEM((8, model // 8), F32),
            pltpu.VMEM((2, 8, model // 8), F32),
            pltpu.VMEM((3, model, width), BF16),
            pltpu.VMEM((width, model), BF16),
            pltpu.VMEM((5, model), F32),
            pltpu.VMEM((rank_w, model), BF16),
            pltpu.VMEM((rank_w, width), BF16),
            pltpu.VMEM((rank_a, model), BF16),
            pltpu.VMEM((rank_a, width), BF16),
            pltpu.VMEM((6, 1, width), F32),
            pltpu.VMEM((2, HS, width), F32),
            pltpu.VMEM((2, HS, width), F32),
            pltpu.VMEM((2, chunk, width), F32),
            pltpu.VMEM((2, chunk, width), F32),
            pltpu.VMEM((2, chunk, width), F32),
            pltpu.VMEM((2, 2, HS, half_w), STATE_TYPE),
            pltpu.VMEM((2, HS, half_w), STATE_TYPE),
            pltpu.VMEM((2, HS, half_w), STATE_TYPE),
            pltpu.VMEM((hops, 2, HS, half_w), STATE_TYPE),
            pltpu.VMEM((HS, half_w), F32),
            pltpu.VMEM((2, 2, HS, half_w), F32),
            pltpu.VMEM((rows, model), F32),
            pltpu.VMEM((rows, model), BF16),
            pltpu.VMEM((n_wt + 1, shard, model), BF16),
            pltpu.VMEM((shard, model), F32),
            dma((16,)), dma((n_wt,)), dma((2,)),
            dma((n_wt - 1, X_PIECES)), dma((n_wt - 1, X_PIECES)), dma((X_PIECES,)),
            dma((2,)), dma((hops,)), dma((hops,)), dma((2,)),
            dma((n_wt, OUT_CHUNKS)), dma((n_wt + 1, OUT_CHUNKS)),
        ],
        compiler_params=pltpu.CompilerParams(
            collective_id=0, has_side_effects=True, vmem_limit_bytes=56 * 1024 * 1024
        ),
    )(
        layer_input, token_shift_rates, input_projection_weight, output_matrix,
        decay_lowrank_first.T, decay_lowrank_second, learning_rate_first.T, learning_rate_second,
        *chan, packed_request_length,
    )


def solution(mesh):
    placed = (
        P(("seq", "wt"), None),
        P(),
        P(None, None, "wt"),
        P("wt", None),
        P(),
        P(None, "wt"),
        P(),
        P(None, "wt"),
        P("wt"),
        P("wt"),
        P("wt"),
        P("wt"),
        P("wt"),
        P("wt"),
        P(),
    )
    return jax.shard_map(
        functools.partial(shards, mesh.shape["seq"], mesh.shape["wt"]),
        mesh=mesh, in_specs=placed, out_specs=P(("seq", "wt"), None), check_vma=False,
    )
```

```python
import functools
import jax
import jax.numpy as jnp
from jax import lax
from jax.experimental import pallas as pl
from jax.experimental.pallas import tpu as pltpu
from jax.sharding import PartitionSpec as P

HS = 64
LANES = 128
LOG_SCALE = 0.6065306597126334
MESH = pl.DeviceIdType.MESH
F32 = jnp.float32
BF16 = jnp.bfloat16
STATE_TYPE = BF16
OUT_CHUNKS = 4
X_PIECES = 4
RELAY_LEAD = 2


def mm(a, b, ca=1, cb=0):
    return lax.dot_general(
        a.astype(BF16), b.astype(BF16), (((ca,), (cb,)), ((), ())), preferred_element_type=F32
    )


def lane(shape):
    return lax.broadcasted_iota(jnp.int32, shape, 1)


def apart(z):
    left = lane(z.shape) < z.shape[1] // 2
    z = z.astype(F32)
    return jnp.concatenate([jnp.where(left, z, 0.0), jnp.where(left, 0.0, z)], axis=0).astype(BF16)


def own_blocks(z):
    rows = z.shape[0] // 2
    return jnp.where(lane((rows, z.shape[1])) < z.shape[1] // 2, z[:rows], z[rows:])


def pieces(z, count):
    out = []
    for _ in range(count):
        part = z.astype(BF16)
        out.append(part)
        z = z - part.astype(F32)
    return out


def head_sums(z):
    row = lax.broadcasted_iota(jnp.int32, (2 * LANES, LANES), 0) % LANES
    same = jnp.where(row // HS == lane((2 * LANES, LANES)) // HS, 1.0, 0.0).astype(BF16)
    return mm(jnp.concatenate(pieces(z, 2), axis=1), same)


def by_pair(fn, width):
    return jnp.concatenate([fn(slice(k, k + LANES)) for k in range(0, width, LANES)], axis=1)


def token_tables(first, rows, lengths):
    pos_c = first + lax.broadcasted_iota(jnp.int32, (rows, 1), 0)
    pos_r = first + lane((1, 2 * rows)) % rows
    far = jnp.int32(2**30)
    start = jnp.int32(0)
    reset = jnp.zeros((rows, 1), jnp.int32)
    seg_c = jnp.zeros((rows, 1), jnp.int32)
    seg_r = jnp.zeros((1, 2 * rows), jnp.int32)
    seg_last = jnp.int32(0)
    for length in lengths:
        reset = jnp.maximum(reset, jnp.where(pos_c == start, 1, 0))
        inside = jnp.where(start >= first, start, far)
        seg_c = seg_c + jnp.where(pos_c >= inside, 1, 0)
        seg_r = seg_r + jnp.where(pos_r >= inside, 1, 0)
        seg_last = seg_last + jnp.where(first + (rows - 1) >= inside, 1, 0)
        start = start + length
    return reset, seg_c, seg_r, seg_last


def chunk_terms(recept, keys, values, decay_in, rate_in, chan, seg_c, seg_r, seg_last):
    rows, width = keys.shape
    decay_bias, rate_bias, key_scale, share, coefficient = chan[:5]
    logw = -LOG_SCALE * jax.nn.sigmoid(decay_bias + decay_in)
    rate = jax.nn.sigmoid(rate_bias + rate_in)
    tri_r = lax.broadcasted_iota(jnp.int32, (rows, 3 * rows), 0)
    tri = jnp.where(tri_r >= lane((rows, 3 * rows)) % rows, 1.0, 0.0).astype(BF16)
    cum = mm(tri, jnp.concatenate(pieces(logw, 3), axis=0))
    center = cum[rows // 2 - 1 : rows // 2]
    last = cum[rows - 1 : rows]
    grow = jnp.exp(cum - center)
    grow_x = jnp.exp(cum - logw - center)
    shrink = jnp.exp(center - cum)
    to_start = jnp.exp(center) * jnp.where(seg_c == 0, 1.0, 0.0)
    to_end = jnp.exp(last - center) * jnp.where(seg_c == seg_last, 1.0, 0.0)
    scaled = keys * key_scale
    squares = scaled * scaled
    norm = by_pair(lambda s: lax.rsqrt(head_sums(squares[:, s]) + 1e-06), width)
    unit = scaled * norm
    keys_mod = keys * (1.0 + (rate - 1.0) * share)
    centered = values - by_pair(lambda s: head_sums(values[:, s]) * (1.0 / HS), width)
    u_c = unit * grow_x
    q_c = recept * grow
    r_c = unit * rate * shrink
    k_c = keys_mod * shrink
    u_0 = u_c * to_start
    q_0 = q_c * to_start
    r_e = r_c * to_end
    k_e = k_c * to_end
    row = lax.broadcasted_iota(jnp.int32, (rows, 2 * rows), 0)
    col = lane((rows, 2 * rows)) % rows
    same = seg_c == seg_r
    strict = jnp.logical_and(same, row > col)
    causal = jnp.logical_and(same, row >= col)
    pairs = [slice(k, k + LANES) for k in range(0, width, LANES)]
    a_ur, a_k, a_qr = [], [], []
    for s in pairs:
        left = jnp.concatenate([u_c[:, s], q_c[:, s]], axis=0)
        right = jnp.concatenate([apart(r_c[:, s]), apart(k_c[:, s])], axis=0)
        both = mm(left, right, 1, 1)
        a_ur.append(jnp.where(strict, both[:rows, : 2 * rows], 0.0))
        a_qr.append(jnp.where(causal, both[rows:, : 2 * rows], 0.0).astype(BF16))
        a_k.append(
            jnp.concatenate(
                [
                    jnp.where(strict, both[:rows, 2 * rows :], 0.0),
                    jnp.where(causal, both[rows:, 2 * rows :], 0.0),
                ],
                axis=0,
            ).astype(BF16)
        )
    kvs = [mm(a, apart(centered[:, s])) for a, s in zip(a_k, pairs)]
    eye = jnp.where(row == col, 1.0, 0.0)
    inverse = None
    size = 1
    while size < rows:
        tile_r, tile_c = row // size, col // size
        corner = jnp.logical_and(tile_r == tile_c + 1, tile_r % 2 == 1)
        lows = [jnp.where(corner, a, 0.0) for a in a_ur]
        if inverse is None:
            inverse = [eye - low for low in lows]
        else:
            halves = [mm(x, apart(low)) for x, low in zip(inverse, lows)]
            inverse = [x - mm(half, apart(x)) for x, half in zip(inverse, halves)]
        size *= 2
    solved = [
        mm(x, jnp.concatenate([apart(u_0[:, s]), apart(kv[:rows])], axis=1))
        for x, kv, s in zip(inverse, kvs, pairs)
    ]
    small_r = lax.broadcasted_iota(jnp.int32, (HS, LANES), 0)
    decay_all = jnp.exp(last) * jnp.where(seg_last == 0, 1.0, 0.0)
    diagonal = small_r == lane((HS, LANES)) % HS
    maps, adds = [], []
    for sol, s in zip(solved, pairs):
        into = jnp.concatenate([r_e[:, s], k_e[:, s]], axis=0)
        right = jnp.concatenate(
            [-sol, jnp.concatenate([jnp.zeros((rows, LANES), F32), centered[:, s]], axis=1)], axis=0
        )
        end = mm(into, right, 0, 0)
        diag = jnp.where(diagonal, jnp.broadcast_to(decay_all[:, s], (HS, LANES)), 0.0)
        maps.append(diag + own_blocks(end[:, :LANES]))
        adds.append(own_blocks(end[:, LANES:]))

    def rest():
        reads, offsets, bonus = [], [], []
        own = recept * keys_mod * coefficient
        for a, sol, kv, s in zip(a_qr, solved, kvs, pairs):
            right = jnp.concatenate([apart(sol[:, :LANES]), apart(sol[:, LANES:])], axis=1)
            out = jnp.concatenate([q_0[:, s], kv[rows:]], axis=1) - mm(a, right)
            reads.append(out[:, :LANES])
            offsets.append(out[:, LANES:])
            bonus.append(head_sums(own[:, s]) * values[:, s])
        return [jnp.concatenate(z, axis=1) for z in (reads, offsets, bonus)]

    return jnp.concatenate(maps, axis=1), jnp.concatenate(adds, axis=1), rest


def kernel(
    n_seq, n_wt, hops,
    x_hbm, rates_hbm, win_hbm, wout_hbm, d1_hbm, d2_hbm, a1_hbm, a2_hbm,
    db_hbm, rb_hbm, ks_hbm, sh_hbm, co_hbm, ga_hbm, len_ref,
    out_ref,
    x_all, edge_src, edge_in, win, wout, rates, d1, d2, a1, a2, chans,
    maps, adds, reads, offsets, bonus,
    lo_src, pair_in, chip_src, lo_in, state, full, part, part_16, rs_in, acc,
    w_sem, edge_send, edge_recv, x_send, x_recv, fwd_sem, pair_sem, lo_send, lo_recv, full_sem,
    rs_send, rs_recv,
):
    b = lax.axis_index("seq")
    w = lax.axis_index("wt")
    shard, model = x_hbm.shape
    rows = shard * n_wt
    width = win.shape[2]
    half_w = width // 2
    chunk = rows // 2
    mid = n_wt // 2
    top = n_wt - 1
    odd = lax.rem(b, 2)
    chip = b // 2
    piece = model // 8
    near = w // mid

    def wt_peer(d):
        return (b, lax.rem(w + d, n_wt))

    def seq_peer(d):
        return (lax.rem(b + d, n_seq), w)

    pair_peer = (b + 1 - 2 * odd, w)
    before = lax.rem(b + n_seq - 1, n_seq)
    after = lax.rem(b + 1, n_seq)

    barrier = pltpu.get_barrier_semaphore()

    def greet(target):
        pl.semaphore_signal(barrier, inc=1, device_id=target, device_id_type=MESH)

    for d in range(1, n_wt):
        greet(wt_peer(d))
    greet(pair_peer)
    for d in range(1, hops + 1):
        @pl.when(b >= 2 * d)
        def _():
            greet((lax.rem(b + n_seq - 2 * d, n_seq), w))

    @pl.when(b >= 1)
    def _():
        greet((before, top))

    mine = pl.ds(pl.multiple_of(w * shard, shard), shard)
    x_load = pltpu.make_async_copy(x_hbm, x_all.at[mine], w_sem.at[0])
    x_load.start()
    small = [(rates_hbm, rates), (d1_hbm, d1), (a1_hbm, a1), (d2_hbm, d2), (a2_hbm, a2)]
    small += [(ref, chans.at[i]) for i, ref in enumerate((db_hbm, rb_hbm, ks_hbm, sh_hbm, co_hbm, ga_hbm))]
    small += [(win_hbm.at[c], win.at[c]) for c in range(3)]
    loads = [pltpu.make_async_copy(src, dst, w_sem.at[1 + i]) for i, (src, dst) in enumerate(small)]
    out_load = pltpu.make_async_copy(wout_hbm, wout, w_sem.at[1 + len(small)])
    for load in loads:
        load.start()
    out_load.start()
    x_load.wait()
    last_row = x_all[pl.ds(pl.multiple_of(w * shard + shard - 16, 16), 16), :][15:16].astype(F32)
    for i in range(8):
        edge_src[i : i + 1, :] = last_row[:, i * piece : (i + 1) * piece]

    sends_edge = jnp.logical_and(w == top, b < n_seq - 1)
    expected = top + 1 + jnp.where(sends_edge, n_wt, 0)
    for d in range(1, hops + 1):
        expected = expected + jnp.where(b + 2 * d < n_seq, 1, 0)
    pl.semaphore_wait(barrier, expected)

    def remote(src, dst, send, recv, target):
        return pltpu.make_async_remote_copy(
            src_ref=src, dst_ref=dst, send_sem=send, recv_sem=recv, device_id=target, device_id_type=MESH
        )

    block_edges = [
        remote(edge_src, edge_in.at[0], edge_send.at[i], edge_recv.at[0], (after, i)) for i in range(n_wt)
    ]
    mid_edges = [
        remote(edge_src, edge_in.at[1], edge_send.at[i], edge_recv.at[1], (b, i)) for i in range(mid, n_wt)
    ]

    @pl.when(sends_edge)
    def _():
        for copy in block_edges:
            copy.start()

    @pl.when(w == mid - 1)
    def _():
        for copy in mid_edges:
            copy.start()

    line = n_wt == 4
    step = model // X_PIECES

    def piece_of(owner, h):
        return x_all.at[pl.ds(pl.multiple_of(owner * shard, shard), shard), pl.ds(h * step, step)]

    def x_copy(d, h):
        place = piece_of(w, h)
        return remote(place, place, x_send.at[d - 1, h], x_recv.at[d - 1, h], wt_peer(d))

    def sends(d):
        if line and d == 2:
            return jnp.logical_or(w == 0, w == top)
        return w >= 0

    pieces = range(X_PIECES)
    if line:
        sequences = [
            [(d, h) for d in (1, 3, 2) for h in pieces],
            [(d, h) for h in pieces for d in (3, 1)],
            [(d, h) for h in pieces for d in (1, 3)],
            [(d, h) for d in (3, 1, 2) for h in pieces],
        ]
    else:
        sequences = [[(d, h) for d in range(1, n_wt) for h in pieces]] * n_wt
    for me, sequence in enumerate(sequences):
        @pl.when(w == me)
        def _():
            for d, h in sequence:
                x_copy(d, h).start()

    relays = [(1, 2, 0, 3), (2, 1, 3, 1)] if line else []

    def relay_copy(owner, target, h):
        place = piece_of(owner, h)
        return remote(place, place, fwd_sem.at[h], x_recv.at[1, h], (b, target))

    def is_near(d):
        return lax.rem(w + n_wt - d, n_wt) // mid == near

    def relayed(d):
        out = w < 0
        for at, _, _, which in relays:
            if which == d:
                out = jnp.logical_or(out, w == at)
        return out

    def relay(h):
        for at, owner, target, d in relays:
            @pl.when(w == at)
            def _():
                x_copy(d, h).wait_recv()
                relay_copy(owner, target, h).start()

    for h in range(RELAY_LEAD):
        relay(h)

    def near_arrival(h):
        if h + RELAY_LEAD < X_PIECES:
            relay(h + RELAY_LEAD)
        for d in range(1, n_wt):
            @pl.when(is_near(d))
            def _():
                x_copy(d, h).wait_recv()

    @pl.when(b >= 1)
    def _():
        block_edges[0].wait_recv()

    @pl.when(near == 1)
    def _():
        mid_edges[0].wait_recv()

    for load in loads:
        load.wait()
    lengths = [len_ref[i] for i in range(len_ref.shape[0])]
    chan = [chans[i] for i in range(6)]
    first_row = lax.broadcasted_iota(jnp.int32, (chunk, 1), 0) == 0

    def do_chunk(which, edge, arrival):
        base = pl.ds(pl.multiple_of(which * chunk, chunk), chunk)
        reset, seg_c, seg_r, seg_last = token_tables(b * rows + which * chunk, chunk, lengths)
        sums = [None] * 5
        for h in range(X_PIECES):
            arrival(h)
            cols = slice(h * step, (h + 1) * step)
            current = x_all[base, cols].astype(F32)
            previous = jnp.where(first_row, edge[:, cols], pltpu.roll(current, 1, 0))
            previous = jnp.where(reset == 1, 0.0, previous)
            delta = previous - current
            for c in range(5):
                mixed = (current + delta * rates[c : c + 1, cols]).astype(BF16)
                if c < 3:
                    term = mm(mixed, win[c, cols, :])
                else:
                    term = mm(mixed, (d1 if c == 3 else a1)[:, cols], 1, 1)
                sums[c] = term if sums[c] is None else sums[c] + term
        decay_in = mm(jnp.tanh(sums[3]), d2[...])
        rate_in = mm(sums[4], a2[...])
        m, a, rest = chunk_terms(*sums[:3], decay_in, rate_in, chan, seg_c, seg_r, seg_last)
        maps[which] = m
        adds[which] = a

        def finish():
            reads[which], offsets[which], bonus[which] = rest()

        return finish

    def edge_row(i):
        return jnp.concatenate([edge_in[i, r : r + 1, :] for r in range(8)], axis=1)

    def near_last_row():
        at = pl.ds(pl.multiple_of((near + 1) * chunk - 16, 16), 16)
        return x_all[at, :][15:16].astype(F32)

    do_chunk(near, jnp.where(near == 0, edge_row(0), edge_row(1)), near_arrival)()

    def far_arrival(h):
        for d in range(1, n_wt):
            @pl.when(jnp.logical_not(jnp.logical_or(is_near(d), relayed(d))))
            def _():
                x_copy(d, h).wait_recv()

    far_rest = do_chunk(1 - near, jnp.where(near == 1, edge_row(0), near_last_row()), far_arrival)

    pairs = [slice(k, k + LANES) for k in range(0, width, LANES)]
    half_pairs = [slice(k, k + LANES) for k in range(0, half_w, LANES)]

    def compose(later, earlier):
        both = mm(later[0], jnp.concatenate([apart(earlier[0]), apart(earlier[1])], axis=1))
        return both[:, :LANES], both[:, LANES:] + later[1]

    for i, s in enumerate(pairs):
        m, a = compose((maps[1, :, s], adds[1, :, s]), (maps[0, :, s], adds[0, :, s]))
        at, cols = divmod(i * LANES, half_w)
        lo_src[at, 0, :, cols : cols + LANES] = m.astype(STATE_TYPE)
        lo_src[at, 1, :, cols : cols + LANES] = a.astype(STATE_TYPE)
    pair_copy = remote(lo_src.at[1 - odd], pair_in, pair_sem.at[0], pair_sem.at[1], pair_peer)
    pair_copy.start()
    far_rest()
    pair_copy.wait_recv()
    is_odd = odd == 1
    mine_lo = lo_src[odd].astype(F32)
    other_lo = pair_in[...].astype(F32)
    even_lo = jnp.where(is_odd, other_lo, mine_lo)
    odd_lo = jnp.where(is_odd, mine_lo, other_lo)
    for s in half_pairs:
        m, a = compose((odd_lo[0, :, s], odd_lo[1, :, s]), (even_lo[0, :, s], even_lo[1, :, s]))
        chip_src[0, :, s] = m.astype(STATE_TYPE)
        chip_src[1, :, s] = a.astype(STATE_TYPE)

    def lo_copy(d):
        if d == hops:
            return remote(
                chip_src.at[1], lo_in.at[d - 1, 1], lo_send.at[d - 1], lo_recv.at[d - 1], seq_peer(2 * d)
            )
        return remote(chip_src, lo_in.at[d - 1], lo_send.at[d - 1], lo_recv.at[d - 1], seq_peer(2 * d))

    for d in range(1, hops + 1):
        @pl.when(b + 2 * d < n_seq)
        def _():
            lo_copy(d).start()

    state[...] = jnp.zeros_like(state)
    inner = []
    for s in pairs:
        right = jnp.concatenate([apart(maps[0, :, s]), apart(adds[0, :, s])], axis=1)
        late = mm(reads[1, :, s], right)
        inner.append(
            (
                jnp.concatenate([reads[0, :, s], late[:, :LANES]], axis=0).astype(BF16),
                jnp.concatenate([offsets[0, :, s], offsets[1, :, s] + late[:, LANES:]], axis=0),
            )
        )
    for d in range(hops, 0, -1):
        @pl.when(chip >= d)
        def _():
            lo_copy(d).wait_recv()
            if d == hops:
                state[...] = lo_in[d - 1, 1].astype(F32)
            else:
                for s in half_pairs:
                    state[:, s] = mm(lo_in[d - 1, 0, :, s], apart(state[:, s])) + lo_in[
                        d - 1, 1, :, s
                    ].astype(F32)

    for s in half_pairs:
        here = state[:, s]
        later = mm(even_lo[0, :, s], apart(here)) + even_lo[1, :, s]
        full[odd, 0, :, s] = jnp.where(is_odd, later, here)
        full[odd, 1, :, s] = jnp.where(is_odd, here, later)
    full_copy = remote(full.at[odd, 1], full.at[odd, 0], full_sem.at[0], full_sem.at[1], pair_peer)
    full_copy.start()
    full_copy.wait_recv()
    mixed = []
    for i, s in enumerate(pairs):
        at, cols = divmod(i * LANES, half_w)
        read, offset = inner[i]
        y = mm(read, apart(full[at, 0, :, cols : cols + LANES])) + offset
        spread = head_sums(y * y) * (1.0 / HS)
        extra = jnp.concatenate([bonus[0, :, s], bonus[1, :, s]], axis=0)
        mixed.append(y * lax.rsqrt(spread + 0.00064) * chan[5][:, s] + extra)
    head_mix = jnp.concatenate(mixed, axis=1).astype(BF16)

    out_load.wait()
    span = model // OUT_CHUNKS
    if line:
        routes = [
            ([(3, 1, n_wt)], [(2, 1, n_wt + 1), (1, 1, 0)], [], [1, 2]),
            ([(0, 0, 1)], [], [(3, 3, 1), (2, 2, 1)], [2, 0]),
            ([(3, 3, 2)], [], [(0, 0, 2), (1, 1, 2)], [1, 3]),
            ([(0, 2, n_wt)], [(1, 2, n_wt + 1), (2, 2, 3)], [], [2, 1]),
        ]
    else:
        routes = []
        for me in range(n_wt):
            others = [(me + d) % n_wt for d in range(1, n_wt)]
            routes.append(([(t, t, me) for t in others], [], [], others))

    def rs_copy(t, to, slot, c):
        owned, cols = pl.ds(t * shard, shard), pl.ds(c * span, span)
        return remote(
            part_16.at[owned, cols], rs_in.at[slot, :, cols], rs_send.at[t, c], rs_recv.at[slot, c], (b, to)
        )

    for c in range(OUT_CHUNKS):
        cols = slice(c * span, (c + 1) * span)
        term = mm(head_mix, wout[:, cols])
        part[:, cols] = term
        part_16[:, cols] = term.astype(BF16)
        for me, (first, _, _, _) in enumerate(routes):
            @pl.when(w == me)
            def _():
                for route in first:
                    rs_copy(*route, c).start()

    for me, (_, later, merged, sources) in enumerate(routes):
        @pl.when(w == me)
        def _():
            for route in later:
                for c in range(OUT_CHUNKS):
                    rs_copy(*route, c).start()
            for i, (t, to, slot) in enumerate(merged):
                owned = slice(t * shard, (t + 1) * shard)
                for c in range(OUT_CHUNKS):
                    cols = slice(c * span, (c + 1) * span)
                    rs_copy(t, to, n_wt + i, c).wait_recv()
                    total = part[owned, cols] + rs_in[n_wt + i, :, cols].astype(F32)
                    part_16[owned, cols] = total.astype(BF16)
                    rs_copy(t, to, slot, c).start()
            held = slice(me * shard, (me + 1) * shard)
            acc[...] = part[held, :] + x_all[held, :].astype(F32)
            for source in sources:
                for c in range(OUT_CHUNKS):
                    cols = slice(c * span, (c + 1) * span)
                    rs_copy(me, (me + 1) % n_wt, source, c).wait_recv()
                    acc[:, cols] += rs_in[source, :, cols].astype(F32)

    out_ref[...] = acc[...].astype(out_ref.dtype)

    @pl.when(sends_edge)
    def _():
        for copy in block_edges:
            copy.wait_send()

    @pl.when(w == mid - 1)
    def _():
        for copy in mid_edges:
            copy.wait_send()

    for d in range(1, n_wt):
        @pl.when(sends(d))
        def _():
            for h in range(X_PIECES):
                x_copy(d, h).wait_send()

    for at, owner, target, d in relays:
        @pl.when(w == at)
        def _():
            for h in range(X_PIECES):
                relay_copy(owner, target, h).wait_send()

    pair_copy.wait_send()
    full_copy.wait_send()
    for d in range(1, hops + 1):
        @pl.when(b + 2 * d < n_seq)
        def _():
            lo_copy(d).wait_send()

    for me, (first, later, merged, _) in enumerate(routes):
        @pl.when(w == me)
        def _():
            for route in first + later + merged:
                for c in range(OUT_CHUNKS):
                    rs_copy(*route, c).wait_send()


def shards(
    n_seq, n_wt,
    layer_input, token_shift_rates, input_projection_weight, output_matrix,
    decay_lowrank_first, decay_lowrank_second, learning_rate_first, learning_rate_second,
    decay_channel_bias, learning_rate_bias, prenorm_key_scale, written_key_share,
    present_step_coefficient, head_norm_gain, packed_request_length,
):
    shard, model = layer_input.shape
    rows = shard * n_wt
    width = decay_lowrank_second.shape[1]
    rank_w, rank_a = decay_lowrank_second.shape[0], learning_rate_second.shape[0]
    hops = (n_seq // 2 + 1) // 2
    half_w, chunk = width // 2, rows // 2
    chan = [
        v.reshape(1, width)
        for v in (
            decay_channel_bias, learning_rate_bias, prenorm_key_scale,
            written_key_share, present_step_coefficient, head_norm_gain,
        )
    ]
    vmem = pl.BlockSpec(memory_space=pltpu.VMEM)
    far = pl.BlockSpec(memory_space=pl.ANY)
    dma = pltpu.SemaphoreType.DMA
    return pl.pallas_call(
        functools.partial(kernel, n_seq, n_wt, hops),
        out_shape=pltpu.VMEM((shard, model), BF16),
        in_specs=[far] * 14 + [pl.BlockSpec(memory_space=pltpu.SMEM)],
        out_specs=vmem,
        scratch_shapes=[
            pltpu.VMEM((rows, model), BF16),
            pltpu.VMEM((8, model // 8), F32),
            pltpu.VMEM((2, 8, model // 8), F32),
            pltpu.VMEM((3, model, width), BF16),
            pltpu.VMEM((width, model), BF16),
            pltpu.VMEM((5, model), F32),
            pltpu.VMEM((rank_w, model), BF16),
            pltpu.VMEM((rank_w, width), BF16),
            pltpu.VMEM((rank_a, model), BF16),
            pltpu.VMEM((rank_a, width), BF16),
            pltpu.VMEM((6, 1, width), F32),
            pltpu.VMEM((2, HS, width), F32),
            pltpu.VMEM((2, HS, width), F32),
            pltpu.VMEM((2, chunk, width), F32),
            pltpu.VMEM((2, chunk, width), F32),
            pltpu.VMEM((2, chunk, width), F32),
            pltpu.VMEM((2, 2, HS, half_w), STATE_TYPE),
            pltpu.VMEM((2, HS, half_w), STATE_TYPE),
            pltpu.VMEM((2, HS, half_w), STATE_TYPE),
            pltpu.VMEM((hops, 2, HS, half_w), STATE_TYPE),
            pltpu.VMEM((HS, half_w), F32),
            pltpu.VMEM((2, 2, HS, half_w), F32),
            pltpu.VMEM((rows, model), F32),
            pltpu.VMEM((rows, model), BF16),
            pltpu.VMEM((n_wt + 2, shard, model), BF16),
            pltpu.VMEM((shard, model), F32),
            dma((16,)), dma((n_wt,)), dma((2,)),
            dma((n_wt - 1, X_PIECES)), dma((n_wt - 1, X_PIECES)), dma((X_PIECES,)),
            dma((2,)), dma((hops,)), dma((hops,)), dma((2,)),
            dma((n_wt, OUT_CHUNKS)), dma((n_wt + 2, OUT_CHUNKS)),
        ],
        compiler_params=pltpu.CompilerParams(
            collective_id=0, has_side_effects=True, vmem_limit_bytes=56 * 1024 * 1024
        ),
    )(
        layer_input, token_shift_rates, input_projection_weight, output_matrix,
        decay_lowrank_first.T, decay_lowrank_second, learning_rate_first.T, learning_rate_second,
        *chan, packed_request_length,
    )


def solution(mesh):
    placed = (
        P(("seq", "wt"), None),
        P(),
        P(None, None, "wt"),
        P("wt", None),
        P(),
        P(None, "wt"),
        P(),
        P(None, "wt"),
        P("wt"),
        P("wt"),
        P("wt"),
        P("wt"),
        P("wt"),
        P("wt"),
        P(),
    )
    return jax.shard_map(
        functools.partial(shards, mesh.shape["seq"], mesh.shape["wt"]),
        mesh=mesh, in_specs=placed, out_specs=P(("seq", "wt"), None), check_vma=False,
    )
```

```python
import functools
import jax
import jax.numpy as jnp
from jax import lax
from jax.experimental import pallas as pl
from jax.experimental.pallas import tpu as pltpu
from jax.sharding import PartitionSpec as P

HS = 64
LANES = 128
LOG_SCALE = 0.6065306597126334
MESH = pl.DeviceIdType.MESH
F32 = jnp.float32
BF16 = jnp.bfloat16
STATE_TYPE = BF16
OUT_CHUNKS = 4
X_PIECES = 4
RELAY_LEAD = 4


def mm(a, b, ca=1, cb=0):
    return lax.dot_general(
        a.astype(BF16), b.astype(BF16), (((ca,), (cb,)), ((), ())), preferred_element_type=F32
    )


def lane(shape):
    return lax.broadcasted_iota(jnp.int32, shape, 1)


def apart(z):
    left = lane(z.shape) < z.shape[1] // 2
    z = z.astype(F32)
    return jnp.concatenate([jnp.where(left, z, 0.0), jnp.where(left, 0.0, z)], axis=0).astype(BF16)


def own_blocks(z):
    rows = z.shape[0] // 2
    return jnp.where(lane((rows, z.shape[1])) < z.shape[1] // 2, z[:rows], z[rows:])


def pieces(z, count):
    out = []
    for _ in range(count):
        part = z.astype(BF16)
        out.append(part)
        z = z - part.astype(F32)
    return out


def head_sums(z):
    row = lax.broadcasted_iota(jnp.int32, (2 * LANES, LANES), 0) % LANES
    same = jnp.where(row // HS == lane((2 * LANES, LANES)) // HS, 1.0, 0.0).astype(BF16)
    return mm(jnp.concatenate(pieces(z, 2), axis=1), same)


def by_pair(fn, width):
    return jnp.concatenate([fn(slice(k, k + LANES)) for k in range(0, width, LANES)], axis=1)


def token_tables(first, rows, lengths):
    pos_c = first + lax.broadcasted_iota(jnp.int32, (rows, 1), 0)
    pos_r = first + lane((1, 2 * rows)) % rows
    far = jnp.int32(2**30)
    start = jnp.int32(0)
    reset = jnp.zeros((rows, 1), jnp.int32)
    seg_c = jnp.zeros((rows, 1), jnp.int32)
    seg_r = jnp.zeros((1, 2 * rows), jnp.int32)
    seg_last = jnp.int32(0)
    for length in lengths:
        reset = jnp.maximum(reset, jnp.where(pos_c == start, 1, 0))
        inside = jnp.where(start >= first, start, far)
        seg_c = seg_c + jnp.where(pos_c >= inside, 1, 0)
        seg_r = seg_r + jnp.where(pos_r >= inside, 1, 0)
        seg_last = seg_last + jnp.where(first + (rows - 1) >= inside, 1, 0)
        start = start + length
    return reset, seg_c, seg_r, seg_last


def chunk_terms(recept, keys, values, decay_in, rate_in, chan, seg_c, seg_r, seg_last):
    rows, width = keys.shape
    decay_bias, rate_bias, key_scale, share, coefficient = chan[:5]
    logw = -LOG_SCALE * jax.nn.sigmoid(decay_bias + decay_in)
    rate = jax.nn.sigmoid(rate_bias + rate_in)
    tri_r = lax.broadcasted_iota(jnp.int32, (rows, 3 * rows), 0)
    tri = jnp.where(tri_r >= lane((rows, 3 * rows)) % rows, 1.0, 0.0).astype(BF16)
    cum = mm(tri, jnp.concatenate(pieces(logw, 3), axis=0))
    center = cum[rows // 2 - 1 : rows // 2]
    last = cum[rows - 1 : rows]
    grow = jnp.exp(cum - center)
    grow_x = jnp.exp(cum - logw - center)
    shrink = jnp.exp(center - cum)
    to_start = jnp.exp(center) * jnp.where(seg_c == 0, 1.0, 0.0)
    to_end = jnp.exp(last - center) * jnp.where(seg_c == seg_last, 1.0, 0.0)
    scaled = keys * key_scale
    squares = scaled * scaled
    norm = by_pair(lambda s: lax.rsqrt(head_sums(squares[:, s]) + 1e-06), width)
    unit = scaled * norm
    keys_mod = keys * (1.0 + (rate - 1.0) * share)
    centered = values - by_pair(lambda s: head_sums(values[:, s]) * (1.0 / HS), width)
    u_c = unit * grow_x
    q_c = recept * grow
    r_c = unit * rate * shrink
    k_c = keys_mod * shrink
    u_0 = u_c * to_start
    q_0 = q_c * to_start
    r_e = r_c * to_end
    k_e = k_c * to_end
    row = lax.broadcasted_iota(jnp.int32, (rows, 2 * rows), 0)
    col = lane((rows, 2 * rows)) % rows
    same = seg_c == seg_r
    strict = jnp.logical_and(same, row > col)
    causal = jnp.logical_and(same, row >= col)
    pairs = [slice(k, k + LANES) for k in range(0, width, LANES)]
    a_ur, a_k, a_qr = [], [], []
    for s in pairs:
        left = jnp.concatenate([u_c[:, s], q_c[:, s]], axis=0)
        right = jnp.concatenate([apart(r_c[:, s]), apart(k_c[:, s])], axis=0)
        both = mm(left, right, 1, 1)
        a_ur.append(jnp.where(strict, both[:rows, : 2 * rows], 0.0))
        a_qr.append(jnp.where(causal, both[rows:, : 2 * rows], 0.0).astype(BF16))
        a_k.append(
            jnp.concatenate(
                [
                    jnp.where(strict, both[:rows, 2 * rows :], 0.0),
                    jnp.where(causal, both[rows:, 2 * rows :], 0.0),
                ],
                axis=0,
            ).astype(BF16)
        )
    kvs = [mm(a, apart(centered[:, s])) for a, s in zip(a_k, pairs)]
    eye = jnp.where(row == col, 1.0, 0.0)
    inverse, carried = None, a_ur
    size = 1
    while size < rows:
        tile_r, tile_c = row // size, col // size
        corner = jnp.logical_and(tile_r == tile_c + 1, tile_r % 2 == 1)
        lows = [jnp.where(corner, a, 0.0).astype(BF16) for a in carried]
        size *= 2
        if inverse is None:
            inverse = [eye - low.astype(F32) for low in lows]
            carried = [a - mm(low, apart(a)) for low, a in zip(lows, carried)]
        elif size < rows:
            steps = [
                mm(low, jnp.concatenate([apart(x), apart(a)], axis=1))
                for low, x, a in zip(lows, inverse, carried)
            ]
            inverse = [x - step[:, : 2 * rows] for x, step in zip(inverse, steps)]
            carried = [a - step[:, 2 * rows :] for a, step in zip(carried, steps)]
        else:
            inverse = [x - mm(low, apart(x)) for low, x in zip(lows, inverse)]
    solved = [
        mm(x, jnp.concatenate([apart(u_0[:, s]), apart(kv[:rows])], axis=1))
        for x, kv, s in zip(inverse, kvs, pairs)
    ]
    small_r = lax.broadcasted_iota(jnp.int32, (HS, LANES), 0)
    decay_all = jnp.exp(last) * jnp.where(seg_last == 0, 1.0, 0.0)
    diagonal = small_r == lane((HS, LANES)) % HS
    maps, adds = [], []
    for sol, s in zip(solved, pairs):
        into = jnp.concatenate([r_e[:, s], k_e[:, s]], axis=0)
        right = jnp.concatenate(
            [-sol, jnp.concatenate([jnp.zeros((rows, LANES), F32), centered[:, s]], axis=1)], axis=0
        )
        end = mm(into, right, 0, 0)
        diag = jnp.where(diagonal, jnp.broadcast_to(decay_all[:, s], (HS, LANES)), 0.0)
        maps.append(diag + own_blocks(end[:, :LANES]))
        adds.append(own_blocks(end[:, LANES:]))

    def rest():
        reads, offsets, bonus = [], [], []
        own = recept * keys_mod * coefficient
        for a, sol, kv, s in zip(a_qr, solved, kvs, pairs):
            right = jnp.concatenate([apart(sol[:, :LANES]), apart(sol[:, LANES:])], axis=1)
            out = jnp.concatenate([q_0[:, s], kv[rows:]], axis=1) - mm(a, right)
            reads.append(out[:, :LANES])
            offsets.append(out[:, LANES:])
            bonus.append(head_sums(own[:, s]) * values[:, s])
        return [jnp.concatenate(z, axis=1) for z in (reads, offsets, bonus)]

    return jnp.concatenate(maps, axis=1), jnp.concatenate(adds, axis=1), rest


def kernel(
    n_seq, n_wt, hops,
    x_hbm, rates_hbm, win_hbm, wout_hbm, d1_hbm, d2_hbm, a1_hbm, a2_hbm,
    db_hbm, rb_hbm, ks_hbm, sh_hbm, co_hbm, ga_hbm, len_ref,
    out_ref,
    x_all, edge_src, edge_in, win, wout, rates, d1, d2, a1, a2, chans,
    maps, adds, reads, offsets, bonus,
    lo_src, pair_in, chip_src, lo_in, state, full, part, part_16, rs_in, acc,
    w_sem, edge_send, edge_recv, x_send, x_recv, fwd_sem, pair_sem, lo_send, lo_recv, full_sem,
    rs_send, rs_recv,
):
    b = lax.axis_index("seq")
    w = lax.axis_index("wt")
    shard, model = x_hbm.shape
    rows = shard * n_wt
    width = win.shape[2]
    half_w = width // 2
    chunk = rows // 2
    mid = n_wt // 2
    top = n_wt - 1
    odd = lax.rem(b, 2)
    chip = b // 2
    piece = model // 8
    near = w // mid

    def wt_peer(d):
        return (b, lax.rem(w + d, n_wt))

    def seq_peer(d):
        return (lax.rem(b + d, n_seq), w)

    pair_peer = (b + 1 - 2 * odd, w)
    before = lax.rem(b + n_seq - 1, n_seq)
    after = lax.rem(b + 1, n_seq)

    barrier = pltpu.get_barrier_semaphore()

    def greet(target):
        pl.semaphore_signal(barrier, inc=1, device_id=target, device_id_type=MESH)

    for d in range(1, n_wt):
        greet(wt_peer(d))
    greet(pair_peer)
    for d in range(1, hops + 1):
        @pl.when(b >= 2 * d)
        def _():
            greet((lax.rem(b + n_seq - 2 * d, n_seq), w))

    @pl.when(b >= 1)
    def _():
        greet((before, top))

    mine = pl.ds(pl.multiple_of(w * shard, shard), shard)
    x_load = pltpu.make_async_copy(x_hbm, x_all.at[mine], w_sem.at[0])
    x_load.start()
    small = [(rates_hbm, rates), (d1_hbm, d1), (a1_hbm, a1), (d2_hbm, d2), (a2_hbm, a2)]
    small += [(ref, chans.at[i]) for i, ref in enumerate((db_hbm, rb_hbm, ks_hbm, sh_hbm, co_hbm, ga_hbm))]
    small += [(win_hbm.at[c], win.at[c]) for c in range(3)]
    loads = [pltpu.make_async_copy(src, dst, w_sem.at[1 + i]) for i, (src, dst) in enumerate(small)]
    out_load = pltpu.make_async_copy(wout_hbm, wout, w_sem.at[1 + len(small)])
    for load in loads:
        load.start()
    out_load.start()
    x_load.wait()
    last_row = x_all[pl.ds(pl.multiple_of(w * shard + shard - 16, 16), 16), :][15:16].astype(F32)
    for i in range(8):
        edge_src[i : i + 1, :] = last_row[:, i * piece : (i + 1) * piece]

    sends_edge = jnp.logical_and(w == top, b < n_seq - 1)
    expected = top + 1 + jnp.where(sends_edge, n_wt, 0)
    for d in range(1, hops + 1):
        expected = expected + jnp.where(b + 2 * d < n_seq, 1, 0)
    pl.semaphore_wait(barrier, expected)

    def remote(src, dst, send, recv, target):
        return pltpu.make_async_remote_copy(
            src_ref=src, dst_ref=dst, send_sem=send, recv_sem=recv, device_id=target, device_id_type=MESH
        )

    block_edges = [
        remote(edge_src, edge_in.at[0], edge_send.at[i], edge_recv.at[0], (after, i)) for i in range(n_wt)
    ]
    mid_edges = [
        remote(edge_src, edge_in.at[1], edge_send.at[i], edge_recv.at[1], (b, i)) for i in range(mid, n_wt)
    ]

    @pl.when(sends_edge)
    def _():
        for copy in block_edges:
            copy.start()

    @pl.when(w == mid - 1)
    def _():
        for copy in mid_edges:
            copy.start()

    line = n_wt == 4
    step = model // X_PIECES

    def piece_of(owner, h):
        return x_all.at[pl.ds(pl.multiple_of(owner * shard, shard), shard), pl.ds(h * step, step)]

    def x_copy(d, h):
        place = piece_of(w, h)
        return remote(place, place, x_send.at[d - 1, h], x_recv.at[d - 1, h], wt_peer(d))

    def sends(d):
        if line and d == 2:
            return jnp.logical_or(w == 0, w == top)
        return w >= 0

    pieces = range(X_PIECES)
    if line:
        sequences = [
            [(d, h) for d in (1, 3, 2) for h in pieces],
            [(d, h) for h in pieces for d in (3, 1)],
            [(d, h) for h in pieces for d in (1, 3)],
            [(d, h) for d in (3, 1, 2) for h in pieces],
        ]
    else:
        sequences = [[(d, h) for d in range(1, n_wt) for h in pieces]] * n_wt
    for me, sequence in enumerate(sequences):
        @pl.when(w == me)
        def _():
            for d, h in sequence:
                x_copy(d, h).start()

    relays = [(1, 2, 0, 3), (2, 1, 3, 1)] if line else []

    def relay_copy(owner, target, h):
        place = piece_of(owner, h)
        return remote(place, place, fwd_sem.at[h], x_recv.at[1, h], (b, target))

    def is_near(d):
        return lax.rem(w + n_wt - d, n_wt) // mid == near

    def relayed(d):
        out = w < 0
        for at, _, _, which in relays:
            if which == d:
                out = jnp.logical_or(out, w == at)
        return out

    def relay(h):
        for at, owner, target, d in relays:
            @pl.when(w == at)
            def _():
                x_copy(d, h).wait_recv()
                relay_copy(owner, target, h).start()

    for h in range(RELAY_LEAD):
        relay(h)

    def near_arrival(h):
        if h + RELAY_LEAD < X_PIECES:
            relay(h + RELAY_LEAD)
        for d in range(1, n_wt):
            @pl.when(is_near(d))
            def _():
                x_copy(d, h).wait_recv()

    @pl.when(b >= 1)
    def _():
        block_edges[0].wait_recv()

    @pl.when(near == 1)
    def _():
        mid_edges[0].wait_recv()

    for load in loads:
        load.wait()
    lengths = [len_ref[i] for i in range(len_ref.shape[0])]
    chan = [chans[i] for i in range(6)]
    first_row = lax.broadcasted_iota(jnp.int32, (chunk, 1), 0) == 0

    def do_chunk(which, edge, arrival):
        base = pl.ds(pl.multiple_of(which * chunk, chunk), chunk)
        reset, seg_c, seg_r, seg_last = token_tables(b * rows + which * chunk, chunk, lengths)
        sums = [None] * 5
        for h in range(X_PIECES):
            arrival(h)
            cols = slice(h * step, (h + 1) * step)
            current = x_all[base, cols].astype(F32)
            previous = jnp.where(first_row, edge[:, cols], pltpu.roll(current, 1, 0))
            previous = jnp.where(reset == 1, 0.0, previous)
            delta = previous - current
            for c in (3, 4, 0, 1, 2):
                mixed = (current + delta * rates[c : c + 1, cols]).astype(BF16)
                if c < 3:
                    term = mm(mixed, win[c, cols, :])
                else:
                    term = mm(mixed, (d1 if c == 3 else a1)[:, cols], 1, 1)
                sums[c] = term if sums[c] is None else sums[c] + term
        decay_in = mm(jnp.tanh(sums[3]), d2[...])
        rate_in = mm(sums[4], a2[...])
        m, a, rest = chunk_terms(*sums[:3], decay_in, rate_in, chan, seg_c, seg_r, seg_last)
        maps[which] = m
        adds[which] = a

        def finish():
            reads[which], offsets[which], bonus[which] = rest()

        return finish

    def edge_row(i):
        return jnp.concatenate([edge_in[i, r : r + 1, :] for r in range(8)], axis=1)

    def near_last_row():
        at = pl.ds(pl.multiple_of((near + 1) * chunk - 16, 16), 16)
        return x_all[at, :][15:16].astype(F32)

    do_chunk(near, jnp.where(near == 0, edge_row(0), edge_row(1)), near_arrival)()

    def far_arrival(h):
        for d in range(1, n_wt):
            @pl.when(jnp.logical_not(jnp.logical_or(is_near(d), relayed(d))))
            def _():
                x_copy(d, h).wait_recv()

    far_rest = do_chunk(1 - near, jnp.where(near == 1, edge_row(0), near_last_row()), far_arrival)

    pairs = [slice(k, k + LANES) for k in range(0, width, LANES)]
    half_pairs = [slice(k, k + LANES) for k in range(0, half_w, LANES)]

    def compose(later, earlier):
        both = mm(later[0], jnp.concatenate([apart(earlier[0]), apart(earlier[1])], axis=1))
        return both[:, :LANES], both[:, LANES:] + later[1]

    for i, s in enumerate(pairs):
        m, a = compose((maps[1, :, s], adds[1, :, s]), (maps[0, :, s], adds[0, :, s]))
        at, cols = divmod(i * LANES, half_w)
        lo_src[at, 0, :, cols : cols + LANES] = m.astype(STATE_TYPE)
        lo_src[at, 1, :, cols : cols + LANES] = a.astype(STATE_TYPE)
    pair_copy = remote(lo_src.at[1 - odd], pair_in, pair_sem.at[0], pair_sem.at[1], pair_peer)
    pair_copy.start()
    far_rest()
    pair_copy.wait_recv()
    is_odd = odd == 1
    mine_lo = lo_src[odd].astype(F32)
    other_lo = pair_in[...].astype(F32)
    even_lo = jnp.where(is_odd, other_lo, mine_lo)
    odd_lo = jnp.where(is_odd, mine_lo, other_lo)
    for s in half_pairs:
        m, a = compose((odd_lo[0, :, s], odd_lo[1, :, s]), (even_lo[0, :, s], even_lo[1, :, s]))
        chip_src[0, :, s] = m.astype(STATE_TYPE)
        chip_src[1, :, s] = a.astype(STATE_TYPE)

    def lo_copy(d):
        if d == hops:
            return remote(
                chip_src.at[1], lo_in.at[d - 1, 1], lo_send.at[d - 1], lo_recv.at[d - 1], seq_peer(2 * d)
            )
        return remote(chip_src, lo_in.at[d - 1], lo_send.at[d - 1], lo_recv.at[d - 1], seq_peer(2 * d))

    for d in range(1, hops + 1):
        @pl.when(b + 2 * d < n_seq)
        def _():
            lo_copy(d).start()

    state[...] = jnp.zeros_like(state)
    inner = []
    for s in pairs:
        right = jnp.concatenate([apart(maps[0, :, s]), apart(adds[0, :, s])], axis=1)
        late = mm(reads[1, :, s], right)
        inner.append(
            (
                jnp.concatenate([reads[0, :, s], late[:, :LANES]], axis=0).astype(BF16),
                jnp.concatenate([offsets[0, :, s], offsets[1, :, s] + late[:, LANES:]], axis=0),
            )
        )
    for d in range(hops, 0, -1):
        @pl.when(chip >= d)
        def _():
            lo_copy(d).wait_recv()
            if d == hops:
                state[...] = lo_in[d - 1, 1].astype(F32)
            else:
                for s in half_pairs:
                    state[:, s] = mm(lo_in[d - 1, 0, :, s], apart(state[:, s])) + lo_in[
                        d - 1, 1, :, s
                    ].astype(F32)

    for s in half_pairs:
        here = state[:, s]
        later = mm(even_lo[0, :, s], apart(here)) + even_lo[1, :, s]
        full[odd, 0, :, s] = jnp.where(is_odd, later, here)
        full[odd, 1, :, s] = jnp.where(is_odd, here, later)
    full_copy = remote(full.at[odd, 1], full.at[odd, 0], full_sem.at[0], full_sem.at[1], pair_peer)
    full_copy.start()
    full_copy.wait_recv()
    mixed = []
    for i, s in enumerate(pairs):
        at, cols = divmod(i * LANES, half_w)
        read, offset = inner[i]
        y = mm(read, apart(full[at, 0, :, cols : cols + LANES])) + offset
        spread = head_sums(y * y) * (1.0 / HS)
        extra = jnp.concatenate([bonus[0, :, s], bonus[1, :, s]], axis=0)
        mixed.append(y * lax.rsqrt(spread + 0.00064) * chan[5][:, s] + extra)
    head_mix = jnp.concatenate(mixed, axis=1).astype(BF16)

    out_load.wait()
    span = model // OUT_CHUNKS
    if line:
        routes = [
            ([(3, 1, n_wt)], [(2, 1, n_wt + 1), (1, 1, 0)], [], [1, 2]),
            ([(0, 0, 1)], [], [(3, 3, 1), (2, 2, 1)], [2, 0]),
            ([(3, 3, 2)], [], [(0, 0, 2), (1, 1, 2)], [1, 3]),
            ([(0, 2, n_wt)], [(1, 2, n_wt + 1), (2, 2, 3)], [], [2, 1]),
        ]
    else:
        routes = []
        for me in range(n_wt):
            others = [(me + d) % n_wt for d in range(1, n_wt)]
            routes.append(([(t, t, me) for t in others], [], [], others))

    def rs_copy(t, to, slot, c):
        owned, cols = pl.ds(t * shard, shard), pl.ds(c * span, span)
        return remote(
            part_16.at[owned, cols], rs_in.at[slot, :, cols], rs_send.at[t, c], rs_recv.at[slot, c], (b, to)
        )

    for c in range(OUT_CHUNKS):
        cols = slice(c * span, (c + 1) * span)
        term = mm(head_mix, wout[:, cols])
        part[:, cols] = term
        part_16[:, cols] = term.astype(BF16)
        for me, (first, _, _, _) in enumerate(routes):
            @pl.when(w == me)
            def _():
                for route in first:
                    rs_copy(*route, c).start()

    for me, (_, later, merged, sources) in enumerate(routes):
        @pl.when(w == me)
        def _():
            for route in later:
                for c in range(OUT_CHUNKS):
                    rs_copy(*route, c).start()
            for i, (t, to, slot) in enumerate(merged):
                owned = slice(t * shard, (t + 1) * shard)
                for c in range(OUT_CHUNKS):
                    cols = slice(c * span, (c + 1) * span)
                    rs_copy(t, to, n_wt + i, c).wait_recv()
                    total = part[owned, cols] + rs_in[n_wt + i, :, cols].astype(F32)
                    part_16[owned, cols] = total.astype(BF16)
                    rs_copy(t, to, slot, c).start()
            held = slice(me * shard, (me + 1) * shard)
            acc[...] = part[held, :] + x_all[held, :].astype(F32)
            for source in sources:
                for c in range(OUT_CHUNKS):
                    cols = slice(c * span, (c + 1) * span)
                    rs_copy(me, (me + 1) % n_wt, source, c).wait_recv()
                    acc[:, cols] += rs_in[source, :, cols].astype(F32)

    out_ref[...] = acc[...].astype(out_ref.dtype)

    @pl.when(sends_edge)
    def _():
        for copy in block_edges:
            copy.wait_send()

    @pl.when(w == mid - 1)
    def _():
        for copy in mid_edges:
            copy.wait_send()

    for d in range(1, n_wt):
        @pl.when(sends(d))
        def _():
            for h in range(X_PIECES):
                x_copy(d, h).wait_send()

    for at, owner, target, d in relays:
        @pl.when(w == at)
        def _():
            for h in range(X_PIECES):
                relay_copy(owner, target, h).wait_send()

    pair_copy.wait_send()
    full_copy.wait_send()
    for d in range(1, hops + 1):
        @pl.when(b + 2 * d < n_seq)
        def _():
            lo_copy(d).wait_send()

    for me, (first, later, merged, _) in enumerate(routes):
        @pl.when(w == me)
        def _():
            for route in first + later + merged:
                for c in range(OUT_CHUNKS):
                    rs_copy(*route, c).wait_send()


def shards(
    n_seq, n_wt,
    layer_input, token_shift_rates, input_projection_weight, output_matrix,
    decay_lowrank_first, decay_lowrank_second, learning_rate_first, learning_rate_second,
    decay_channel_bias, learning_rate_bias, prenorm_key_scale, written_key_share,
    present_step_coefficient, head_norm_gain, packed_request_length,
):
    shard, model = layer_input.shape
    rows = shard * n_wt
    width = decay_lowrank_second.shape[1]
    rank_w, rank_a = decay_lowrank_second.shape[0], learning_rate_second.shape[0]
    hops = (n_seq // 2 + 1) // 2
    half_w, chunk = width // 2, rows // 2
    chan = [
        v.reshape(1, width)
        for v in (
            decay_channel_bias, learning_rate_bias, prenorm_key_scale,
            written_key_share, present_step_coefficient, head_norm_gain,
        )
    ]
    vmem = pl.BlockSpec(memory_space=pltpu.VMEM)
    far = pl.BlockSpec(memory_space=pl.ANY)
    dma = pltpu.SemaphoreType.DMA
    return pl.pallas_call(
        functools.partial(kernel, n_seq, n_wt, hops),
        out_shape=pltpu.VMEM((shard, model), BF16),
        in_specs=[far] * 14 + [pl.BlockSpec(memory_space=pltpu.SMEM)],
        out_specs=vmem,
        scratch_shapes=[
            pltpu.VMEM((rows, model), BF16),
            pltpu.VMEM((8, model // 8), F32),
            pltpu.VMEM((2, 8, model // 8), F32),
            pltpu.VMEM((3, model, width), BF16),
            pltpu.VMEM((width, model), BF16),
            pltpu.VMEM((5, model), F32),
            pltpu.VMEM((rank_w, model), BF16),
            pltpu.VMEM((rank_w, width), BF16),
            pltpu.VMEM((rank_a, model), BF16),
            pltpu.VMEM((rank_a, width), BF16),
            pltpu.VMEM((6, 1, width), F32),
            pltpu.VMEM((2, HS, width), F32),
            pltpu.VMEM((2, HS, width), F32),
            pltpu.VMEM((2, chunk, width), F32),
            pltpu.VMEM((2, chunk, width), F32),
            pltpu.VMEM((2, chunk, width), F32),
            pltpu.VMEM((2, 2, HS, half_w), STATE_TYPE),
            pltpu.VMEM((2, HS, half_w), STATE_TYPE),
            pltpu.VMEM((2, HS, half_w), STATE_TYPE),
            pltpu.VMEM((hops, 2, HS, half_w), STATE_TYPE),
            pltpu.VMEM((HS, half_w), F32),
            pltpu.VMEM((2, 2, HS, half_w), F32),
            pltpu.VMEM((rows, model), F32),
            pltpu.VMEM((rows, model), BF16),
            pltpu.VMEM((n_wt + 2, shard, model), BF16),
            pltpu.VMEM((shard, model), F32),
            dma((16,)), dma((n_wt,)), dma((2,)),
            dma((n_wt - 1, X_PIECES)), dma((n_wt - 1, X_PIECES)), dma((X_PIECES,)),
            dma((2,)), dma((hops,)), dma((hops,)), dma((2,)),
            dma((n_wt, OUT_CHUNKS)), dma((n_wt + 2, OUT_CHUNKS)),
        ],
        compiler_params=pltpu.CompilerParams(
            collective_id=0, has_side_effects=True, vmem_limit_bytes=56 * 1024 * 1024
        ),
    )(
        layer_input, token_shift_rates, input_projection_weight, output_matrix,
        decay_lowrank_first.T, decay_lowrank_second, learning_rate_first.T, learning_rate_second,
        *chan, packed_request_length,
    )


def solution(mesh):
    placed = (
        P(("seq", "wt"), None),
        P(),
        P(None, None, "wt"),
        P("wt", None),
        P(),
        P(None, "wt"),
        P(),
        P(None, "wt"),
        P("wt"),
        P("wt"),
        P("wt"),
        P("wt"),
        P("wt"),
        P("wt"),
        P(),
    )
    return jax.shard_map(
        functools.partial(shards, mesh.shape["seq"], mesh.shape["wt"]),
        mesh=mesh, in_specs=placed, out_specs=P(("seq", "wt"), None), check_vma=False,
    )
```

```python
import functools
import jax
import jax.numpy as jnp
from jax import lax
from jax.experimental import pallas as pl
from jax.experimental.pallas import tpu as pltpu
from jax.sharding import PartitionSpec as P

HS = 64
LANES = 128
LOG_SCALE = 0.6065306597126334
MESH = pl.DeviceIdType.MESH
F32 = jnp.float32
BF16 = jnp.bfloat16
STATE_TYPE = BF16
OUT_CHUNKS = 4
PASS_LAG = 0
X_PIECES = 4
RELAY_LEAD = 4


def mm(a, b, ca=1, cb=0):
    return lax.dot_general(
        a.astype(BF16), b.astype(BF16), (((ca,), (cb,)), ((), ())), preferred_element_type=F32
    )


def lane(shape):
    return lax.broadcasted_iota(jnp.int32, shape, 1)


def apart(z):
    left = lane(z.shape) < z.shape[1] // 2
    z = z.astype(F32)
    return jnp.concatenate([jnp.where(left, z, 0.0), jnp.where(left, 0.0, z)], axis=0).astype(BF16)


def own_blocks(z):
    rows = z.shape[0] // 2
    return jnp.where(lane((rows, z.shape[1])) < z.shape[1] // 2, z[:rows], z[rows:])


def pieces(z, count):
    out = []
    for _ in range(count):
        part = z.astype(BF16)
        out.append(part)
        z = z - part.astype(F32)
    return out


def head_sums(z):
    row = lax.broadcasted_iota(jnp.int32, (2 * LANES, LANES), 0) % LANES
    same = jnp.where(row // HS == lane((2 * LANES, LANES)) // HS, 1.0, 0.0).astype(BF16)
    return mm(jnp.concatenate(pieces(z, 2), axis=1), same)


def by_pair(fn, width):
    return jnp.concatenate([fn(slice(k, k + LANES)) for k in range(0, width, LANES)], axis=1)


def token_tables(first, rows, lengths):
    pos_c = first + lax.broadcasted_iota(jnp.int32, (rows, 1), 0)
    pos_r = first + lane((1, 2 * rows)) % rows
    far = jnp.int32(2**30)
    start = jnp.int32(0)
    reset = jnp.zeros((rows, 1), jnp.int32)
    seg_c = jnp.zeros((rows, 1), jnp.int32)
    seg_r = jnp.zeros((1, 2 * rows), jnp.int32)
    seg_last = jnp.int32(0)
    for length in lengths:
        reset = jnp.maximum(reset, jnp.where(pos_c == start, 1, 0))
        inside = jnp.where(start >= first, start, far)
        seg_c = seg_c + jnp.where(pos_c >= inside, 1, 0)
        seg_r = seg_r + jnp.where(pos_r >= inside, 1, 0)
        seg_last = seg_last + jnp.where(first + (rows - 1) >= inside, 1, 0)
        start = start + length
    return reset, seg_c, seg_r, seg_last


def chunk_terms(recept, keys, values, decay_in, rate_in, chan, seg_c, seg_r, seg_last):
    rows, width = keys.shape
    decay_bias, rate_bias, key_scale, share, coefficient = chan[:5]
    logw = -LOG_SCALE * jax.nn.sigmoid(decay_bias + decay_in)
    rate = jax.nn.sigmoid(rate_bias + rate_in)
    tri_r = lax.broadcasted_iota(jnp.int32, (rows, 3 * rows), 0)
    tri = jnp.where(tri_r >= lane((rows, 3 * rows)) % rows, 1.0, 0.0).astype(BF16)
    cum = mm(tri, jnp.concatenate(pieces(logw, 3), axis=0))
    center = cum[rows // 2 - 1 : rows // 2]
    last = cum[rows - 1 : rows]
    grow = jnp.exp(cum - center)
    grow_x = jnp.exp(cum - logw - center)
    shrink = jnp.exp(center - cum)
    to_start = jnp.exp(center) * jnp.where(seg_c == 0, 1.0, 0.0)
    to_end = jnp.exp(last - center) * jnp.where(seg_c == seg_last, 1.0, 0.0)
    scaled = keys * key_scale
    squares = scaled * scaled
    norm = by_pair(lambda s: lax.rsqrt(head_sums(squares[:, s]) + 1e-06), width)
    unit = scaled * norm
    keys_mod = keys * (1.0 + (rate - 1.0) * share)
    centered = values - by_pair(lambda s: head_sums(values[:, s]) * (1.0 / HS), width)
    u_c = unit * grow_x
    q_c = recept * grow
    r_c = unit * rate * shrink
    k_c = keys_mod * shrink
    u_0 = u_c * to_start
    q_0 = q_c * to_start
    r_e = r_c * to_end
    k_e = k_c * to_end
    row = lax.broadcasted_iota(jnp.int32, (rows, 2 * rows), 0)
    col = lane((rows, 2 * rows)) % rows
    same = seg_c == seg_r
    strict = jnp.logical_and(same, row > col)
    causal = jnp.logical_and(same, row >= col)
    pairs = [slice(k, k + LANES) for k in range(0, width, LANES)]
    a_ur, a_k, a_qr = [], [], []
    for s in pairs:
        left = jnp.concatenate([u_c[:, s], q_c[:, s]], axis=0)
        right = jnp.concatenate([apart(r_c[:, s]), apart(k_c[:, s])], axis=0)
        both = mm(left, right, 1, 1)
        a_ur.append(jnp.where(strict, both[:rows, : 2 * rows], 0.0))
        a_qr.append(jnp.where(causal, both[rows:, : 2 * rows], 0.0).astype(BF16))
        a_k.append(
            jnp.concatenate(
                [
                    jnp.where(strict, both[:rows, 2 * rows :], 0.0),
                    jnp.where(causal, both[rows:, 2 * rows :], 0.0),
                ],
                axis=0,
            ).astype(BF16)
        )
    kvs = [mm(a, apart(centered[:, s])) for a, s in zip(a_k, pairs)]
    eye = jnp.where(row == col, 1.0, 0.0)
    inverse, carried = None, a_ur
    size = 1
    while size < rows:
        tile_r, tile_c = row // size, col // size
        corner = jnp.logical_and(tile_r == tile_c + 1, tile_r % 2 == 1)
        lows = [jnp.where(corner, a, 0.0).astype(BF16) for a in carried]
        size *= 2
        if inverse is None:
            inverse = [eye - low.astype(F32) for low in lows]
            carried = [a - mm(low, apart(a)) for low, a in zip(lows, carried)]
        elif size < rows:
            steps = [
                mm(low, jnp.concatenate([apart(x), apart(a)], axis=1))
                for low, x, a in zip(lows, inverse, carried)
            ]
            inverse = [x - step[:, : 2 * rows] for x, step in zip(inverse, steps)]
            carried = [a - step[:, 2 * rows :] for a, step in zip(carried, steps)]
        else:
            inverse = [x - mm(low, apart(x)) for low, x in zip(lows, inverse)]
    solved = [
        mm(x, jnp.concatenate([apart(u_0[:, s]), apart(kv[:rows])], axis=1))
        for x, kv, s in zip(inverse, kvs, pairs)
    ]
    small_r = lax.broadcasted_iota(jnp.int32, (HS, LANES), 0)
    decay_all = jnp.exp(last) * jnp.where(seg_last == 0, 1.0, 0.0)
    diagonal = small_r == lane((HS, LANES)) % HS
    maps, adds = [], []
    for sol, s in zip(solved, pairs):
        into = jnp.concatenate([r_e[:, s], k_e[:, s]], axis=0)
        right = jnp.concatenate(
            [-sol, jnp.concatenate([jnp.zeros((rows, LANES), F32), centered[:, s]], axis=1)], axis=0
        )
        end = mm(into, right, 0, 0)
        diag = jnp.where(diagonal, jnp.broadcast_to(decay_all[:, s], (HS, LANES)), 0.0)
        maps.append(diag + own_blocks(end[:, :LANES]))
        adds.append(own_blocks(end[:, LANES:]))

    def rest():
        reads, offsets, bonus = [], [], []
        own = recept * keys_mod * coefficient
        for a, sol, kv, s in zip(a_qr, solved, kvs, pairs):
            right = jnp.concatenate([apart(sol[:, :LANES]), apart(sol[:, LANES:])], axis=1)
            out = jnp.concatenate([q_0[:, s], kv[rows:]], axis=1) - mm(a, right)
            reads.append(out[:, :LANES])
            offsets.append(out[:, LANES:])
            bonus.append(head_sums(own[:, s]) * values[:, s])
        return [jnp.concatenate(z, axis=1) for z in (reads, offsets, bonus)]

    return jnp.concatenate(maps, axis=1), jnp.concatenate(adds, axis=1), rest


def kernel(
    n_seq, n_wt, hops,
    x_hbm, rates_hbm, win_hbm, wout_hbm, d1_hbm, d2_hbm, a1_hbm, a2_hbm,
    db_hbm, rb_hbm, ks_hbm, sh_hbm, co_hbm, ga_hbm, len_hbm,
    out_ref,
    x_all, edge_src, edge_in, win, wout, rates, d1, d2, a1, a2, chans, len_ref,
    maps, adds, reads, offsets, bonus,
    lo_src, pair_in, chip_src, lo_in, state, full, part, part_16, rs_in, acc,
    w_sem, edge_send, edge_recv, x_send, x_recv, fwd_sem, pair_sem, lo_send, lo_recv, full_sem,
    rs_send, rs_recv,
):
    b = lax.axis_index("seq")
    w = lax.axis_index("wt")
    shard, model = x_hbm.shape
    rows = shard * n_wt
    width = win.shape[2]
    half_w = width // 2
    chunk = rows // 2
    mid = n_wt // 2
    top = n_wt - 1
    odd = lax.rem(b, 2)
    chip = b // 2
    piece = model // 8
    near = w // mid

    def wt_peer(d):
        return (b, lax.rem(w + d, n_wt))

    def seq_peer(d):
        return (lax.rem(b + d, n_seq), w)

    pair_peer = (b + 1 - 2 * odd, w)
    before = lax.rem(b + n_seq - 1, n_seq)
    after = lax.rem(b + 1, n_seq)

    barrier = pltpu.get_barrier_semaphore()

    def greet(target):
        pl.semaphore_signal(barrier, inc=1, device_id=target, device_id_type=MESH)

    for d in range(1, n_wt):
        greet(wt_peer(d))
    greet(pair_peer)
    for d in range(1, hops + 1):
        @pl.when(b >= 2 * d)
        def _():
            greet((lax.rem(b + n_seq - 2 * d, n_seq), w))

    @pl.when(b >= 1)
    def _():
        greet((before, top))

    mine = pl.ds(pl.multiple_of(w * shard, shard), shard)
    x_load = pltpu.make_async_copy(x_hbm, x_all.at[mine], w_sem.at[0])
    x_load.start()
    small = [(len_hbm, len_ref), (rates_hbm, rates), (d1_hbm, d1), (a1_hbm, a1), (d2_hbm, d2), (a2_hbm, a2)]
    small += [(ref, chans.at[i]) for i, ref in enumerate((db_hbm, rb_hbm, ks_hbm, sh_hbm, co_hbm, ga_hbm))]
    small += [(win_hbm.at[c], win.at[c]) for c in range(3)]
    loads = [pltpu.make_async_copy(src, dst, w_sem.at[1 + i]) for i, (src, dst) in enumerate(small)]
    out_load = pltpu.make_async_copy(wout_hbm, wout, w_sem.at[1 + len(small)])
    for load in loads:
        load.start()
    out_load.start()
    x_load.wait()
    last_row = x_all[pl.ds(pl.multiple_of(w * shard + shard - 16, 16), 16), :][15:16].astype(F32)
    for i in range(8):
        edge_src[i : i + 1, :] = last_row[:, i * piece : (i + 1) * piece]

    sends_edge = jnp.logical_and(w == top, b < n_seq - 1)
    expected = top + 1 + jnp.where(sends_edge, n_wt, 0)
    for d in range(1, hops + 1):
        expected = expected + jnp.where(b + 2 * d < n_seq, 1, 0)
    pl.semaphore_wait(barrier, expected)

    def remote(src, dst, send, recv, target):
        return pltpu.make_async_remote_copy(
            src_ref=src, dst_ref=dst, send_sem=send, recv_sem=recv, device_id=target, device_id_type=MESH
        )

    block_edges = [
        remote(edge_src, edge_in.at[0], edge_send.at[i], edge_recv.at[0], (after, i)) for i in range(n_wt)
    ]
    mid_edges = [
        remote(edge_src, edge_in.at[1], edge_send.at[i], edge_recv.at[1], (b, i)) for i in range(mid, n_wt)
    ]

    @pl.when(sends_edge)
    def _():
        for copy in block_edges:
            copy.start()

    @pl.when(w == mid - 1)
    def _():
        for copy in mid_edges:
            copy.start()

    line = n_wt == 4
    step = model // X_PIECES

    def piece_of(owner, h):
        return x_all.at[pl.ds(pl.multiple_of(owner * shard, shard), shard), pl.ds(h * step, step)]

    def x_copy(d, h):
        place = piece_of(w, h)
        return remote(place, place, x_send.at[d - 1, h], x_recv.at[d - 1, h], wt_peer(d))

    def sends(d):
        if line and d == 2:
            return jnp.logical_or(w == 0, w == top)
        return w >= 0

    pieces = range(X_PIECES)
    if line:
        sequences = [
            [(d, h) for d in (1, 3, 2) for h in pieces],
            [(d, h) for h in pieces for d in (3, 1)],
            [(d, h) for h in pieces for d in (1, 3)],
            [(d, h) for d in (3, 1, 2) for h in pieces],
        ]
    else:
        sequences = [[(d, h) for d in range(1, n_wt) for h in pieces]] * n_wt
    for me, sequence in enumerate(sequences):
        @pl.when(w == me)
        def _():
            for d, h in sequence:
                x_copy(d, h).start()

    relays = [(1, 2, 0, 3), (2, 1, 3, 1)] if line else []

    def relay_copy(owner, target, h):
        place = piece_of(owner, h)
        return remote(place, place, fwd_sem.at[h], x_recv.at[1, h], (b, target))

    def is_near(d):
        return lax.rem(w + n_wt - d, n_wt) // mid == near

    def relayed(d):
        out = w < 0
        for at, _, _, which in relays:
            if which == d:
                out = jnp.logical_or(out, w == at)
        return out

    def relay(h):
        for at, owner, target, d in relays:
            @pl.when(w == at)
            def _():
                x_copy(d, h).wait_recv()
                relay_copy(owner, target, h).start()

    for h in range(RELAY_LEAD):
        relay(h)

    def near_arrival(h):
        if h + RELAY_LEAD < X_PIECES:
            relay(h + RELAY_LEAD)
        for d in range(1, n_wt):
            @pl.when(is_near(d))
            def _():
                x_copy(d, h).wait_recv()

    @pl.when(b >= 1)
    def _():
        block_edges[0].wait_recv()

    @pl.when(near == 1)
    def _():
        mid_edges[0].wait_recv()

    for load in loads:
        load.wait()
    lengths = [len_ref[i] for i in range(len_ref.shape[0])]
    chan = [chans[i] for i in range(6)]
    first_row = lax.broadcasted_iota(jnp.int32, (chunk, 1), 0) == 0

    def do_chunk(which, edge, arrival):
        base = pl.ds(pl.multiple_of(which * chunk, chunk), chunk)
        reset, seg_c, seg_r, seg_last = token_tables(b * rows + which * chunk, chunk, lengths)
        sums = [None] * 5
        for h in range(X_PIECES):
            arrival(h)
            cols = slice(h * step, (h + 1) * step)
            current = x_all[base, cols].astype(F32)
            previous = jnp.where(first_row, edge[:, cols], pltpu.roll(current, 1, 0))
            previous = jnp.where(reset == 1, 0.0, previous)
            delta = previous - current
            for c in (3, 4, 0, 1, 2):
                mixed = (current + delta * rates[c : c + 1, cols]).astype(BF16)
                if c < 3:
                    term = mm(mixed, win[c, cols, :])
                else:
                    term = mm(mixed, (d1 if c == 3 else a1)[:, cols], 1, 1)
                sums[c] = term if sums[c] is None else sums[c] + term
        decay_in = mm(jnp.tanh(sums[3]), d2[...])
        rate_in = mm(sums[4], a2[...])
        m, a, rest = chunk_terms(*sums[:3], decay_in, rate_in, chan, seg_c, seg_r, seg_last)
        maps[which] = m
        adds[which] = a

        def finish():
            reads[which], offsets[which], bonus[which] = rest()

        return finish

    def edge_row(i):
        return jnp.concatenate([edge_in[i, r : r + 1, :] for r in range(8)], axis=1)

    def near_last_row():
        at = pl.ds(pl.multiple_of((near + 1) * chunk - 16, 16), 16)
        return x_all[at, :][15:16].astype(F32)

    do_chunk(near, jnp.where(near == 0, edge_row(0), edge_row(1)), near_arrival)()

    def far_arrival(h):
        for d in range(1, n_wt):
            @pl.when(jnp.logical_not(jnp.logical_or(is_near(d), relayed(d))))
            def _():
                x_copy(d, h).wait_recv()

    far_rest = do_chunk(1 - near, jnp.where(near == 1, edge_row(0), near_last_row()), far_arrival)

    pairs = [slice(k, k + LANES) for k in range(0, width, LANES)]
    half_pairs = [slice(k, k + LANES) for k in range(0, half_w, LANES)]

    def compose(later, earlier):
        both = mm(later[0], jnp.concatenate([apart(earlier[0]), apart(earlier[1])], axis=1))
        return both[:, :LANES], both[:, LANES:] + later[1]

    for i, s in enumerate(pairs):
        m, a = compose((maps[1, :, s], adds[1, :, s]), (maps[0, :, s], adds[0, :, s]))
        at, cols = divmod(i * LANES, half_w)
        lo_src[at, 0, :, cols : cols + LANES] = m.astype(STATE_TYPE)
        lo_src[at, 1, :, cols : cols + LANES] = a.astype(STATE_TYPE)
    pair_copy = remote(lo_src.at[1 - odd], pair_in, pair_sem.at[0], pair_sem.at[1], pair_peer)
    pair_copy.start()
    far_rest()
    pair_copy.wait_recv()
    is_odd = odd == 1
    mine_lo = lo_src[odd].astype(F32)
    other_lo = pair_in[...].astype(F32)
    even_lo = jnp.where(is_odd, other_lo, mine_lo)
    odd_lo = jnp.where(is_odd, mine_lo, other_lo)
    for s in half_pairs:
        m, a = compose((odd_lo[0, :, s], odd_lo[1, :, s]), (even_lo[0, :, s], even_lo[1, :, s]))
        chip_src[0, :, s] = m.astype(STATE_TYPE)
        chip_src[1, :, s] = a.astype(STATE_TYPE)

    def lo_copy(d, i):
        return remote(
            chip_src.at[i], lo_in.at[d - 1, i], lo_send.at[d - 1, i], lo_recv.at[d - 1, i], seq_peer(2 * d)
        )

    for i in (1, 0):
        for d in range(1, hops + i):
            @pl.when(jnp.logical_and(b + 2 * d < n_seq, chip >= 1 - i))
            def _():
                lo_copy(d, i).start()

    state[...] = jnp.zeros_like(state)
    inner = []
    for s in pairs:
        right = jnp.concatenate([apart(maps[0, :, s]), apart(adds[0, :, s])], axis=1)
        late = mm(reads[1, :, s], right)
        inner.append(
            (
                jnp.concatenate([reads[0, :, s], late[:, :LANES]], axis=0).astype(BF16),
                jnp.concatenate([offsets[0, :, s], offsets[1, :, s] + late[:, LANES:]], axis=0),
            )
        )
    for d in range(hops, 0, -1):
        @pl.when(chip >= d)
        def _():
            lo_copy(d, 1).wait_recv()

        if d == hops:
            @pl.when(chip >= d)
            def _():
                state[...] = lo_in[d - 1, 1].astype(F32)
        else:
            @pl.when(chip == d)
            def _():
                state[...] = lo_in[d - 1, 1].astype(F32)

            @pl.when(chip > d)
            def _():
                lo_copy(d, 0).wait_recv()
                for s in half_pairs:
                    state[:, s] = mm(lo_in[d - 1, 0, :, s], apart(state[:, s])) + lo_in[
                        d - 1, 1, :, s
                    ].astype(F32)

    for s in half_pairs:
        here = state[:, s]
        later = mm(even_lo[0, :, s], apart(here)) + even_lo[1, :, s]
        full[odd, 0, :, s] = jnp.where(is_odd, later, here)
        full[odd, 1, :, s] = jnp.where(is_odd, here, later)
    full_copy = remote(full.at[odd, 1], full.at[odd, 0], full_sem.at[0], full_sem.at[1], pair_peer)
    full_copy.start()
    full_copy.wait_recv()
    mixed = []
    for i, s in enumerate(pairs):
        at, cols = divmod(i * LANES, half_w)
        read, offset = inner[i]
        y = mm(read, apart(full[at, 0, :, cols : cols + LANES])) + offset
        spread = head_sums(y * y) * (1.0 / HS)
        extra = jnp.concatenate([bonus[0, :, s], bonus[1, :, s]], axis=0)
        mixed.append(y * lax.rsqrt(spread + 0.00064) * chan[5][:, s] + extra)
    head_mix = jnp.concatenate(mixed, axis=1).astype(BF16)

    out_load.wait()
    span = model // OUT_CHUNKS
    if line:
        routes = [
            ([(3, 1, n_wt)], [(2, 1, n_wt + 1), (1, 1, 0)], [], [1, 2]),
            ([(0, 0, 1)], [], [(3, 3, 1), (2, 2, 1)], [2, 0]),
            ([(3, 3, 2)], [], [(0, 0, 2), (1, 1, 2)], [1, 3]),
            ([(0, 2, n_wt)], [(1, 2, n_wt + 1), (2, 2, 3)], [], [2, 1]),
        ]
    else:
        routes = []
        for me in range(n_wt):
            others = [(me + d) % n_wt for d in range(1, n_wt)]
            routes.append(([(t, t, me) for t in others], [], [], others))

    def rs_copy(t, to, slot, c):
        owned, cols = pl.ds(t * shard, shard), pl.ds(c * span, span)
        return remote(
            part_16.at[owned, cols], rs_in.at[slot, :, cols], rs_send.at[t, c], rs_recv.at[slot, c], (b, to)
        )

    def pass_on(i, t, to, slot, c):
        owned, cols = slice(t * shard, (t + 1) * shard), slice(c * span, (c + 1) * span)
        rs_copy(t, to, n_wt + i, c).wait_recv()
        part_16[owned, cols] = (part[owned, cols] + rs_in[n_wt + i, :, cols].astype(F32)).astype(BF16)
        rs_copy(t, to, slot, c).start()

    for c in range(OUT_CHUNKS):
        cols = slice(c * span, (c + 1) * span)
        term = mm(head_mix, wout[:, cols])
        part[:, cols] = term
        part_16[:, cols] = term.astype(BF16)
        for me, (first, _, merged, _) in enumerate(routes):
            @pl.when(w == me)
            def _():
                for route in first:
                    rs_copy(*route, c).start()
                if merged and c >= PASS_LAG:
                    pass_on(0, *merged[0], c - PASS_LAG)

    for me, (_, later, merged, sources) in enumerate(routes):
        @pl.when(w == me)
        def _():
            for route in later:
                for c in range(OUT_CHUNKS):
                    rs_copy(*route, c).start()
            for i, route in enumerate(merged):
                for c in range(OUT_CHUNKS - PASS_LAG if i == 0 else 0, OUT_CHUNKS):
                    pass_on(i, *route, c)
            held = slice(me * shard, (me + 1) * shard)
            acc[...] = part[held, :] + x_all[held, :].astype(F32)
            for source in sources:
                for c in range(OUT_CHUNKS):
                    cols = slice(c * span, (c + 1) * span)
                    rs_copy(me, (me + 1) % n_wt, source, c).wait_recv()
                    acc[:, cols] += rs_in[source, :, cols].astype(F32)

    out_ref[...] = acc[...].astype(out_ref.dtype)

    @pl.when(sends_edge)
    def _():
        for copy in block_edges:
            copy.wait_send()

    @pl.when(w == mid - 1)
    def _():
        for copy in mid_edges:
            copy.wait_send()

    for d in range(1, n_wt):
        @pl.when(sends(d))
        def _():
            for h in range(X_PIECES):
                x_copy(d, h).wait_send()

    for at, owner, target, d in relays:
        @pl.when(w == at)
        def _():
            for h in range(X_PIECES):
                relay_copy(owner, target, h).wait_send()

    pair_copy.wait_send()
    full_copy.wait_send()
    for i in (1, 0):
        for d in range(1, hops + i):
            @pl.when(jnp.logical_and(b + 2 * d < n_seq, chip >= 1 - i))
            def _():
                lo_copy(d, i).wait_send()

    for me, (first, later, merged, _) in enumerate(routes):
        @pl.when(w == me)
        def _():
            for route in first + later + merged:
                for c in range(OUT_CHUNKS):
                    rs_copy(*route, c).wait_send()


def shards(
    n_seq, n_wt,
    layer_input, token_shift_rates, input_projection_weight, output_matrix,
    decay_lowrank_first, decay_lowrank_second, learning_rate_first, learning_rate_second,
    decay_channel_bias, learning_rate_bias, prenorm_key_scale, written_key_share,
    present_step_coefficient, head_norm_gain, packed_request_length,
):
    shard, model = layer_input.shape
    rows = shard * n_wt
    width = decay_lowrank_second.shape[1]
    rank_w, rank_a = decay_lowrank_second.shape[0], learning_rate_second.shape[0]
    hops = (n_seq // 2 + 1) // 2
    half_w, chunk = width // 2, rows // 2
    chan = [
        v.reshape(1, width)
        for v in (
            decay_channel_bias, learning_rate_bias, prenorm_key_scale,
            written_key_share, present_step_coefficient, head_norm_gain,
        )
    ]
    vmem = pl.BlockSpec(memory_space=pltpu.VMEM)
    far = pl.BlockSpec(memory_space=pl.ANY)
    dma = pltpu.SemaphoreType.DMA
    return pl.pallas_call(
        functools.partial(kernel, n_seq, n_wt, hops),
        out_shape=pltpu.VMEM((shard, model), BF16),
        in_specs=[far] * 15,
        out_specs=vmem,
        scratch_shapes=[
            pltpu.VMEM((rows, model), BF16),
            pltpu.VMEM((8, model // 8), F32),
            pltpu.VMEM((2, 8, model // 8), F32),
            pltpu.VMEM((3, model, width), BF16),
            pltpu.VMEM((width, model), BF16),
            pltpu.VMEM((5, model), F32),
            pltpu.VMEM((rank_w, model), BF16),
            pltpu.VMEM((rank_w, width), BF16),
            pltpu.VMEM((rank_a, model), BF16),
            pltpu.VMEM((rank_a, width), BF16),
            pltpu.VMEM((6, 1, width), F32),
            pltpu.SMEM(packed_request_length.shape, jnp.int32),
            pltpu.VMEM((2, HS, width), F32),
            pltpu.VMEM((2, HS, width), F32),
            pltpu.VMEM((2, chunk, width), F32),
            pltpu.VMEM((2, chunk, width), F32),
            pltpu.VMEM((2, chunk, width), F32),
            pltpu.VMEM((2, 2, HS, half_w), STATE_TYPE),
            pltpu.VMEM((2, HS, half_w), STATE_TYPE),
            pltpu.VMEM((2, HS, half_w), STATE_TYPE),
            pltpu.VMEM((hops, 2, HS, half_w), STATE_TYPE),
            pltpu.VMEM((HS, half_w), F32),
            pltpu.VMEM((2, 2, HS, half_w), F32),
            pltpu.VMEM((rows, model), F32),
            pltpu.VMEM((rows, model), BF16),
            pltpu.VMEM((n_wt + 2, shard, model), BF16),
            pltpu.VMEM((shard, model), F32),
            dma((17,)), dma((n_wt,)), dma((2,)),
            dma((n_wt - 1, X_PIECES)), dma((n_wt - 1, X_PIECES)), dma((X_PIECES,)),
            dma((2,)), dma((hops, 2)), dma((hops, 2)), dma((2,)),
            dma((n_wt, OUT_CHUNKS)), dma((n_wt + 2, OUT_CHUNKS)),
        ],
        compiler_params=pltpu.CompilerParams(
            collective_id=0, has_side_effects=True, vmem_limit_bytes=56 * 1024 * 1024
        ),
    )(
        layer_input, token_shift_rates, input_projection_weight, output_matrix,
        decay_lowrank_first.T, decay_lowrank_second, learning_rate_first.T, learning_rate_second,
        *chan, packed_request_length,
    )


def solution(mesh):
    placed = (
        P(("seq", "wt"), None),
        P(),
        P(None, None, "wt"),
        P("wt", None),
        P(),
        P(None, "wt"),
        P(),
        P(None, "wt"),
        P("wt"),
        P("wt"),
        P("wt"),
        P("wt"),
        P("wt"),
        P("wt"),
        P(),
    )
    return jax.shard_map(
        functools.partial(shards, mesh.shape["seq"], mesh.shape["wt"]),
        mesh=mesh, in_specs=placed, out_specs=P(("seq", "wt"), None), check_vma=False,
    )
```
